512 devices in a mesh: ctx: 16 (over z_lo, core), head: 8 (over x, z_hi), dp: 4 (over y).
Axes of the slice: x: 4, y: 4, z: 16 (z_hi: 2, z_lo: 8; z = z_hi * 8 + z_lo), core: 2. Of those that a mesh axis runs over, the one named last changes fastest.
Arguments:
- queries: bfloat16 [8192, 4096], P(('dp', 'ctx'), 'head'), parts along dimension 0, may hold values from -6 to 6
- key_rows: bfloat16 [8192, 4096], P(('dp', 'ctx'), 'head'), parts along dimension 0, may hold values from -6 to 6
- value_rows: bfloat16 [8192, 4096], P(('dp', 'ctx'), 'head'), parts along dimension 0, may hold values from -6 to 6
- gate_values: bfloat16 [8192, 4096], P(('dp', 'ctx'), 'head'), parts along dimension 0, may hold values from -6 to 6
- cotangent: bfloat16 [8192, 4096], P(('dp', 'ctx'), 'head'), parts along dimension 0, may hold values from -6 to 6
- decay_rates: float32 [16, 4096], P(None, 'head'), may hold values from 0 to 1, as said below
- residues: float32 [16, 4096], P(None, 'head'), may hold values from -4 to 4
- skip_gain: float32 [4096], P('head'), may hold values from -6 to 6
Outputs:
- queries_adjoint: bfloat16 [8192, 4096], P(('dp', 'ctx'), 'head'), parts along dimension 0
- keys_adjoint: bfloat16 [8192, 4096], P(('dp', 'ctx'), 'head'), parts along dimension 0
- values_adjoint: bfloat16 [8192, 4096], P(('dp', 'ctx'), 'head'), parts along dimension 0
- gate_adjoint: bfloat16 [8192, 4096], P(('dp', 'ctx'), 'head'), parts along dimension 0
- residues_adjoint: float32 [64, 4096], P('dp', 'head'), parts along dimension 0
The draws below stay inside these ranges and needn't reach their ends.
There are 4 independent parts, one for each index of `dp`. The reference program is written for one: setup_inputs(seed, part) draws one part's arguments, and reference() takes and returns one part's arrays. A program takes and returns all parts, laid end to end along the dimension named above; an argument that names none is the same for every part. Nothing has to cross between parts.
Inputs may be any that keep to these rules, and one draw needn't show every extreme that they name: `decay_rates`: every rate lies between 0.6 / 2048 and 1/16 per position.
All inputs are finite; a program needn't handle non-finite values.
Results may differ from the reference program's by a relative error of at most 0.0094.
Values may be sent and summed in bfloat16 or wider, within the bound.
No kernel may reach another device: no remote copies, remote signals or barrier semaphores. Data moves between devices by JAX's collectives and lax.ppermute only.
A program may use at most 64 MiB of HBM per device.

```python
import math
import jax
import jax.numpy as jnp
from jax import lax

HEADS = 32
HEAD = 128
POLES = 16
TOK_DEV = 128
WIN = 4
TOKENS = 2048
CH = 4096
N_CTX = 16


def paired_draw(key):
    base_key = jax.random.fold_in(key, 4242)
    query_key, other_key = jax.random.split(base_key, 2)
    shape_pair = (TOKENS, HEADS * HEAD)
    query_part = jnp.clip(2.5 * jax.random.normal(query_key, shape_pair, jnp.float32), -6.0, 6.0)
    key_part = jnp.clip(jax.random.normal(other_key, shape_pair, jnp.float32), -6.0, 6.0)
    return (query_part, key_part)


def draw_queries(key, part):
    return paired_draw(key)[0].astype(jnp.bfloat16)


def draw_key_rows(key, part):
    return paired_draw(key)[1].astype(jnp.bfloat16)


def draw_decay_rates(key, part):
    pick_key, slow_key, fast_key = jax.random.split(jax.random.fold_in(key, 99), 3)
    shape_rates = (POLES, HEADS * HEAD)
    slow_share = 0.5
    slow_low = math.log(0.6 / TOKENS)
    slow_high = math.log(2.3 / TOKENS)
    fast_low = math.log(1.0 / 64.0)
    fast_high = math.log(1.0 / 16.0)
    slow_rates = jnp.exp(slow_low + jax.random.uniform(slow_key, shape_rates, jnp.float32) * (slow_high - slow_low))
    fast_rates = jnp.exp(fast_low + jax.random.uniform(fast_key, shape_rates, jnp.float32) * (fast_high - fast_low))
    picked = jax.random.uniform(pick_key, shape_rates, jnp.float32) < slow_share
    return jnp.where(picked, slow_rates, fast_rates).astype(jnp.float32)


def levels(key, extent, cuts, least, top_value):
    def one(position, parts):
        heights = jax.random.uniform(jax.random.fold_in(jax.random.fold_in(key, 6), position), (parts,), jnp.float32, least / len(cuts), top_value / len(cuts))
        return jnp.repeat(jnp.exp(heights), extent[position] // parts).reshape((-1,) + (1,) * (len(extent) - position - 1))

    gain = one(*cuts[0])
    for cut in cuts[1:]:
        gain = gain * one(*cut)
    return gain


def gaussian(own_key, dims, width, limit, shards=(), held_as=jnp.bfloat16):
    values = width * jax.random.normal(own_key, dims, jnp.float32)
    if shards:
        values = values * levels(own_key, dims, shards, -0.22, 0.18)
    return jnp.clip(values, -limit, limit).astype(held_as)


def setup_inputs(seed: int = 0, part: int = 0) -> dict:
    splits = jax.random.split(jax.random.key(seed), 9)
    own_keys = jax.random.split(jax.random.fold_in(splits[8], part), 9)
    return {
        "queries": draw_queries(jax.random.fold_in(jax.random.fold_in(splits[8], part), 71), part),
        "key_rows": draw_key_rows(jax.random.fold_in(jax.random.fold_in(splits[8], part), 71), part),
        "value_rows": gaussian(own_keys[2], (TOKENS, CH), 1.0, 6.0, ((0, 16), (1, 8))),
        "gate_values": gaussian(own_keys[3], (TOKENS, CH), 1.0, 6.0, ((0, 16), (1, 8))),
        "cotangent": gaussian(own_keys[4], (TOKENS, CH), 1.0, 6.0, ((0, 16), (1, 8))),
        "decay_rates": draw_decay_rates(jax.random.fold_in(splits[8], 71), part),
        "residues": gaussian(splits[6], (POLES, CH), 0.25, 4.0, ((1, 8),), jnp.float32),
        "skip_gain": gaussian(splits[7], (CH,), 1.0, 6.0, ((0, 8),), jnp.float32),
    }


def to_half(array):
    return lax.optimization_barrier(array.astype(jnp.bfloat16)).astype(jnp.float32)

def window_mask(row_count):
    row_ids = jnp.arange(row_count)[:, None, None]
    lag_ids = jnp.arange(WIN + 1)[None, :, None]
    column_ids = jnp.arange(row_count)[None, None, :]
    return ((lag_ids > 0) | (column_ids <= row_ids)) & ((lag_ids < WIN) | (column_ids > row_ids))

def modal_pass(signal, damping, opening, mixing, skip_gain, partner, weights):
    piece_rows = min(128, TOK_DEV)
    pieces = TOKENS // piece_rows
    offsets = jnp.arange(piece_rows, dtype=jnp.float32)[:, None, None]
    growth = jnp.exp(damping[None] * offsets)
    shrink = jnp.exp(-damping[None] * offsets)
    entering = jnp.exp(-damping[None] * (offsets + 1.0))

    def advance(carried, head_item):
        segment, matched = head_item
        local_part = shrink * jnp.cumsum(growth * segment[:, None, :], axis=0)
        states = local_part + entering * carried[None]
        mixture = lax.optimization_barrier(jnp.sum(mixing[None] * states, axis=1)) + skip_gain[None] * segment
        product = lax.optimization_barrier(jnp.sum(weights[None] * matched[:, None, :] * states, axis=0))
        return (states[-1], (mixture, product))
    closing, (mixture, product) = lax.scan(advance, opening, (signal.reshape(pieces, piece_rows, -1), partner.reshape(pieces, piece_rows, -1)))
    return (closing, mixture.reshape(TOKENS, -1), lax.optimization_barrier(jnp.sum(product, axis=0)))

def periodic_pass(signal, damping, mixing, skip_gain, partner, weights):
    zero_state = jnp.zeros(damping.shape, jnp.float32)
    closing, unused_mix, unused_sum = modal_pass(signal, damping, zero_state, mixing, skip_gain, partner, weights)
    loop_gap = -jnp.expm1(-damping * TOKENS)
    closing_again, mixture, product = modal_pass(signal, damping, closing / loop_gap, mixing, skip_gain, partner, weights)
    return (mixture, product)

def head_pass(head_item):
    query_head, key_head, value_head, adjoint_head = [member.astype(jnp.float32) for member in head_item]
    key_window = jnp.stack([jnp.roll(key_head, lag_block, axis=0) for lag_block in range(WIN + 1)])
    value_window = jnp.stack([jnp.roll(value_head, lag_block, axis=0) for lag_block in range(WIN + 1)])
    scale_factor = 1.0 / math.sqrt(HEAD)
    scores = jnp.einsum('nre,knse->nrks', query_head, key_window) * scale_factor
    allowed = window_mask(TOK_DEV)[None]
    masked = jnp.where(allowed, scores, -jnp.inf)
    row_top = lax.optimization_barrier(jnp.max(masked, axis=(2, 3), keepdims=True))
    raised = jnp.exp(masked - row_top)
    probability = raised / lax.optimization_barrier(jnp.sum(raised, axis=(2, 3), keepdims=True))
    rounded_prob = to_half(probability)
    attended = jnp.einsum('nrks,knse->nre', rounded_prob, value_window).astype(jnp.bfloat16)
    weight_adjoint = jnp.einsum('nre,knse->nrks', adjoint_head, value_window)
    inner_sum = lax.optimization_barrier(jnp.sum(probability * weight_adjoint, axis=(2, 3), keepdims=True))
    score_adjoint = to_half(probability * (weight_adjoint - inner_sum) * scale_factor)
    query_adjoint = jnp.einsum('nrks,knse->nre', score_adjoint, key_window).astype(jnp.bfloat16)
    key_parts = to_half(jnp.einsum('nrks,nre->knse', score_adjoint, query_head))
    value_parts = to_half(jnp.einsum('nrks,nre->knse', rounded_prob, adjoint_head))
    key_total = sum((jnp.roll(key_parts[lag_block], -lag_block, axis=0) for lag_block in range(WIN + 1)))
    value_total = sum((jnp.roll(value_parts[lag_block], -lag_block, axis=0) for lag_block in range(WIN + 1)))
    return (attended, query_adjoint, key_total.astype(jnp.bfloat16), value_total.astype(jnp.bfloat16))

def split_heads(array):
    return array.reshape(N_CTX, TOK_DEV, HEADS, HEAD).transpose(2, 0, 1, 3)

def merge_heads(array):
    return array.transpose(1, 2, 0, 3).reshape(TOKENS, HEADS * HEAD)

def reference(queries, key_rows, value_rows, gate_values, cotangent, decay_rates, residues, skip_gain):
    damping = decay_rates
    weights = jnp.sqrt(-jnp.expm1(-2.0 * damping))
    mixing = residues * weights
    delta_rows = cotangent.astype(jnp.float32) * gate_values.astype(jnp.float32)
    no_partner = jnp.zeros_like(delta_rows)
    reversed_mix, unused_sum = periodic_pass(delta_rows[::-1], damping, mixing, skip_gain, no_partner, weights)
    attended_adjoint = reversed_mix[::-1].astype(jnp.bfloat16)
    attended, query_adjoint, key_adjoint, value_adjoint = lax.map(head_pass, (split_heads(queries), split_heads(key_rows), split_heads(value_rows), split_heads(attended_adjoint)))
    mixture, residue_sum = periodic_pass(merge_heads(attended).astype(jnp.float32), damping, mixing, skip_gain, delta_rows, weights)
    gate_adjoint = (cotangent.astype(jnp.float32) * mixture).astype(jnp.bfloat16)
    return (merge_heads(query_adjoint), merge_heads(key_adjoint), merge_heads(value_adjoint), gate_adjoint, residue_sum)
```

```python
import math

import jax
import jax.numpy as jnp
from jax import lax
from jax.experimental import pallas as pl
from jax.experimental.pallas import tpu as pltpu
from jax.sharding import PartitionSpec as P

HEAD = 128
WIN = 4
LANES = 128
SUBS = 8
GROUP = 8
F32 = jnp.float32
BF16 = jnp.bfloat16


def call(body, outs, scratch=(), in_specs=None, count=0, name=None):
    specs = [pl.BlockSpec(memory_space=pltpu.SMEM)]
    specs += [pl.BlockSpec(memory_space=pltpu.VMEM)] * (count - 1)
    return pl.pallas_call(
        body,
        out_shape=[jax.ShapeDtypeStruct(s, d) for s, d in outs],
        in_specs=specs,
        out_specs=[pl.BlockSpec(memory_space=pltpu.VMEM)] * len(outs),
        scratch_shapes=list(scratch),
        name=name,
    )


def halves(core, width):
    own = pl.multiple_of(core * width, LANES)
    other = pl.multiple_of((1 - core) * width, LANES)
    return own, other


def pack_body(pos, q, k, v, gate, cot, keep_kv, give_kv, give_all):
    width = q.shape[1] // 2
    own, other = halves(pos[0], width)
    keep_kv[0] = k[:, pl.ds(own, width)]
    keep_kv[1] = v[:, pl.ds(own, width)]
    k_give = k[:, pl.ds(other, width)]
    v_give = v[:, pl.ds(other, width)]
    give_kv[0] = k_give
    give_kv[1] = v_give
    give_all[0] = k_give
    give_all[1] = v_give
    give_all[2] = q[:, pl.ds(other, width)]
    give_all[3] = gate[:, pl.ds(other, width)]
    give_all[4] = cot[:, pl.ds(other, width)]


def rows3(values):
    return jnp.broadcast_to(values[:, None, :], (values.shape[0], SUBS, values.shape[1]))


def each_group(poles, width, body):
    pole_groups = poles // GROUP
    lane_groups = width // LANES

    def step(index, carry):
        lane_group = index // pole_groups
        first_lane = pl.multiple_of(lane_group * LANES, LANES)
        first_pole = pl.multiple_of((index % pole_groups) * GROUP, GROUP)
        body(first_pole, lane_group, first_lane)
        return carry

    lax.fori_loop(0, pole_groups * lane_groups, step, 0)


def head_body(pos, gate, cot, given, rates, delta, totals, slots, head_ref):
    rows, channels = gate.shape
    width = channels // 2
    poles = rates.shape[0]
    chips = slots.shape[0]
    own, other = halves(pos[0], width)
    tokens = delta.shape[1]
    steps = tokens // SUBS
    mine = pl.multiple_of(pos[0] * rows, rows)
    theirs = pl.multiple_of((1 - pos[0]) * rows, rows)
    for lane_group in range(width // LANES):
        lanes = slice(lane_group * LANES, (lane_group + 1) * LANES)
        at_own = pl.ds(own + lane_group * LANES, LANES)
        delta[lane_group, pl.ds(mine, rows), :] = gate[:, at_own].astype(F32) * cot[:, at_own].astype(F32)
        delta[lane_group, pl.ds(theirs, rows), :] = given[3, :, lanes].astype(F32) * given[
            4, :, lanes
        ].astype(F32)

    def group(first_pole, lane_group, first_lane):
        rate = rates[pl.ds(first_pole, GROUP), pl.ds(own + first_lane, LANES)]
        lam = rows3(jnp.exp(-rate))
        state = jnp.zeros((GROUP, SUBS, LANES), F32)
        for j in reversed(range(steps)):
            state = lam * state + delta[lane_group, pl.ds(j, SUBS, stride=steps), :][None]
        totals[pl.ds(first_pole, GROUP), :, pl.ds(first_lane, LANES)] = state
        block = lax.broadcasted_iota(jnp.int32, (GROUP, SUBS, LANES), 1).astype(F32)
        power = jnp.exp(-rows3(rate) * (block * steps))
        head_ref[pl.ds(first_pole, GROUP), pl.ds(first_lane, LANES)] = jnp.sum(power * state, axis=1)

    each_group(poles, width, group)
    rate = rates[:, pl.ds(own, width)]
    send_slots(slots, head_ref[...], rate, tokens, chips, lambda k: pos[1] - k)


def send_slots(slots, state, rate, tokens, chips, place):
    decay = jnp.exp(-rate * tokens)
    value = state / (1.0 - jnp.exp(-rate * (tokens * chips)))
    for k in range(1, chips + 1):
        slots[lax.rem(place(k) + 2 * chips, chips), 0 : rate.shape[0], :] = value.astype(BF16)
        if k < chips:
            value = value * decay


def block_ids(shape):
    return lax.broadcasted_iota(jnp.int32, shape, 1)


def entering_later(totals, incoming, lam_block):
    ids = block_ids(totals.shape)
    value = jnp.where(ids == SUBS - 1, rows3(incoming), pltpu.roll(totals, SUBS - 1, 1))
    power = lam_block
    for shift in (1, 2, 4):
        moved = pltpu.roll(value, SUBS - shift, 1)
        value = value + jnp.where(ids < SUBS - shift, power * moved, 0.0)
        power = power * power
    return value


def entering_earlier(totals, arriving, lam_block):
    ids = block_ids(totals.shape)
    value = jnp.where(ids == 0, rows3(arriving), pltpu.roll(totals, 1, 1))
    power = lam_block
    for shift in (1, 2, 4):
        moved = pltpu.roll(value, shift, 1)
        value = value + jnp.where(ids >= shift, power * moved, 0.0)
        power = power * power
    return value


def pole_weights(rate):
    tangent = jnp.tanh(rate)
    return jnp.sqrt(2.0 * tangent / (1.0 + tangent))


def attention_body(
    pos,
    q,
    keep_kv,
    given,
    same1,
    cross1,
    same2,
    cross2,
    delta,
    totals,
    slots_in,
    rates,
    residues,
    skip,
    dq_keep,
    dkv_keep,
    swap_out,
    out_same1,
    out_cross1,
    out_same2,
    out_cross2,
    attended,
    tail_totals,
    slots,
    qbuf,
    kbuf,
    vbuf,
    adj32,
    adj16,
    dk_acc,
    dv_acc,
    incoming_ref,
    tail_ref,
    part_ref,
    dqbuf,
):
    core = pos[0]
    rows, channels = q.shape
    width = channels // 2
    poles = rates.shape[0]
    tokens = delta.shape[1]
    steps = tokens // SUBS
    chips = slots.shape[0]
    own, other = halves(core, width)
    mine = pl.multiple_of(core * rows, rows)
    theirs = pl.multiple_of((1 - core) * rows, rows)
    scale = 1.0 / math.sqrt(HEAD)

    incoming = slots_in[0].astype(F32)
    for j in range(1, chips):
        incoming = incoming + slots_in[j].astype(F32)
    incoming_ref[...] = incoming

    for lane_group in range(width // LANES):
        gain = skip[:, pl.ds(own + lane_group * LANES, LANES)]
        for j in range(steps):
            at = pl.ds(j, SUBS, stride=steps)
            adj32[lane_group, at, :] = gain * delta[lane_group, at, :]

    def adjoint_group(first_pole, lane_group, first_lane):
        rate = rates[pl.ds(first_pole, GROUP), pl.ds(own + first_lane, LANES)]
        lam = rows3(jnp.exp(-rate))
        mixing = rows3(
            residues[pl.ds(first_pole, GROUP), pl.ds(own + first_lane, LANES)] * pole_weights(rate)
        )
        lane_at = pl.ds(first_lane, LANES)
        state = entering_later(
            totals[pl.ds(first_pole, GROUP), :, lane_at],
            incoming_ref[pl.ds(first_pole, GROUP), lane_at],
            rows3(jnp.exp(-rate * steps)),
        )
        for j in reversed(range(steps)):
            at = pl.ds(j, SUBS, stride=steps)
            state = lam * state + delta[lane_group, at, :][None]
            adj32[lane_group, at, :] = adj32[lane_group, at, :] + jnp.sum(mixing * state, axis=0)

    each_group(poles, width, adjoint_group)
    adj16[...] = adj32[...].astype(BF16)

    qbuf[pl.ds(mine, rows), :] = q[:, pl.ds(own, width)]
    qbuf[pl.ds(theirs, rows), :] = given[2]
    for slot, buf in ((0, kbuf), (1, vbuf)):
        buf[pl.ds(mine, rows), :] = same2[slot]
        buf[pl.ds(theirs, rows), :] = cross2[slot]
        buf[pl.ds(mine + tokens, rows), :] = same1[slot]
        buf[pl.ds(theirs + tokens, rows), :] = cross1[slot]
        buf[pl.ds(mine + 2 * tokens, rows), :] = keep_kv[slot]
        buf[pl.ds(theirs + 2 * tokens, rows), :] = given[slot]

    span = (WIN + 1) * rows
    key_ids = lax.broadcasted_iota(jnp.int32, (span, rows), 0)
    row_ids = lax.broadcasted_iota(jnp.int32, (span, rows), 1)
    allowed = (key_ids > row_ids) & (key_ids <= row_ids + WIN * rows)
    over_keys = (((0,), (0,)), ((), ()))
    over_head = (((1,), (1,)), ((), ()))
    for head in range(width // HEAD):
        at_head = slice(head * HEAD, (head + 1) * HEAD)
        for block in range(tokens // rows):
            at_rows = slice(block * rows, (block + 1) * rows)
            at_keys = slice(block * rows, block * rows + span)
            query = qbuf[at_rows, at_head]
            key = kbuf[at_keys, at_head]
            value = vbuf[at_keys, at_head]
            adjoint = adj16[head, at_rows, :]
            scores = lax.dot_general(key, query, over_head, preferred_element_type=F32) * scale
            scores = jnp.where(allowed, scores, -jnp.inf)
            raised = jnp.exp(scores - jnp.max(scores, axis=0, keepdims=True))
            probability = raised * (1.0 / jnp.sum(raised, axis=0, keepdims=True))
            rounded = probability.astype(BF16)
            attended[head, at_rows, :] = (
                lax.dot_general(rounded, value, over_keys, preferred_element_type=F32)
                .astype(BF16)
                .astype(F32)
            )
            weight = lax.dot_general(value, adjoint, over_head, preferred_element_type=F32)
            inner = jnp.sum(probability * weight, axis=0, keepdims=True)
            score_adjoint = (probability * (weight - inner) * scale).astype(BF16)
            dqbuf[at_rows, at_head] = lax.dot_general(
                score_adjoint, key, over_keys, preferred_element_type=F32
            ).astype(BF16)
            dk = jnp.dot(score_adjoint, query, preferred_element_type=F32)
            dv = jnp.dot(rounded, adjoint, preferred_element_type=F32)
            if block == 0:
                dk_acc[at_keys, at_head] = dk
                dv_acc[at_keys, at_head] = dv
            else:
                edge = span - rows
                first = slice(block * rows, block * rows + edge)
                last = slice(block * rows + edge, block * rows + span)
                dk_acc[first, at_head] = dk_acc[first, at_head] + dk[:edge]
                dv_acc[first, at_head] = dv_acc[first, at_head] + dv[:edge]
                dk_acc[last, at_head] = dk[edge:]
                dv_acc[last, at_head] = dv[edge:]

    for slot, acc in ((0, dk_acc), (1, dv_acc)):
        out_same2[slot] = acc[pl.ds(mine, rows), :].astype(BF16)
        out_cross2[slot] = acc[pl.ds(theirs, rows), :].astype(BF16)
        out_same1[slot] = acc[pl.ds(mine + tokens, rows), :].astype(BF16)
        out_cross1[slot] = acc[pl.ds(theirs + tokens, rows), :].astype(BF16)
        dkv_keep[slot] = acc[pl.ds(mine + 2 * tokens, rows), :]
        swap_out[slot] = acc[pl.ds(theirs + 2 * tokens, rows), :].astype(BF16)
    swap_out[2] = dqbuf[pl.ds(theirs, rows), :]
    dq_keep[...] = dqbuf[pl.ds(mine, rows), :]

    def tail_group(first_pole, lane_group, first_lane):
        rate = rates[pl.ds(first_pole, GROUP), pl.ds(own + first_lane, LANES)]
        pole_at = pl.ds(first_pole, GROUP)
        lane_at = pl.ds(first_lane, LANES)
        lam = rows3(jnp.exp(-rate))
        state = jnp.zeros((GROUP, SUBS, LANES), F32)
        matched = jnp.zeros((GROUP, SUBS, LANES), F32)
        for j in range(steps):
            at = pl.ds(j, SUBS, stride=steps)
            state = lam * state + attended[lane_group, at, :][None]
            matched = matched + delta[lane_group, at, :][None] * state
        tail_totals[pole_at, :, lane_at] = state
        lam_block = rows3(jnp.exp(-rate * steps))
        entering = entering_earlier(state, jnp.zeros((GROUP, LANES), F32), lam_block)
        full = state + lam_block * entering
        tail = full[:, SUBS - 1, :]
        matched = matched + lam * totals[pole_at, :, lane_at] * entering
        part = jnp.sum(matched, axis=1) + jnp.exp(-rate) * tail * incoming_ref[pole_at, lane_at]
        tail_ref[pole_at, lane_at] = tail
        part_ref[pole_at, lane_at] = pole_weights(rate) * part

    each_group(poles, width, tail_group)
    rate = rates[:, pl.ds(own, width)]
    send_slots(slots, tail_ref[...], rate, tokens, chips, lambda k: pos[1] + k)
    part = part_ref[...].astype(BF16)
    for j in range(chips):
        slots[j, poles : 2 * poles, :] = part


def gate_body(
    pos,
    cot,
    given,
    attended,
    tail_totals,
    slots_in,
    rates,
    residues,
    skip,
    gate_keep,
    gate_give,
    res_keep,
    mix32,
    arriving_ref,
):
    core = pos[0]
    rows, channels = cot.shape
    width = channels // 2
    poles = rates.shape[0]
    tokens = attended.shape[1]
    steps = tokens // SUBS
    chips = slots_in.shape[0]
    own, other = halves(core, width)
    mine = pl.multiple_of(core * rows, rows)
    theirs = pl.multiple_of((1 - core) * rows, rows)
    both = slots_in[0].astype(F32)
    for j in range(1, chips):
        both = both + slots_in[j].astype(F32)
    arriving_ref[...] = both[:poles]
    total = both[poles:]
    res_keep[...] = total
    high = total.astype(BF16)
    gate_give[rows : rows + poles, :] = high
    gate_give[rows + poles : rows + 2 * poles, :] = (total - high.astype(F32)).astype(BF16)
    for lane_group in range(width // LANES):
        gain = skip[:, pl.ds(own + lane_group * LANES, LANES)]
        for j in range(steps):
            at = pl.ds(j, SUBS, stride=steps)
            mix32[lane_group, at, :] = gain * attended[lane_group, at, :]

    def group(first_pole, lane_group, first_lane):
        rate = rates[pl.ds(first_pole, GROUP), pl.ds(own + first_lane, LANES)]
        lam = rows3(jnp.exp(-rate))
        mixing = rows3(
            residues[pl.ds(first_pole, GROUP), pl.ds(own + first_lane, LANES)] * pole_weights(rate)
        )
        lane_at = pl.ds(first_lane, LANES)
        pole_at = pl.ds(first_pole, GROUP)
        state = entering_earlier(
            tail_totals[pole_at, :, lane_at],
            arriving_ref[pole_at, lane_at],
            rows3(jnp.exp(-rate * steps)),
        )
        for j in range(steps):
            at = pl.ds(j, SUBS, stride=steps)
            state = lam * state + attended[lane_group, at, :][None]
            mix32[lane_group, at, :] = mix32[lane_group, at, :] + jnp.sum(mixing * state, axis=0)

    each_group(poles, width, group)
    for lane_group in range(width // LANES):
        lanes = slice(lane_group * LANES, (lane_group + 1) * LANES)
        at_own = pl.ds(own + lane_group * LANES, LANES)
        gate_keep[:, lanes] = (
            cot[:, at_own].astype(F32) * mix32[lane_group, pl.ds(mine, rows), :]
        ).astype(BF16)
        gate_give[0:rows, lanes] = (
            given[4, :, lanes].astype(F32) * mix32[lane_group, pl.ds(theirs, rows), :]
        ).astype(BF16)


def final_body(
    pos,
    dq_keep,
    dkv_keep,
    swap_in,
    same1,
    cross1,
    same2,
    cross2,
    gate_keep,
    gate_in,
    res_keep,
    dq,
    dk,
    dv,
    dgate,
    dres,
):
    rows, width = dq_keep.shape
    poles = res_keep.shape[0]
    own, other = halves(pos[0], width)
    for slot, out in ((0, dk), (1, dv)):
        out[:, pl.ds(own, width)] = (
            dkv_keep[slot] + same1[slot].astype(F32) + same2[slot].astype(F32)
        ).astype(BF16)
        out[:, pl.ds(other, width)] = (
            swap_in[slot].astype(F32) + cross1[slot].astype(F32) + cross2[slot].astype(F32)
        ).astype(BF16)
    dq[:, pl.ds(own, width)] = dq_keep[...]
    dq[:, pl.ds(other, width)] = swap_in[2]
    dgate[:, pl.ds(own, width)] = gate_keep[...]
    dgate[:, pl.ds(other, width)] = gate_in[0:rows, :]
    dres[:, pl.ds(own, width)] = res_keep[...]
    dres[:, pl.ds(other, width)] = gate_in[rows : rows + poles, :].astype(F32) + gate_in[
        rows + poles : rows + 2 * poles, :
    ].astype(F32)


def chip_shift(array, by, crossed):
    members = lax.axis_size("ctx")
    pairs = []
    for source in range(members):
        chip, core = source // 2, source % 2
        target = ((chip + by) % (members // 2)) * 2 + ((1 - core) if crossed else core)
        pairs.append((source, target))
    return lax.ppermute(array, "ctx", pairs)


def chip_exchange(slots):
    members = lax.axis_size("ctx")
    groups = [list(range(core, members, 2)) for core in range(2)]
    return lax.all_to_all(slots, "ctx", 0, 0, axis_index_groups=groups)


def local(queries, key_rows, value_rows, gate_values, cotangent, decay_rates, residues, skip_gain):
    rows, channels = queries.shape
    width = channels // 2
    poles = decay_rates.shape[0]
    chips = lax.axis_size("ctx") // 2
    tokens = 2 * rows
    place = lax.axis_index("ctx")
    pos = jnp.stack([place % 2, place // 2]).astype(jnp.int32)
    skip = skip_gain.reshape(1, channels)
    pair = (2, rows, width)
    keep_kv, give_kv, give_all = call(
        pack_body, [(pair, BF16), (pair, BF16), ((5, rows, width), BF16)], count=6, name="pack"
    )(pos, queries, key_rows, value_rows, gate_values, cotangent)
    given = chip_shift(give_all, 0, True)
    same1 = chip_shift(keep_kv, 1, False)
    cross1 = chip_shift(give_kv, 1, True)
    same2 = chip_shift(keep_kv, 2, False)
    cross2 = chip_shift(give_kv, 2, True)
    delta, totals, head_slots = call(
        head_body,
        [
            ((width // LANES, tokens, LANES), F32),
            ((poles, SUBS, width), F32),
            ((chips, poles, width), BF16),
        ],
        scratch=[pltpu.VMEM((poles, width), F32)],
        count=5,
        name="head_states",
    )(pos, gate_values, cotangent, given, decay_rates)
    head_in = chip_exchange(head_slots)
    span = (WIN + 2) * rows
    outs = call(
        attention_body,
        [
            ((rows, width), BF16),
            (pair, F32),
            ((3, rows, width), BF16),
            (pair, BF16),
            (pair, BF16),
            (pair, BF16),
            (pair, BF16),
            ((width // LANES, tokens, LANES), F32),
            ((poles, SUBS, width), F32),
            ((chips, 2 * poles, width), BF16),
        ],
        scratch=[
            pltpu.VMEM((tokens, width), BF16),
            pltpu.VMEM((span, width), BF16),
            pltpu.VMEM((span, width), BF16),
            pltpu.VMEM((width // LANES, tokens, LANES), F32),
            pltpu.VMEM((width // LANES, tokens, LANES), BF16),
            pltpu.VMEM((span, width), F32),
            pltpu.VMEM((span, width), F32),
            pltpu.VMEM((poles, width), F32),
            pltpu.VMEM((poles, width), F32),
            pltpu.VMEM((poles, width), F32),
            pltpu.VMEM((tokens, width), BF16),
        ],
        count=14,
        name="attention",
    )(
        pos,
        queries,
        keep_kv,
        given,
        same1,
        cross1,
        same2,
        cross2,
        delta,
        totals,
        head_in,
        decay_rates,
        residues,
        skip,
    )
    dq_keep, dkv_keep, swap_out, out_same1, out_cross1, out_same2, out_cross2 = outs[:7]
    attended, tail_totals, tail_slots = outs[7:]
    tail_in = chip_exchange(tail_slots)
    back_same1 = chip_shift(out_same1, -1, False)
    back_cross1 = chip_shift(out_cross1, -1, True)
    back_same2 = chip_shift(out_same2, -2, False)
    back_cross2 = chip_shift(out_cross2, -2, True)
    swap_in = chip_shift(swap_out, 0, True)
    gate_keep, gate_give, res_keep = call(
        gate_body,
        [
            ((rows, width), BF16),
            ((rows + 2 * poles, width), BF16),
            ((poles, width), F32),
        ],
        scratch=[pltpu.VMEM((width // LANES, tokens, LANES), F32), pltpu.VMEM((poles, width), F32)],
        count=9,
        name="gate",
    )(pos, cotangent, given, attended, tail_totals, tail_in, decay_rates, residues, skip)
    gate_in = chip_shift(gate_give, 0, True)
    full = (rows, channels)
    return tuple(
        call(
            final_body,
            [(full, BF16), (full, BF16), (full, BF16), (full, BF16), ((poles, channels), F32)],
            count=11,
            name="final",
        )(
            pos,
            dq_keep,
            dkv_keep,
            swap_in,
            back_same1,
            back_cross1,
            back_same2,
            back_cross2,
            gate_keep,
            gate_in,
            res_keep,
        )
    )


def solution(mesh):
    wide = P(("dp", "ctx"), "head")
    in_specs = (wide, wide, wide, wide, wide, P(None, "head"), P(None, "head"), P("head"))
    out_specs = (wide, wide, wide, wide, P("dp", "head"))
    return jax.shard_map(local, mesh=mesh, in_specs=in_specs, out_specs=out_specs, check_vma=False)
```

```python
import math

import jax
import jax.numpy as jnp
from jax import lax
from jax.experimental import pallas as pl
from jax.experimental.pallas import tpu as pltpu
from jax.sharding import PartitionSpec as P

HEAD = 128
WIN = 4
LANES = 128
SUBS = 8
GROUP = 8
F32 = jnp.float32
BF16 = jnp.bfloat16


def call(body, outs, scratch=(), near=(), name=None):
    def run(*args):
        args = [
            pltpu.with_memory_space_constraint(a, pltpu.VMEM) if n in near else a
            for n, a in enumerate(args)
        ]
        return pl.pallas_call(
            body,
            out_shape=[
                pltpu.VMEM(s, d) if local_out else jax.ShapeDtypeStruct(s, d) for s, d, local_out in outs
            ],
            in_specs=[pl.BlockSpec(memory_space=pltpu.VMEM)] * len(args),
            out_specs=[pl.BlockSpec(memory_space=pltpu.VMEM)] * len(outs),
            scratch_shapes=list(scratch),
            compiler_params=pltpu.CompilerParams(vmem_limit_bytes=8 * 1024 * 1024),
            name=name,
        )(*args)

    return run


def place():
    index = lax.axis_index("ctx")
    return lax.rem(index, 2), lax.div(index, 2)


def halves(core, width):
    own = pl.multiple_of(core * width, LANES)
    other = pl.multiple_of((1 - core) * width, LANES)
    return own, other


def pack_kv_body(k, v, keep_kv, give_kv):
    width = k.shape[1] // 2
    own, other = halves(place()[0], width)
    for slot, array in ((0, k), (1, v)):
        keep_kv[slot] = array[:, pl.ds(own, width)]
        give_kv[slot] = array[:, pl.ds(other, width)]


def pack_body(give_kv, q, gate, cot, give_all):
    width = q.shape[1] // 2
    own, other = halves(place()[0], width)
    give_all[0] = give_kv[0]
    give_all[1] = give_kv[1]
    give_all[2] = q[:, pl.ds(other, width)]
    give_all[3] = gate[:, pl.ds(other, width)]
    give_all[4] = cot[:, pl.ds(other, width)]


def rows3(values):
    return jnp.broadcast_to(values[:, None, :], (values.shape[0], SUBS, values.shape[1]))


def each_group(poles, width, body):
    pole_groups = poles // GROUP
    lane_groups = width // LANES

    def step(index, carry):
        lane_group = index // pole_groups
        first_lane = pl.multiple_of(lane_group * LANES, LANES)
        first_pole = pl.multiple_of((index % pole_groups) * GROUP, GROUP)
        body(first_pole, lane_group, first_lane)
        return carry

    lax.fori_loop(0, pole_groups * lane_groups, step, 0)


def head_body(gate, cot, given, rates, delta, totals, slots, head_ref):
    rows, channels = gate.shape
    width = channels // 2
    poles = rates.shape[0]
    chips = slots.shape[0]
    core, chip = place()
    own, other = halves(core, width)
    tokens = delta.shape[1]
    steps = tokens // SUBS
    mine = pl.multiple_of(core * rows, rows)
    theirs = pl.multiple_of((1 - core) * rows, rows)
    for lane_group in range(width // LANES):
        lanes = slice(lane_group * LANES, (lane_group + 1) * LANES)
        at_own = pl.ds(own + lane_group * LANES, LANES)
        delta[lane_group, pl.ds(mine, rows), :] = gate[:, at_own].astype(F32) * cot[:, at_own].astype(F32)
        delta[lane_group, pl.ds(theirs, rows), :] = given[3, :, lanes].astype(F32) * given[
            4, :, lanes
        ].astype(F32)

    def group(first_pole, lane_group, first_lane):
        rate = rates[pl.ds(first_pole, GROUP), pl.ds(own + first_lane, LANES)]
        lam = rows3(jnp.exp(-rate))
        state = jnp.zeros((GROUP, SUBS, LANES), F32)
        for j in reversed(range(steps)):
            state = lam * state + delta[lane_group, pl.ds(j, SUBS, stride=steps), :][None]
        totals[pl.ds(first_pole, GROUP), :, pl.ds(first_lane, LANES)] = state
        block = lax.broadcasted_iota(jnp.int32, (GROUP, SUBS, LANES), 1).astype(F32)
        power = jnp.exp(-rows3(rate) * (block * steps))
        head_ref[pl.ds(first_pole, GROUP), pl.ds(first_lane, LANES)] = jnp.sum(power * state, axis=1)

    each_group(poles, width, group)
    rate = rates[:, pl.ds(own, width)]
    send_slots(slots, head_ref[...], rate, tokens, chips, lambda k: chip - k)


def send_slots(slots, state, rate, tokens, chips, place):
    decay = jnp.exp(-rate * tokens)
    value = state / (1.0 - jnp.exp(-rate * (tokens * chips)))
    for k in range(1, chips + 1):
        slots[lax.rem(place(k) + 2 * chips, chips), 0 : rate.shape[0], :] = value.astype(BF16)
        if k < chips:
            value = value * decay


def block_ids(shape):
    return lax.broadcasted_iota(jnp.int32, shape, 1)


def entering_later(totals, incoming, lam_block):
    ids = block_ids(totals.shape)
    value = jnp.where(ids == SUBS - 1, rows3(incoming), pltpu.roll(totals, SUBS - 1, 1))
    power = lam_block
    for shift in (1, 2, 4):
        moved = pltpu.roll(value, SUBS - shift, 1)
        value = value + jnp.where(ids < SUBS - shift, power * moved, 0.0)
        power = power * power
    return value


def entering_earlier(totals, arriving, lam_block):
    ids = block_ids(totals.shape)
    value = jnp.where(ids == 0, rows3(arriving), pltpu.roll(totals, 1, 1))
    power = lam_block
    for shift in (1, 2, 4):
        moved = pltpu.roll(value, shift, 1)
        value = value + jnp.where(ids >= shift, power * moved, 0.0)
        power = power * power
    return value


def pole_weights(rate):
    tangent = jnp.tanh(rate)
    return jnp.sqrt(2.0 * tangent / (1.0 + tangent))


def adjoint_body(delta, totals, slots_in, rates, residues, skip, adj16, incoming_ref, adj32):
    width = delta.shape[0] * LANES
    poles = rates.shape[0]
    tokens = delta.shape[1]
    steps = tokens // SUBS
    chips = slots_in.shape[0]
    core, chip = place()
    own, other = halves(core, width)
    incoming = slots_in[0].astype(F32)
    for j in range(1, chips):
        incoming = incoming + slots_in[j].astype(F32)
    incoming_ref[...] = incoming

    for lane_group in range(width // LANES):
        gain = skip[:, pl.ds(own + lane_group * LANES, LANES)]
        for j in range(steps):
            at = pl.ds(j, SUBS, stride=steps)
            adj32[lane_group, at, :] = gain * delta[lane_group, at, :]

    def adjoint_group(first_pole, lane_group, first_lane):
        rate = rates[pl.ds(first_pole, GROUP), pl.ds(own + first_lane, LANES)]
        lam = rows3(jnp.exp(-rate))
        mixing = rows3(
            residues[pl.ds(first_pole, GROUP), pl.ds(own + first_lane, LANES)] * pole_weights(rate)
        )
        lane_at = pl.ds(first_lane, LANES)
        state = entering_later(
            totals[pl.ds(first_pole, GROUP), :, lane_at],
            incoming_ref[pl.ds(first_pole, GROUP), lane_at],
            rows3(jnp.exp(-rate * steps)),
        )
        for j in reversed(range(steps)):
            at = pl.ds(j, SUBS, stride=steps)
            state = lam * state + delta[lane_group, at, :][None]
            adj32[lane_group, at, :] = adj32[lane_group, at, :] + jnp.sum(mixing * state, axis=0)

    each_group(poles, width, adjoint_group)
    adj16[...] = adj32[...].astype(BF16)


def attention_body(
    q,
    keep_kv,
    given,
    same1,
    cross1,
    same2,
    cross2,
    delta,
    totals,
    adj16,
    incoming_ref,
    rates,
    dq_keep,
    dkv_keep,
    swap_out,
    out_same1,
    out_cross1,
    out_same2,
    out_cross2,
    attended,
    tail_totals,
    slots,
    qbuf,
    kbuf,
    vbuf,
    dk_acc,
    dv_acc,
    tail_ref,
    part_ref,
    dqbuf,
):
    core, chip = place()
    rows, channels = q.shape
    width = channels // 2
    poles = rates.shape[0]
    tokens = delta.shape[1]
    steps = tokens // SUBS
    chips = slots.shape[0]
    own, other = halves(core, width)
    mine = pl.multiple_of(core * rows, rows)
    theirs = pl.multiple_of((1 - core) * rows, rows)
    scale = 1.0 / math.sqrt(HEAD)

    qbuf[pl.ds(mine, rows), :] = q[:, pl.ds(own, width)]
    qbuf[pl.ds(theirs, rows), :] = given[2]
    for slot, buf in ((0, kbuf), (1, vbuf)):
        buf[pl.ds(mine, rows), :] = same2[slot]
        buf[pl.ds(theirs, rows), :] = cross2[slot]
        buf[pl.ds(mine + tokens, rows), :] = same1[slot]
        buf[pl.ds(theirs + tokens, rows), :] = cross1[slot]
        buf[pl.ds(mine + 2 * tokens, rows), :] = keep_kv[slot]
        buf[pl.ds(theirs + 2 * tokens, rows), :] = given[slot]

    span = (WIN + 1) * rows
    key_ids = lax.broadcasted_iota(jnp.int32, (span, rows), 0)
    row_ids = lax.broadcasted_iota(jnp.int32, (span, rows), 1)
    allowed = (key_ids > row_ids) & (key_ids <= row_ids + WIN * rows)
    over_keys = (((0,), (0,)), ((), ()))
    over_head = (((1,), (1,)), ((), ()))
    for head in range(width // HEAD):
        at_head = slice(head * HEAD, (head + 1) * HEAD)
        for block in range(tokens // rows):
            at_rows = slice(block * rows, (block + 1) * rows)
            at_keys = slice(block * rows, block * rows + span)
            query = qbuf[at_rows, at_head]
            key = kbuf[at_keys, at_head]
            value = vbuf[at_keys, at_head]
            adjoint = adj16[head, at_rows, :]
            scores = lax.dot_general(key, query, over_head, preferred_element_type=F32) * scale
            scores = jnp.where(allowed, scores, -jnp.inf)
            raised = jnp.exp(scores - jnp.max(scores, axis=0, keepdims=True))
            probability = raised * (1.0 / jnp.sum(raised, axis=0, keepdims=True))
            rounded = probability.astype(BF16)
            attended[head, at_rows, :] = (
                lax.dot_general(rounded, value, over_keys, preferred_element_type=F32)
                .astype(BF16)
                .astype(F32)
            )
            weight = lax.dot_general(value, adjoint, over_head, preferred_element_type=F32)
            inner = jnp.sum(probability * weight, axis=0, keepdims=True)
            score_adjoint = (probability * (weight - inner) * scale).astype(BF16)
            dqbuf[at_rows, at_head] = lax.dot_general(
                score_adjoint, key, over_keys, preferred_element_type=F32
            ).astype(BF16)
            dk = jnp.dot(score_adjoint, query, preferred_element_type=F32)
            dv = jnp.dot(rounded, adjoint, preferred_element_type=F32)
            if block == 0:
                dk_acc[at_keys, at_head] = dk
                dv_acc[at_keys, at_head] = dv
            else:
                edge = span - rows
                first = slice(block * rows, block * rows + edge)
                last = slice(block * rows + edge, block * rows + span)
                dk_acc[first, at_head] = dk_acc[first, at_head] + dk[:edge]
                dv_acc[first, at_head] = dv_acc[first, at_head] + dv[:edge]
                dk_acc[last, at_head] = dk[edge:]
                dv_acc[last, at_head] = dv[edge:]

    for slot, acc in ((0, dk_acc), (1, dv_acc)):
        out_same2[slot] = acc[pl.ds(mine, rows), :].astype(BF16)
        out_cross2[slot] = acc[pl.ds(theirs, rows), :].astype(BF16)
        out_same1[slot] = acc[pl.ds(mine + tokens, rows), :].astype(BF16)
        out_cross1[slot] = acc[pl.ds(theirs + tokens, rows), :].astype(BF16)
        dkv_keep[slot] = acc[pl.ds(mine + 2 * tokens, rows), :]
        swap_out[slot] = acc[pl.ds(theirs + 2 * tokens, rows), :].astype(BF16)
    swap_out[2] = dqbuf[pl.ds(theirs, rows), :]
    dq_keep[...] = dqbuf[pl.ds(mine, rows), :]

    def tail_group(first_pole, lane_group, first_lane):
        rate = rates[pl.ds(first_pole, GROUP), pl.ds(own + first_lane, LANES)]
        pole_at = pl.ds(first_pole, GROUP)
        lane_at = pl.ds(first_lane, LANES)
        lam = rows3(jnp.exp(-rate))
        state = jnp.zeros((GROUP, SUBS, LANES), F32)
        matched = jnp.zeros((GROUP, SUBS, LANES), F32)
        for j in range(steps):
            at = pl.ds(j, SUBS, stride=steps)
            state = lam * state + attended[lane_group, at, :][None]
            matched = matched + delta[lane_group, at, :][None] * state
        tail_totals[pole_at, :, lane_at] = state
        lam_block = rows3(jnp.exp(-rate * steps))
        entering = entering_earlier(state, jnp.zeros((GROUP, LANES), F32), lam_block)
        full = state + lam_block * entering
        tail = full[:, SUBS - 1, :]
        matched = matched + lam * totals[pole_at, :, lane_at] * entering
        part = jnp.sum(matched, axis=1) + jnp.exp(-rate) * tail * incoming_ref[pole_at, lane_at]
        tail_ref[pole_at, lane_at] = tail
        part_ref[pole_at, lane_at] = pole_weights(rate) * part

    each_group(poles, width, tail_group)
    rate = rates[:, pl.ds(own, width)]
    send_slots(slots, tail_ref[...], rate, tokens, chips, lambda k: chip + k)
    part = part_ref[...].astype(BF16)
    for j in range(chips):
        slots[j, poles : 2 * poles, :] = part


def gate_body(cot,
    given,
    attended,
    tail_totals,
    slots_in,
    rates,
    residues,
    skip,
    gate_keep,
    gate_give,
    res_keep,
    mix32,
    arriving_ref,
):
    core, chip = place()
    rows, channels = cot.shape
    width = channels // 2
    poles = rates.shape[0]
    tokens = attended.shape[1]
    steps = tokens // SUBS
    chips = slots_in.shape[0]
    own, other = halves(core, width)
    mine = pl.multiple_of(core * rows, rows)
    theirs = pl.multiple_of((1 - core) * rows, rows)
    both = slots_in[0].astype(F32)
    for j in range(1, chips):
        both = both + slots_in[j].astype(F32)
    arriving_ref[...] = both[:poles]
    total = both[poles:]
    res_keep[...] = total
    high = total.astype(BF16)
    gate_give[rows : rows + poles, :] = high
    gate_give[rows + poles : rows + 2 * poles, :] = (total - high.astype(F32)).astype(BF16)
    for lane_group in range(width // LANES):
        gain = skip[:, pl.ds(own + lane_group * LANES, LANES)]
        for j in range(steps):
            at = pl.ds(j, SUBS, stride=steps)
            mix32[lane_group, at, :] = gain * attended[lane_group, at, :]

    def group(first_pole, lane_group, first_lane):
        rate = rates[pl.ds(first_pole, GROUP), pl.ds(own + first_lane, LANES)]
        lam = rows3(jnp.exp(-rate))
        mixing = rows3(
            residues[pl.ds(first_pole, GROUP), pl.ds(own + first_lane, LANES)] * pole_weights(rate)
        )
        lane_at = pl.ds(first_lane, LANES)
        pole_at = pl.ds(first_pole, GROUP)
        state = entering_earlier(
            tail_totals[pole_at, :, lane_at],
            arriving_ref[pole_at, lane_at],
            rows3(jnp.exp(-rate * steps)),
        )
        for j in range(steps):
            at = pl.ds(j, SUBS, stride=steps)
            state = lam * state + attended[lane_group, at, :][None]
            mix32[lane_group, at, :] = mix32[lane_group, at, :] + jnp.sum(mixing * state, axis=0)

    each_group(poles, width, group)
    for lane_group in range(width // LANES):
        lanes = slice(lane_group * LANES, (lane_group + 1) * LANES)
        at_own = pl.ds(own + lane_group * LANES, LANES)
        gate_keep[:, lanes] = (
            cot[:, at_own].astype(F32) * mix32[lane_group, pl.ds(mine, rows), :]
        ).astype(BF16)
        gate_give[0:rows, lanes] = (
            given[4, :, lanes].astype(F32) * mix32[lane_group, pl.ds(theirs, rows), :]
        ).astype(BF16)


def final_body(dq_keep,
    dkv_keep,
    swap_in,
    same1,
    cross1,
    same2,
    cross2,
    gate_keep,
    gate_in,
    res_keep,
    dq,
    dk,
    dv,
    dgate,
    dres,
):
    rows, width = dq_keep.shape
    poles = res_keep.shape[0]
    own, other = halves(place()[0], width)
    for slot, out in ((0, dk), (1, dv)):
        out[:, pl.ds(own, width)] = (
            dkv_keep[slot] + same1[slot].astype(F32) + same2[slot].astype(F32)
        ).astype(BF16)
        out[:, pl.ds(other, width)] = (
            swap_in[slot].astype(F32) + cross1[slot].astype(F32) + cross2[slot].astype(F32)
        ).astype(BF16)
    dq[:, pl.ds(own, width)] = dq_keep[...]
    dq[:, pl.ds(other, width)] = swap_in[2]
    dgate[:, pl.ds(own, width)] = gate_keep[...]
    dgate[:, pl.ds(other, width)] = gate_in[0:rows, :]
    dres[:, pl.ds(own, width)] = res_keep[...]
    dres[:, pl.ds(other, width)] = gate_in[rows : rows + poles, :].astype(F32) + gate_in[
        rows + poles : rows + 2 * poles, :
    ].astype(F32)


def chip_shift(array, by, crossed):
    members = lax.axis_size("ctx")
    pairs = []
    for source in range(members):
        chip, core = source // 2, source % 2
        target = ((chip + by) % (members // 2)) * 2 + ((1 - core) if crossed else core)
        pairs.append((source, target))
    return lax.ppermute(array, "ctx", pairs)


def chip_exchange(slots):
    members = lax.axis_size("ctx")
    groups = [list(range(core, members, 2)) for core in range(2)]
    return lax.all_to_all(slots, "ctx", 0, 0, axis_index_groups=groups)


def local(queries, key_rows, value_rows, gate_values, cotangent, decay_rates, residues, skip_gain):
    rows, channels = queries.shape
    width = channels // 2
    poles = decay_rates.shape[0]
    chips = lax.axis_size("ctx") // 2
    tokens = 2 * rows
    skip = skip_gain.reshape(1, channels)
    groups = width // LANES
    pair = (2, rows, width)
    split = (groups, tokens, LANES)
    states = (poles, SUBS, width)
    span = (WIN + 2) * rows
    keep_kv, give_kv = call(pack_kv_body, [(pair, BF16, True), (pair, BF16, True)], name="pack_kv")(
        key_rows, value_rows
    )
    (give_all,) = call(pack_body, [((5, rows, width), BF16, True)], near=(0,), name="pack")(
        give_kv, queries, gate_values, cotangent
    )
    same2 = chip_shift(keep_kv, 2, False)
    cross2 = chip_shift(give_kv, 2, True)
    same1 = chip_shift(keep_kv, 1, False)
    cross1 = chip_shift(give_kv, 1, True)
    given = chip_shift(give_all, 0, True)
    delta, totals, head_slots = call(
        head_body,
        [(split, F32, True), (states, F32, True), ((chips, poles, width), BF16, True)],
        scratch=[pltpu.VMEM((poles, width), F32)],
        near=(2,),
        name="head_states",
    )(gate_values, cotangent, given, decay_rates)
    head_in = chip_exchange(head_slots)
    adjoint, incoming = call(
        adjoint_body,
        [(split, BF16, True), ((poles, width), F32, True)],
        scratch=[pltpu.VMEM(split, F32)],
        near=(0, 1, 2),
        name="adjoint",
    )(delta, totals, head_in, decay_rates, residues, skip)
    outs = call(
        attention_body,
        [
            ((rows, width), BF16, True),
            (pair, F32, True),
            ((3, rows, width), BF16, True),
            (pair, BF16, True),
            (pair, BF16, True),
            (pair, BF16, True),
            (pair, BF16, True),
            (split, F32, True),
            (states, F32, True),
            ((chips, 2 * poles, width), BF16, True),
        ],
        scratch=[
            pltpu.VMEM((tokens, width), BF16),
            pltpu.VMEM((span, width), BF16),
            pltpu.VMEM((span, width), BF16),
            pltpu.VMEM((span, width), F32),
            pltpu.VMEM((span, width), F32),
            pltpu.VMEM((poles, width), F32),
            pltpu.VMEM((poles, width), F32),
            pltpu.VMEM((tokens, width), BF16),
        ],
        near=tuple(range(1, 11)),
        name="attention",
    )(
        queries,
        keep_kv,
        given,
        same1,
        cross1,
        same2,
        cross2,
        delta,
        totals,
        adjoint,
        incoming,
        decay_rates,
    )
    dq_keep, dkv_keep, swap_out, out_same1, out_cross1, out_same2, out_cross2 = outs[:7]
    attended, tail_totals, tail_slots = outs[7:]
    back_same2 = chip_shift(out_same2, -2, False)
    back_cross2 = chip_shift(out_cross2, -2, True)
    back_same1 = chip_shift(out_same1, -1, False)
    back_cross1 = chip_shift(out_cross1, -1, True)
    tail_in = chip_exchange(tail_slots)
    swap_in = chip_shift(swap_out, 0, True)
    gate_keep, gate_give, res_keep = call(
        gate_body,
        [
            ((rows, width), BF16, True),
            ((rows + 2 * poles, width), BF16, True),
            ((poles, width), F32, True),
        ],
        scratch=[pltpu.VMEM(split, F32), pltpu.VMEM((poles, width), F32)],
        near=(1, 2, 3, 4),
        name="gate",
    )(cotangent, given, attended, tail_totals, tail_in, decay_rates, residues, skip)
    gate_in = chip_shift(gate_give, 0, True)
    full = (rows, channels)
    wide = (full, BF16, False)
    return tuple(
        call(
            final_body,
            [wide, wide, wide, wide, ((poles, channels), F32, False)],
            near=tuple(range(10)),
            name="final",
        )(
            dq_keep,
            dkv_keep,
            swap_in,
            back_same1,
            back_cross1,
            back_same2,
            back_cross2,
            gate_keep,
            gate_in,
            res_keep,
        )
    )


def solution(mesh):
    wide = P(("dp", "ctx"), "head")
    in_specs = (wide, wide, wide, wide, wide, P(None, "head"), P(None, "head"), P("head"))
    out_specs = (wide, wide, wide, wide, P("dp", "head"))
    return jax.shard_map(local, mesh=mesh, in_specs=in_specs, out_specs=out_specs, check_vma=False)
```

```python
import math

import jax
import jax.numpy as jnp
from jax import lax
from jax.experimental import pallas as pl
from jax.experimental.pallas import tpu as pltpu
from jax.sharding import PartitionSpec as P

HEAD = 128
WIN = 4
LANES = 128
SUBS = 8
GROUP = 8
FORWARD_COST = pl.CostEstimate(flops=10**11, transcendentals=0, bytes_accessed=10**8)
F32 = jnp.float32
BF16 = jnp.bfloat16
OVER_KEYS = (((0,), (0,)), ((), ()))
OVER_HEAD = (((1,), (1,)), ((), ()))


def call(body, outs, scratch=(), near=(), far=(), cost=None, name=None):
    def run(*args):
        args = list(args)
        specs = []
        for n in range(len(args)):
            space = pltpu.HBM if n in far else pltpu.VMEM
            specs.append(pl.BlockSpec(memory_space=space))
            if n in near or n in far:
                args[n] = pltpu.with_memory_space_constraint(args[n], space)
        return pl.pallas_call(
            body,
            out_shape=[
                pltpu.VMEM(s, d) if local_out else jax.ShapeDtypeStruct(s, d) for s, d, local_out in outs
            ],
            in_specs=specs,
            out_specs=[pl.BlockSpec(memory_space=pltpu.VMEM)] * len(outs),
            scratch_shapes=list(scratch),
            compiler_params=pltpu.CompilerParams(vmem_limit_bytes=8 * 1024 * 1024),
            cost_estimate=cost,
            name=name,
        )(*args)

    return run


def place():
    index = lax.axis_index("ctx")
    return lax.rem(index, 2), lax.div(index, 2)


def halves(core, width):
    own = pl.multiple_of(core * width, LANES)
    other = pl.multiple_of((1 - core) * width, LANES)
    return own, other


def pack_body(
    k, v, q, gate, cot, rates, residues, skip, keep_kv, give_kv, keep_rest, give_all, params, buf, small, sems
):
    width = k.shape[1] // 2
    poles = rates.shape[0]
    own, other = halves(place()[0], width)
    arrays = (k, v, q, gate, cot)
    copies = [pltpu.make_async_copy(a, buf.at[n], sems.at[n]) for n, a in enumerate(arrays)]
    for n, (array, first, count) in enumerate(
        ((rates, 0, poles), (residues, poles, poles), (skip, 2 * poles, 1))
    ):
        copies.append(
            pltpu.make_async_copy(array, small.at[pl.ds(first, count)], sems.at[len(arrays) + n])
        )
    for copy in copies:
        copy.start()
    for n in range(len(arrays)):
        copies[n].wait()
        give = buf[n, :, pl.ds(other, width)]
        keep = buf[n, :, pl.ds(own, width)]
        give_all[n] = give
        if n < 2:
            give_kv[n] = give
            keep_kv[n] = keep
        else:
            keep_rest[n - 2] = keep
    for copy in copies[len(arrays) :]:
        copy.wait()
    params[...] = small[0 : 2 * poles + 1, pl.ds(own, width)]


def rows3(values):
    return jnp.broadcast_to(values[:, None, :], (values.shape[0], SUBS, values.shape[1]))


def each_group(poles, width, body):
    pole_groups = poles // GROUP
    lane_groups = width // LANES

    def step(index, carry):
        lane_group = index // pole_groups
        first_lane = pl.multiple_of(lane_group * LANES, LANES)
        first_pole = pl.multiple_of((index % pole_groups) * GROUP, GROUP)
        body(first_pole, lane_group, first_lane)
        return carry

    lax.fori_loop(0, pole_groups * lane_groups, step, 0)


def head_body(keep_rest, given, params, delta, totals, slots, head_ref):
    rows, width = keep_rest.shape[1:]
    poles = totals.shape[0]
    chips = slots.shape[0]
    core, chip = place()
    own, other = halves(core, width)
    tokens = delta.shape[1]
    steps = tokens // SUBS
    mine = pl.multiple_of(core * rows, rows)
    theirs = pl.multiple_of((1 - core) * rows, rows)
    for lane_group in range(width // LANES):
        lanes = slice(lane_group * LANES, (lane_group + 1) * LANES)
        delta[lane_group, pl.ds(mine, rows), :] = keep_rest[1, :, lanes].astype(F32) * keep_rest[
            2, :, lanes
        ].astype(F32)
        delta[lane_group, pl.ds(theirs, rows), :] = given[3, :, lanes].astype(F32) * given[
            4, :, lanes
        ].astype(F32)

    def group(first_pole, lane_group, first_lane):
        rate = params[pl.ds(first_pole, GROUP), pl.ds(first_lane, LANES)]
        lam = rows3(jnp.exp(-rate))
        state = jnp.zeros((GROUP, SUBS, LANES), F32)
        for j in reversed(range(steps)):
            state = lam * state + delta[lane_group, pl.ds(j, SUBS, stride=steps), :][None]
        totals[pl.ds(first_pole, GROUP), :, pl.ds(first_lane, LANES)] = state
        block = lax.broadcasted_iota(jnp.int32, (GROUP, SUBS, LANES), 1).astype(F32)
        power = jnp.exp(-rows3(rate) * (block * steps))
        head_ref[pl.ds(first_pole, GROUP), pl.ds(first_lane, LANES)] = jnp.sum(power * state, axis=1)

    each_group(poles, width, group)
    head = head_ref[...].astype(BF16)
    for j in range(chips):
        slots[j] = head


def around(own, rate, tokens, order, out):
    decay = jnp.exp(-rate * tokens)
    value = own(order[-1])
    power = decay
    for n in reversed(order[:-1]):
        value = value + power * own(n)
        power = power * decay
    value = value / (1.0 - jnp.exp(-rate * (tokens * len(order))))
    for n in order:
        out[n] = value
        value = own(n) + decay * value


def block_ids(shape):
    return lax.broadcasted_iota(jnp.int32, shape, 1)


def entering_later(totals, incoming, lam_block):
    ids = block_ids(totals.shape)
    value = jnp.where(ids == SUBS - 1, rows3(incoming), pltpu.roll(totals, SUBS - 1, 1))
    power = lam_block
    for shift in (1, 2, 4):
        moved = pltpu.roll(value, SUBS - shift, 1)
        value = value + jnp.where(ids < SUBS - shift, power * moved, 0.0)
        power = power * power
    return value


def entering_earlier(totals, arriving, lam_block):
    ids = block_ids(totals.shape)
    value = jnp.where(ids == 0, rows3(arriving), pltpu.roll(totals, 1, 1))
    power = lam_block
    for shift in (1, 2, 4):
        moved = pltpu.roll(value, shift, 1)
        value = value + jnp.where(ids >= shift, power * moved, 0.0)
        power = power * power
    return value


def pole_weights(rate):
    tangent = jnp.tanh(rate)
    return jnp.sqrt(2.0 * tangent / (1.0 + tangent))


def assemble(core, keep_rest, keep_kv, given, same1, cross1, same2, cross2, qbuf, kbuf, vbuf):
    rows = keep_rest.shape[1]
    tokens = 2 * rows
    mine = pl.multiple_of(core * rows, rows)
    theirs = pl.multiple_of((1 - core) * rows, rows)
    qbuf[pl.ds(mine, rows), :] = keep_rest[0]
    qbuf[pl.ds(theirs, rows), :] = given[2]
    for slot, buf in ((0, kbuf), (1, vbuf)):
        buf[pl.ds(mine, rows), :] = same2[slot]
        buf[pl.ds(theirs, rows), :] = cross2[slot]
        buf[pl.ds(mine + tokens, rows), :] = same1[slot]
        buf[pl.ds(theirs + tokens, rows), :] = cross1[slot]
        buf[pl.ds(mine + 2 * tokens, rows), :] = keep_kv[slot]
        buf[pl.ds(theirs + 2 * tokens, rows), :] = given[slot]


def allowed_pairs(rows):
    span = (WIN + 1) * rows
    key_ids = lax.broadcasted_iota(jnp.int32, (span, rows), 0)
    row_ids = lax.broadcasted_iota(jnp.int32, (span, rows), 1)
    return (key_ids > row_ids) & (key_ids <= row_ids + WIN * rows)


def forward_body(
    keep_rest,
    keep_kv,
    given,
    same1,
    cross1,
    same2,
    cross2,
    delta,
    totals,
    params,
    stats,
    attended,
    tail_totals,
    slots,
    qbuf,
    kbuf,
    vbuf,
    tail_ref,
    part_ref,
):
    rows, width = keep_rest.shape[1:]
    poles = totals.shape[0]
    tokens = delta.shape[1]
    steps = tokens // SUBS
    chips = slots.shape[0]
    core, chip = place()
    scale = 1.0 / math.sqrt(HEAD)
    assemble(core, keep_rest, keep_kv, given, same1, cross1, same2, cross2, qbuf, kbuf, vbuf)
    span = (WIN + 1) * rows
    allowed = allowed_pairs(rows)
    for head in range(width // HEAD):
        at_head = slice(head * HEAD, (head + 1) * HEAD)
        for block in range(tokens // rows):
            at_rows = slice(block * rows, (block + 1) * rows)
            at_keys = slice(block * rows, block * rows + span)
            scores = (
                lax.dot_general(
                    kbuf[at_keys, at_head], qbuf[at_rows, at_head], OVER_HEAD, preferred_element_type=F32
                )
                * scale
            )
            scores = jnp.where(allowed, scores, -jnp.inf)
            top = jnp.max(scores, axis=0, keepdims=True)
            raised = jnp.exp(scores - top)
            share = 1.0 / jnp.sum(raised, axis=0, keepdims=True)
            probability = raised * share
            stats[head, block, 0:1, :] = top
            stats[head, block, 1:2, :] = share
            attended[head, at_rows, :] = (
                lax.dot_general(
                    probability.astype(BF16), vbuf[at_keys, at_head], OVER_KEYS, preferred_element_type=F32
                )
                .astype(BF16)
                .astype(F32)
            )

    def tail_group(first_pole, lane_group, first_lane):
        rate = params[pl.ds(first_pole, GROUP), pl.ds(first_lane, LANES)]
        pole_at = pl.ds(first_pole, GROUP)
        lane_at = pl.ds(first_lane, LANES)
        lam = rows3(jnp.exp(-rate))
        state = jnp.zeros((GROUP, SUBS, LANES), F32)
        matched = jnp.zeros((GROUP, SUBS, LANES), F32)
        for j in range(steps):
            at = pl.ds(j, SUBS, stride=steps)
            state = lam * state + attended[lane_group, at, :][None]
            matched = matched + delta[lane_group, at, :][None] * state
        tail_totals[pole_at, :, lane_at] = state
        lam_block = rows3(jnp.exp(-rate * steps))
        entering = entering_earlier(state, jnp.zeros((GROUP, LANES), F32), lam_block)
        full = state + lam_block * entering
        matched = matched + lam * totals[pole_at, :, lane_at] * entering
        tail_ref[pole_at, lane_at] = full[:, SUBS - 1, :]
        part_ref[pole_at, lane_at] = jnp.sum(matched, axis=1)

    each_group(poles, width, tail_group)
    tail = tail_ref[...].astype(BF16)
    part = part_ref[...].astype(BF16)
    for j in range(chips):
        slots[j, 0:poles, :] = tail
        slots[j, poles : 2 * poles, :] = part


def backward_body(
    keep_rest,
    keep_kv,
    given,
    same1,
    cross1,
    same2,
    cross2,
    stats,
    delta,
    totals,
    slots_in,
    params,
    dq_keep,
    dkv_keep,
    swap_out,
    out_same1,
    out_cross1,
    out_same2,
    out_cross2,
    incoming_all,
    qbuf,
    kbuf,
    vbuf,
    adj16,
    adj32,
    dk_acc,
    dv_acc,
    dqbuf,
):
    tokens, width = qbuf.shape
    rows = tokens // 2
    poles = totals.shape[0]
    steps = tokens // SUBS
    chips = slots_in.shape[0]
    core, chip = place()
    mine = pl.multiple_of(core * rows, rows)
    theirs = pl.multiple_of((1 - core) * rows, rows)
    scale = 1.0 / math.sqrt(HEAD)
    assemble(core, keep_rest, keep_kv, given, same1, cross1, same2, cross2, qbuf, kbuf, vbuf)

    around(
        lambda n: slots_in[n].astype(F32),
        params[0:poles, :],
        tokens,
        list(reversed(range(chips))),
        incoming_all,
    )
    for lane_group in range(width // LANES):
        gain = params[2 * poles : 2 * poles + 1, lane_group * LANES : (lane_group + 1) * LANES]
        adj32[lane_group] = gain * delta[lane_group]

    def adjoint_group(first_pole, lane_group, first_lane):
        rate = params[pl.ds(first_pole, GROUP), pl.ds(first_lane, LANES)]
        lam = rows3(jnp.exp(-rate))
        mixing = rows3(
            params[pl.ds(poles + first_pole, GROUP), pl.ds(first_lane, LANES)] * pole_weights(rate)
        )
        lane_at = pl.ds(first_lane, LANES)
        state = entering_later(
            totals[pl.ds(first_pole, GROUP), :, lane_at],
            incoming_all[chip, pl.ds(first_pole, GROUP), lane_at],
            rows3(jnp.exp(-rate * steps)),
        )
        for j in reversed(range(steps)):
            at = pl.ds(j, SUBS, stride=steps)
            state = lam * state + delta[lane_group, at, :][None]
            adj32[lane_group, at, :] = adj32[lane_group, at, :] + jnp.sum(mixing * state, axis=0)

    each_group(poles, width, adjoint_group)
    adj16[...] = adj32[...].astype(BF16)

    span = (WIN + 1) * rows
    allowed = allowed_pairs(rows)
    for head in range(width // HEAD):
        at_head = slice(head * HEAD, (head + 1) * HEAD)
        for block in range(tokens // rows):
            at_rows = slice(block * rows, (block + 1) * rows)
            at_keys = slice(block * rows, block * rows + span)
            query = qbuf[at_rows, at_head]
            key = kbuf[at_keys, at_head]
            value = vbuf[at_keys, at_head]
            adjoint = adj16[head, at_rows, :]
            scores = lax.dot_general(key, query, OVER_HEAD, preferred_element_type=F32) * scale
            scores = jnp.where(allowed, scores, -jnp.inf)
            probability = jnp.exp(scores - stats[head, block, 0:1, :]) * stats[head, block, 1:2, :]
            rounded = probability.astype(BF16)
            weight = lax.dot_general(value, adjoint, OVER_HEAD, preferred_element_type=F32)
            inner = jnp.sum(probability * weight, axis=0, keepdims=True)
            score_adjoint = (probability * (weight - inner) * scale).astype(BF16)
            dqbuf[at_rows, at_head] = lax.dot_general(
                score_adjoint, key, OVER_KEYS, preferred_element_type=F32
            ).astype(BF16)
            dk = jnp.dot(score_adjoint, query, preferred_element_type=F32)
            dv = jnp.dot(rounded, adjoint, preferred_element_type=F32)
            if block == 0:
                dk_acc[at_keys, at_head] = dk
                dv_acc[at_keys, at_head] = dv
            else:
                edge = span - rows
                first = slice(block * rows, block * rows + edge)
                last = slice(block * rows + edge, block * rows + span)
                dk_acc[first, at_head] = dk_acc[first, at_head] + dk[:edge]
                dv_acc[first, at_head] = dv_acc[first, at_head] + dv[:edge]
                dk_acc[last, at_head] = dk[edge:]
                dv_acc[last, at_head] = dv[edge:]

    for slot, acc in ((0, dk_acc), (1, dv_acc)):
        out_same2[slot] = acc[pl.ds(mine, rows), :].astype(BF16)
        out_cross2[slot] = acc[pl.ds(theirs, rows), :].astype(BF16)
        out_same1[slot] = acc[pl.ds(mine + tokens, rows), :].astype(BF16)
        out_cross1[slot] = acc[pl.ds(theirs + tokens, rows), :].astype(BF16)
        dkv_keep[slot] = acc[pl.ds(mine + 2 * tokens, rows), :]
        swap_out[slot] = acc[pl.ds(theirs + 2 * tokens, rows), :].astype(BF16)
    swap_out[2] = dqbuf[pl.ds(theirs, rows), :]
    dq_keep[...] = dqbuf[pl.ds(mine, rows), :]


def gate_body(
    keep_rest,
    given,
    attended,
    tail_totals,
    slots_in,
    incoming_all,
    params,
    gate_keep,
    gate_give,
    res_keep,
    mix32,
    arriving_ref,
):
    core, chip = place()
    rows, width = keep_rest.shape[1:]
    poles = tail_totals.shape[0]
    tokens = attended.shape[1]
    steps = tokens // SUBS
    chips = slots_in.shape[0]
    mine = pl.multiple_of(core * rows, rows)
    theirs = pl.multiple_of((1 - core) * rows, rows)
    rate = params[0:poles, :]
    around(
        lambda n: slots_in[n, 0:poles, :].astype(F32), rate, tokens, list(range(chips)), arriving_ref
    )
    parts = slots_in[0, poles : 2 * poles, :].astype(F32)
    crossed = slots_in[0, 0:poles, :].astype(F32) * incoming_all[0]
    for n in range(1, chips):
        parts = parts + slots_in[n, poles : 2 * poles, :].astype(F32)
        crossed = crossed + slots_in[n, 0:poles, :].astype(F32) * incoming_all[n]
    total = pole_weights(rate) * (parts + jnp.exp(-rate) * crossed)
    res_keep[...] = total
    high = total.astype(BF16)
    gate_give[rows : rows + poles, :] = high
    gate_give[rows + poles : rows + 2 * poles, :] = (total - high.astype(F32)).astype(BF16)
    for lane_group in range(width // LANES):
        gain = params[2 * poles : 2 * poles + 1, lane_group * LANES : (lane_group + 1) * LANES]
        mix32[lane_group] = gain * attended[lane_group]

    def group(first_pole, lane_group, first_lane):
        rate = params[pl.ds(first_pole, GROUP), pl.ds(first_lane, LANES)]
        lam = rows3(jnp.exp(-rate))
        mixing = rows3(
            params[pl.ds(poles + first_pole, GROUP), pl.ds(first_lane, LANES)] * pole_weights(rate)
        )
        lane_at = pl.ds(first_lane, LANES)
        pole_at = pl.ds(first_pole, GROUP)
        state = entering_earlier(
            tail_totals[pole_at, :, lane_at],
            arriving_ref[chip, pole_at, lane_at],
            rows3(jnp.exp(-rate * steps)),
        )
        for j in range(steps):
            at = pl.ds(j, SUBS, stride=steps)
            state = lam * state + attended[lane_group, at, :][None]
            mix32[lane_group, at, :] = mix32[lane_group, at, :] + jnp.sum(mixing * state, axis=0)

    each_group(poles, width, group)
    for lane_group in range(width // LANES):
        lanes = slice(lane_group * LANES, (lane_group + 1) * LANES)
        gate_keep[:, lanes] = (
            keep_rest[2, :, lanes].astype(F32) * mix32[lane_group, pl.ds(mine, rows), :]
        ).astype(BF16)
        gate_give[0:rows, lanes] = (
            given[4, :, lanes].astype(F32) * mix32[lane_group, pl.ds(theirs, rows), :]
        ).astype(BF16)


def final_body(dq_keep,
    dkv_keep,
    swap_in,
    same1,
    cross1,
    same2,
    cross2,
    gate_keep,
    gate_in,
    res_keep,
    dq,
    dk,
    dv,
    dgate,
    dres,
):
    rows, width = dq_keep.shape
    poles = res_keep.shape[0]
    own, other = halves(place()[0], width)
    for slot, out in ((0, dk), (1, dv)):
        out[:, pl.ds(own, width)] = (
            dkv_keep[slot] + same1[slot].astype(F32) + same2[slot].astype(F32)
        ).astype(BF16)
        out[:, pl.ds(other, width)] = (
            swap_in[slot].astype(F32) + cross1[slot].astype(F32) + cross2[slot].astype(F32)
        ).astype(BF16)
    dq[:, pl.ds(own, width)] = dq_keep[...]
    dq[:, pl.ds(other, width)] = swap_in[2]
    dgate[:, pl.ds(own, width)] = gate_keep[...]
    dgate[:, pl.ds(other, width)] = gate_in[0:rows, :]
    dres[:, pl.ds(own, width)] = res_keep[...]
    dres[:, pl.ds(other, width)] = gate_in[rows : rows + poles, :].astype(F32) + gate_in[
        rows + poles : rows + 2 * poles, :
    ].astype(F32)


def chip_shift(array, by, crossed):
    members = lax.axis_size("ctx")
    pairs = []
    for source in range(members):
        chip, core = source // 2, source % 2
        target = ((chip + by) % (members // 2)) * 2 + ((1 - core) if crossed else core)
        pairs.append((source, target))
    return lax.ppermute(array, "ctx", pairs)


def chip_exchange(slots):
    members = lax.axis_size("ctx")
    groups = [list(range(core, members, 2)) for core in range(2)]
    return lax.all_to_all(slots, "ctx", 0, 0, axis_index_groups=groups)


def local(queries, key_rows, value_rows, gate_values, cotangent, decay_rates, residues, skip_gain):
    rows, channels = queries.shape
    width = channels // 2
    poles = decay_rates.shape[0]
    chips = lax.axis_size("ctx") // 2
    tokens = 2 * rows
    skip = skip_gain.reshape(1, channels)
    groups = width // LANES
    pair = (2, rows, width)
    split = (groups, tokens, LANES)
    states = (poles, SUBS, width)
    span = (WIN + 2) * rows
    keep_kv, give_kv, keep_rest, give_all, params = call(
        pack_body,
        [
            (pair, BF16, True),
            (pair, BF16, True),
            ((3, rows, width), BF16, True),
            ((5, rows, width), BF16, True),
            ((2 * poles + 1, width), F32, True),
        ],
        scratch=[
            pltpu.VMEM((5, rows, channels), BF16),
            pltpu.VMEM((2 * poles + SUBS, channels), F32),
            pltpu.SemaphoreType.DMA((8,)),
        ],
        far=tuple(range(8)),
        name="pack",
    )(key_rows, value_rows, queries, gate_values, cotangent, decay_rates, residues, skip)
    same2 = chip_shift(keep_kv, 2, False)
    cross2 = chip_shift(give_kv, 2, True)
    same1 = chip_shift(keep_kv, 1, False)
    cross1 = chip_shift(give_kv, 1, True)
    given = chip_shift(give_all, 0, True)
    delta, totals, head_slots = call(
        head_body,
        [(split, F32, True), (states, F32, True), ((chips, poles, width), BF16, True)],
        scratch=[pltpu.VMEM((poles, width), F32)],
        near=(0, 1, 2),
        name="head_states",
    )(keep_rest, given, params)
    head_in = chip_exchange(head_slots)
    halo = (keep_rest, keep_kv, given, same1, cross1, same2, cross2)
    halo_buffers = [
        pltpu.VMEM((tokens, width), BF16),
        pltpu.VMEM((span, width), BF16),
        pltpu.VMEM((span, width), BF16),
    ]
    stats, attended, tail_totals, tail_slots = call(
        forward_body,
        [
            ((groups, 2, SUBS, rows), F32, True),
            (split, F32, True),
            (states, F32, True),
            ((chips, 2 * poles, width), BF16, True),
        ],
        scratch=halo_buffers + [pltpu.VMEM((poles, width), F32), pltpu.VMEM((poles, width), F32)],
        near=tuple(range(10)),
        cost=FORWARD_COST,
        name="forward",
    )(*halo, delta, totals, params)
    tail_in = chip_exchange(tail_slots)
    outs = call(
        backward_body,
        [
            ((rows, width), BF16, True),
            (pair, F32, True),
            ((3, rows, width), BF16, True),
            (pair, BF16, True),
            (pair, BF16, True),
            (pair, BF16, True),
            (pair, BF16, True),
            ((chips, poles, width), F32, True),
        ],
        scratch=halo_buffers
        + [
            pltpu.VMEM(split, BF16),
            pltpu.VMEM(split, F32),
            pltpu.VMEM((span, width), F32),
            pltpu.VMEM((span, width), F32),
            pltpu.VMEM((tokens, width), BF16),
        ],
        near=tuple(range(12)),
        name="backward",
    )(*halo, stats, delta, totals, head_in, params)
    dq_keep, dkv_keep, swap_out, out_same1, out_cross1, out_same2, out_cross2, incoming_all = outs
    back_same2 = chip_shift(out_same2, -2, False)
    back_cross2 = chip_shift(out_cross2, -2, True)
    back_same1 = chip_shift(out_same1, -1, False)
    back_cross1 = chip_shift(out_cross1, -1, True)
    swap_in = chip_shift(swap_out, 0, True)
    gate_keep, gate_give, res_keep = call(
        gate_body,
        [
            ((rows, width), BF16, True),
            ((rows + 2 * poles, width), BF16, True),
            ((poles, width), F32, True),
        ],
        scratch=[pltpu.VMEM(split, F32), pltpu.VMEM((chips, poles, width), F32)],
        near=tuple(range(7)),
        name="gate",
    )(keep_rest, given, attended, tail_totals, tail_in, incoming_all, params)
    gate_in = chip_shift(gate_give, 0, True)
    full = (rows, channels)
    wide = (full, BF16, False)
    return tuple(
        call(
            final_body,
            [wide, wide, wide, wide, ((poles, channels), F32, False)],
            near=tuple(range(10)),
            name="final",
        )(
            dq_keep,
            dkv_keep,
            swap_in,
            back_same1,
            back_cross1,
            back_same2,
            back_cross2,
            gate_keep,
            gate_in,
            res_keep,
        )
    )


def solution(mesh):
    wide = P(("dp", "ctx"), "head")
    in_specs = (wide, wide, wide, wide, wide, P(None, "head"), P(None, "head"), P("head"))
    out_specs = (wide, wide, wide, wide, P("dp", "head"))
    return jax.shard_map(local, mesh=mesh, in_specs=in_specs, out_specs=out_specs, check_vma=False)
```

```python
import math

import jax
import jax.numpy as jnp
from jax import lax
from jax.experimental import pallas as pl
from jax.experimental.pallas import tpu as pltpu
from jax.sharding import PartitionSpec as P

HEAD = 128
WIN = 4
LANES = 128
SUBS = 8
GROUP = 8
EARLY = pl.CostEstimate(flops=10**11, transcendentals=0, bytes_accessed=10**8)
F32 = jnp.float32
BF16 = jnp.bfloat16
OVER_KEYS = (((0,), (0,)), ((), ()))
OVER_HEAD = (((1,), (1,)), ((), ()))


def call(body, outs, scratch=(), near=(), far=(), cost=None, name=None):
    def run(*args):
        args = list(args)
        specs = []
        for n in range(len(args)):
            space = pltpu.HBM if n in far else pltpu.VMEM
            specs.append(pl.BlockSpec(memory_space=space))
            if n in near or n in far:
                args[n] = pltpu.with_memory_space_constraint(args[n], space)
        return pl.pallas_call(
            body,
            out_shape=[
                pltpu.VMEM(s, d) if local_out else jax.ShapeDtypeStruct(s, d) for s, d, local_out in outs
            ],
            in_specs=specs,
            out_specs=[pl.BlockSpec(memory_space=pltpu.VMEM)] * len(outs),
            scratch_shapes=list(scratch),
            compiler_params=pltpu.CompilerParams(vmem_limit_bytes=8 * 1024 * 1024),
            cost_estimate=cost,
            name=name,
        )(*args)

    return run


def place():
    index = lax.axis_index("ctx")
    return lax.rem(index, 2), lax.div(index, 2)


def halves(core, width):
    own = pl.multiple_of(core * width, LANES)
    other = pl.multiple_of((1 - core) * width, LANES)
    return own, other


def pack_body(
    k, v, q, gate, cot, rates, residues, skip, keep_kv, give_kv, keep_rest, give_all, params, buf, small, sems
):
    width = k.shape[1] // 2
    poles = rates.shape[0]
    own, other = halves(place()[0], width)
    arrays = (k, v, q, gate, cot)
    copies = [pltpu.make_async_copy(a, buf.at[n], sems.at[n]) for n, a in enumerate(arrays)]
    for n, (array, first, count) in enumerate(
        ((rates, 0, poles), (residues, poles, poles), (skip, 2 * poles, 1))
    ):
        copies.append(
            pltpu.make_async_copy(array, small.at[pl.ds(first, count)], sems.at[len(arrays) + n])
        )
    for copy in copies:
        copy.start()
    for n in range(len(arrays)):
        copies[n].wait()
        give = buf[n, :, pl.ds(other, width)]
        keep = buf[n, :, pl.ds(own, width)]
        give_all[n] = give
        if n < 2:
            give_kv[n] = give
            keep_kv[n] = keep
        else:
            keep_rest[n - 2] = keep
    for copy in copies[len(arrays) :]:
        copy.wait()
    params[...] = small[0 : 2 * poles + 1, pl.ds(own, width)]


def rows3(values):
    return jnp.broadcast_to(values[:, None, :], (values.shape[0], SUBS, values.shape[1]))


def each_group(poles, width, body):
    pole_groups = poles // GROUP
    lane_groups = width // LANES

    def step(index, carry):
        lane_group = index // pole_groups
        first_lane = pl.multiple_of(lane_group * LANES, LANES)
        first_pole = pl.multiple_of((index % pole_groups) * GROUP, GROUP)
        body(first_pole, lane_group, first_lane)
        return carry

    lax.fori_loop(0, pole_groups * lane_groups, step, 0)


def head_body(keep_rest, given, params, delta, totals, slots, head_ref):
    rows, width = keep_rest.shape[1:]
    poles = totals.shape[0]
    chips = slots.shape[0]
    core, chip = place()
    own, other = halves(core, width)
    tokens = delta.shape[1]
    steps = tokens // SUBS
    mine = pl.multiple_of(core * rows, rows)
    theirs = pl.multiple_of((1 - core) * rows, rows)
    for lane_group in range(width // LANES):
        lanes = slice(lane_group * LANES, (lane_group + 1) * LANES)
        delta[lane_group, pl.ds(mine, rows), :] = keep_rest[1, :, lanes].astype(F32) * keep_rest[
            2, :, lanes
        ].astype(F32)
        delta[lane_group, pl.ds(theirs, rows), :] = given[3, :, lanes].astype(F32) * given[
            4, :, lanes
        ].astype(F32)

    def group(first_pole, lane_group, first_lane):
        rate = params[pl.ds(first_pole, GROUP), pl.ds(first_lane, LANES)]
        lam = rows3(jnp.exp(-rate))
        state = jnp.zeros((GROUP, SUBS, LANES), F32)
        for j in reversed(range(steps)):
            state = lam * state + delta[lane_group, pl.ds(j, SUBS, stride=steps), :][None]
        totals[pl.ds(first_pole, GROUP), :, pl.ds(first_lane, LANES)] = state
        block = lax.broadcasted_iota(jnp.int32, (GROUP, SUBS, LANES), 1).astype(F32)
        power = jnp.exp(-rows3(rate) * (block * steps))
        head_ref[pl.ds(first_pole, GROUP), pl.ds(first_lane, LANES)] = jnp.sum(power * state, axis=1)

    each_group(poles, width, group)
    head = head_ref[...].astype(BF16)
    for j in range(chips):
        slots[j] = head


def around(own, rate, tokens, order, out):
    decay = jnp.exp(-rate * tokens)
    value = own(order[-1])
    power = decay
    for n in reversed(order[:-1]):
        value = value + power * own(n)
        power = power * decay
    value = value / (1.0 - jnp.exp(-rate * (tokens * len(order))))
    for n in order:
        out[n] = value
        value = own(n) + decay * value


def block_ids(shape):
    return lax.broadcasted_iota(jnp.int32, shape, 1)


def entering_later(totals, incoming, lam_block):
    ids = block_ids(totals.shape)
    value = jnp.where(ids == SUBS - 1, rows3(incoming), pltpu.roll(totals, SUBS - 1, 1))
    power = lam_block
    for shift in (1, 2, 4):
        moved = pltpu.roll(value, SUBS - shift, 1)
        value = value + jnp.where(ids < SUBS - shift, power * moved, 0.0)
        power = power * power
    return value


def entering_earlier(totals, arriving, lam_block):
    ids = block_ids(totals.shape)
    value = jnp.where(ids == 0, rows3(arriving), pltpu.roll(totals, 1, 1))
    power = lam_block
    for shift in (1, 2, 4):
        moved = pltpu.roll(value, shift, 1)
        value = value + jnp.where(ids >= shift, power * moved, 0.0)
        power = power * power
    return value


def pole_weights(rate):
    tangent = jnp.tanh(rate)
    return jnp.sqrt(2.0 * tangent / (1.0 + tangent))


def assemble(core, keep_rest, keep_kv, given, same1, cross1, same2, cross2, qbuf, kbuf, vbuf):
    rows = keep_rest.shape[1]
    tokens = 2 * rows
    mine = pl.multiple_of(core * rows, rows)
    theirs = pl.multiple_of((1 - core) * rows, rows)
    qbuf[pl.ds(mine, rows), :] = keep_rest[0]
    qbuf[pl.ds(theirs, rows), :] = given[2]
    for slot, buf in ((0, kbuf), (1, vbuf)):
        buf[pl.ds(mine, rows), :] = same2[slot]
        buf[pl.ds(theirs, rows), :] = cross2[slot]
        buf[pl.ds(mine + tokens, rows), :] = same1[slot]
        buf[pl.ds(theirs + tokens, rows), :] = cross1[slot]
        buf[pl.ds(mine + 2 * tokens, rows), :] = keep_kv[slot]
        buf[pl.ds(theirs + 2 * tokens, rows), :] = given[slot]


def allowed_pairs(rows):
    span = (WIN + 1) * rows
    key_ids = lax.broadcasted_iota(jnp.int32, (span, rows), 0)
    row_ids = lax.broadcasted_iota(jnp.int32, (span, rows), 1)
    return (key_ids > row_ids) & (key_ids <= row_ids + WIN * rows)


def forward_body(
    keep_rest,
    keep_kv,
    given,
    same1,
    cross1,
    same2,
    cross2,
    delta,
    totals,
    params,
    stats,
    attended,
    tail_totals,
    slots,
    qbuf,
    kbuf,
    vbuf,
    tail_ref,
    part_ref,
):
    rows, width = keep_rest.shape[1:]
    poles = totals.shape[0]
    tokens = delta.shape[1]
    steps = tokens // SUBS
    chips = slots.shape[0]
    core, chip = place()
    scale = 1.0 / math.sqrt(HEAD)
    assemble(core, keep_rest, keep_kv, given, same1, cross1, same2, cross2, qbuf, kbuf, vbuf)
    span = (WIN + 1) * rows
    allowed = allowed_pairs(rows)
    for head in range(width // HEAD):
        at_head = slice(head * HEAD, (head + 1) * HEAD)
        for block in range(tokens // rows):
            at_rows = slice(block * rows, (block + 1) * rows)
            at_keys = slice(block * rows, block * rows + span)
            scores = (
                lax.dot_general(
                    kbuf[at_keys, at_head], qbuf[at_rows, at_head], OVER_HEAD, preferred_element_type=F32
                )
                * scale
            )
            scores = jnp.where(allowed, scores, -jnp.inf)
            top = jnp.max(scores, axis=0, keepdims=True)
            raised = jnp.exp(scores - top)
            share = 1.0 / jnp.sum(raised, axis=0, keepdims=True)
            probability = raised * share
            stats[head, block, 0:1, :] = top
            stats[head, block, 1:2, :] = share
            attended[head, at_rows, :] = (
                lax.dot_general(
                    probability.astype(BF16), vbuf[at_keys, at_head], OVER_KEYS, preferred_element_type=F32
                )
                .astype(BF16)
                .astype(F32)
            )

    def tail_group(first_pole, lane_group, first_lane):
        rate = params[pl.ds(first_pole, GROUP), pl.ds(first_lane, LANES)]
        pole_at = pl.ds(first_pole, GROUP)
        lane_at = pl.ds(first_lane, LANES)
        lam = rows3(jnp.exp(-rate))
        state = jnp.zeros((GROUP, SUBS, LANES), F32)
        matched = jnp.zeros((GROUP, SUBS, LANES), F32)
        for j in range(steps):
            at = pl.ds(j, SUBS, stride=steps)
            state = lam * state + attended[lane_group, at, :][None]
            matched = matched + delta[lane_group, at, :][None] * state
        tail_totals[pole_at, :, lane_at] = state
        lam_block = rows3(jnp.exp(-rate * steps))
        entering = entering_earlier(state, jnp.zeros((GROUP, LANES), F32), lam_block)
        full = state + lam_block * entering
        matched = matched + lam * totals[pole_at, :, lane_at] * entering
        tail_ref[pole_at, lane_at] = full[:, SUBS - 1, :]
        part_ref[pole_at, lane_at] = jnp.sum(matched, axis=1)

    each_group(poles, width, tail_group)
    tail = tail_ref[...].astype(BF16)
    part = part_ref[...].astype(BF16)
    for j in range(chips):
        slots[j, 0:poles, :] = tail
        slots[j, poles : 2 * poles, :] = part


def backward_body(
    keep_rest,
    keep_kv,
    given,
    same1,
    cross1,
    same2,
    cross2,
    stats,
    delta,
    totals,
    slots_in,
    params,
    dq_keep,
    dkv_keep,
    swap_out,
    out_same1,
    out_cross1,
    out_same2,
    out_cross2,
    incoming_all,
    qbuf,
    kbuf,
    vbuf,
    adj16,
    adj32,
    dk_acc,
    dv_acc,
    dqbuf,
):
    tokens, width = qbuf.shape
    rows = tokens // 2
    poles = totals.shape[0]
    steps = tokens // SUBS
    chips = slots_in.shape[0]
    core, chip = place()
    mine = pl.multiple_of(core * rows, rows)
    theirs = pl.multiple_of((1 - core) * rows, rows)
    scale = 1.0 / math.sqrt(HEAD)
    assemble(core, keep_rest, keep_kv, given, same1, cross1, same2, cross2, qbuf, kbuf, vbuf)

    around(
        lambda n: slots_in[n].astype(F32),
        params[0:poles, :],
        tokens,
        list(reversed(range(chips))),
        incoming_all,
    )
    for lane_group in range(width // LANES):
        gain = params[2 * poles : 2 * poles + 1, lane_group * LANES : (lane_group + 1) * LANES]
        adj32[lane_group] = gain * delta[lane_group]

    def adjoint_group(first_pole, lane_group, first_lane):
        rate = params[pl.ds(first_pole, GROUP), pl.ds(first_lane, LANES)]
        lam = rows3(jnp.exp(-rate))
        mixing = rows3(
            params[pl.ds(poles + first_pole, GROUP), pl.ds(first_lane, LANES)] * pole_weights(rate)
        )
        lane_at = pl.ds(first_lane, LANES)
        state = entering_later(
            totals[pl.ds(first_pole, GROUP), :, lane_at],
            incoming_all[chip, pl.ds(first_pole, GROUP), lane_at],
            rows3(jnp.exp(-rate * steps)),
        )
        for j in reversed(range(steps)):
            at = pl.ds(j, SUBS, stride=steps)
            state = lam * state + delta[lane_group, at, :][None]
            adj32[lane_group, at, :] = adj32[lane_group, at, :] + jnp.sum(mixing * state, axis=0)

    each_group(poles, width, adjoint_group)
    adj16[...] = adj32[...].astype(BF16)

    span = (WIN + 1) * rows
    allowed = allowed_pairs(rows)
    for head in range(width // HEAD):
        at_head = slice(head * HEAD, (head + 1) * HEAD)
        for block in range(tokens // rows):
            at_rows = slice(block * rows, (block + 1) * rows)
            at_keys = slice(block * rows, block * rows + span)
            query = qbuf[at_rows, at_head]
            key = kbuf[at_keys, at_head]
            value = vbuf[at_keys, at_head]
            adjoint = adj16[head, at_rows, :]
            scores = lax.dot_general(key, query, OVER_HEAD, preferred_element_type=F32) * scale
            scores = jnp.where(allowed, scores, -jnp.inf)
            probability = jnp.exp(scores - stats[head, block, 0:1, :]) * stats[head, block, 1:2, :]
            rounded = probability.astype(BF16)
            weight = lax.dot_general(value, adjoint, OVER_HEAD, preferred_element_type=F32)
            inner = jnp.sum(probability * weight, axis=0, keepdims=True)
            score_adjoint = (probability * (weight - inner) * scale).astype(BF16)
            dqbuf[at_rows, at_head] = lax.dot_general(
                score_adjoint, key, OVER_KEYS, preferred_element_type=F32
            ).astype(BF16)
            dk = jnp.dot(score_adjoint, query, preferred_element_type=F32)
            dv = jnp.dot(rounded, adjoint, preferred_element_type=F32)
            if block == 0:
                dk_acc[at_keys, at_head] = dk
                dv_acc[at_keys, at_head] = dv
            else:
                edge = span - rows
                first = slice(block * rows, block * rows + edge)
                last = slice(block * rows + edge, block * rows + span)
                dk_acc[first, at_head] = dk_acc[first, at_head] + dk[:edge]
                dv_acc[first, at_head] = dv_acc[first, at_head] + dv[:edge]
                dk_acc[last, at_head] = dk[edge:]
                dv_acc[last, at_head] = dv[edge:]

    for slot, acc in ((0, dk_acc), (1, dv_acc)):
        out_same2[slot] = acc[pl.ds(mine, rows), :].astype(BF16)
        out_cross2[slot] = acc[pl.ds(theirs, rows), :].astype(BF16)
        out_same1[slot] = acc[pl.ds(mine + tokens, rows), :].astype(BF16)
        out_cross1[slot] = acc[pl.ds(theirs + tokens, rows), :].astype(BF16)
        dkv_keep[slot] = acc[pl.ds(mine + 2 * tokens, rows), :]
        swap_out[slot] = acc[pl.ds(theirs + 2 * tokens, rows), :].astype(BF16)
    swap_out[2] = dqbuf[pl.ds(theirs, rows), :]
    dq_keep[...] = dqbuf[pl.ds(mine, rows), :]


def far_body(dkv_keep, same2, cross2, total):
    for slot in range(2):
        total[0, slot] = dkv_keep[slot] + same2[slot].astype(F32)
        total[1, slot] = cross2[slot].astype(F32)


def gate_body(
    keep_rest,
    given,
    attended,
    tail_totals,
    slots_in,
    incoming_all,
    params,
    far_total,
    gate_keep,
    gate_give,
    res_keep,
    mix32,
    arriving_ref,
):
    core, chip = place()
    rows, width = keep_rest.shape[1:]
    poles = tail_totals.shape[0]
    tokens = attended.shape[1]
    steps = tokens // SUBS
    chips = slots_in.shape[0]
    mine = pl.multiple_of(core * rows, rows)
    theirs = pl.multiple_of((1 - core) * rows, rows)
    rate = params[0:poles, :]
    around(
        lambda n: slots_in[n, 0:poles, :].astype(F32), rate, tokens, list(range(chips)), arriving_ref
    )
    parts = slots_in[0, poles : 2 * poles, :].astype(F32)
    crossed = slots_in[0, 0:poles, :].astype(F32) * incoming_all[0]
    for n in range(1, chips):
        parts = parts + slots_in[n, poles : 2 * poles, :].astype(F32)
        crossed = crossed + slots_in[n, 0:poles, :].astype(F32) * incoming_all[n]
    total = pole_weights(rate) * (parts + jnp.exp(-rate) * crossed)
    res_keep[...] = total
    high = total.astype(BF16)
    gate_give[rows : rows + poles, :] = high
    gate_give[rows + poles : rows + 2 * poles, :] = (total - high.astype(F32)).astype(BF16)
    for lane_group in range(width // LANES):
        gain = params[2 * poles : 2 * poles + 1, lane_group * LANES : (lane_group + 1) * LANES]
        mix32[lane_group] = gain * attended[lane_group]

    def group(first_pole, lane_group, first_lane):
        rate = params[pl.ds(first_pole, GROUP), pl.ds(first_lane, LANES)]
        lam = rows3(jnp.exp(-rate))
        mixing = rows3(
            params[pl.ds(poles + first_pole, GROUP), pl.ds(first_lane, LANES)] * pole_weights(rate)
        )
        lane_at = pl.ds(first_lane, LANES)
        pole_at = pl.ds(first_pole, GROUP)
        state = entering_earlier(
            tail_totals[pole_at, :, lane_at],
            arriving_ref[chip, pole_at, lane_at],
            rows3(jnp.exp(-rate * steps)),
        )
        for j in range(steps):
            at = pl.ds(j, SUBS, stride=steps)
            state = lam * state + attended[lane_group, at, :][None]
            mix32[lane_group, at, :] = mix32[lane_group, at, :] + jnp.sum(mixing * state, axis=0)

    each_group(poles, width, group)
    for lane_group in range(width // LANES):
        lanes = slice(lane_group * LANES, (lane_group + 1) * LANES)
        gate_keep[:, lanes] = (
            keep_rest[2, :, lanes].astype(F32) * mix32[lane_group, pl.ds(mine, rows), :]
        ).astype(BF16)
        gate_give[0:rows, lanes] = (
            given[4, :, lanes].astype(F32) * mix32[lane_group, pl.ds(theirs, rows), :]
        ).astype(BF16)


def final_body(
    dq_keep, far_total, swap_in, same1, cross1, gate_keep, gate_in, res_keep, dq, dk, dv, dgate, dres
):
    rows, width = dq_keep.shape
    poles = res_keep.shape[0]
    own, other = halves(place()[0], width)
    for slot, out in ((0, dk), (1, dv)):
        out[:, pl.ds(own, width)] = (
            far_total[0, slot] + same1[slot].astype(F32)
        ).astype(BF16)
        out[:, pl.ds(other, width)] = (
            far_total[1, slot] + swap_in[slot].astype(F32) + cross1[slot].astype(F32)
        ).astype(BF16)
    dq[:, pl.ds(own, width)] = dq_keep[...]
    dq[:, pl.ds(other, width)] = swap_in[2]
    dgate[:, pl.ds(own, width)] = gate_keep[...]
    dgate[:, pl.ds(other, width)] = gate_in[0:rows, :]
    dres[:, pl.ds(own, width)] = res_keep[...]
    dres[:, pl.ds(other, width)] = gate_in[rows : rows + poles, :].astype(F32) + gate_in[
        rows + poles : rows + 2 * poles, :
    ].astype(F32)


def chip_shift(array, by, crossed):
    members = lax.axis_size("ctx")
    pairs = []
    for source in range(members):
        chip, core = source // 2, source % 2
        target = ((chip + by) % (members // 2)) * 2 + ((1 - core) if crossed else core)
        pairs.append((source, target))
    return lax.ppermute(array, "ctx", pairs)


def chip_exchange(slots):
    members = lax.axis_size("ctx")
    groups = [list(range(core, members, 2)) for core in range(2)]
    return lax.all_to_all(slots, "ctx", 0, 0, axis_index_groups=groups)


def local(queries, key_rows, value_rows, gate_values, cotangent, decay_rates, residues, skip_gain):
    rows, channels = queries.shape
    width = channels // 2
    poles = decay_rates.shape[0]
    chips = lax.axis_size("ctx") // 2
    tokens = 2 * rows
    skip = skip_gain.reshape(1, channels)
    groups = width // LANES
    pair = (2, rows, width)
    split = (groups, tokens, LANES)
    states = (poles, SUBS, width)
    span = (WIN + 2) * rows
    keep_kv, give_kv, keep_rest, give_all, params = call(
        pack_body,
        [
            (pair, BF16, True),
            (pair, BF16, True),
            ((3, rows, width), BF16, True),
            ((5, rows, width), BF16, True),
            ((2 * poles + 1, width), F32, True),
        ],
        scratch=[
            pltpu.VMEM((5, rows, channels), BF16),
            pltpu.VMEM((2 * poles + SUBS, channels), F32),
            pltpu.SemaphoreType.DMA((8,)),
        ],
        far=tuple(range(8)),
        name="pack",
    )(key_rows, value_rows, queries, gate_values, cotangent, decay_rates, residues, skip)
    same2 = chip_shift(keep_kv, 2, False)
    cross2 = chip_shift(give_kv, 2, True)
    same1 = chip_shift(keep_kv, 1, False)
    cross1 = chip_shift(give_kv, 1, True)
    given = chip_shift(give_all, 0, True)
    delta, totals, head_slots = call(
        head_body,
        [(split, F32, True), (states, F32, True), ((chips, poles, width), BF16, True)],
        scratch=[pltpu.VMEM((poles, width), F32)],
        near=(0, 1, 2),
        name="head_states",
    )(keep_rest, given, params)
    head_in = chip_exchange(head_slots)
    halo = (keep_rest, keep_kv, given, same1, cross1, same2, cross2)
    halo_buffers = [
        pltpu.VMEM((tokens, width), BF16),
        pltpu.VMEM((span, width), BF16),
        pltpu.VMEM((span, width), BF16),
    ]
    stats, attended, tail_totals, tail_slots = call(
        forward_body,
        [
            ((groups, 2, SUBS, rows), F32, True),
            (split, F32, True),
            (states, F32, True),
            ((chips, 2 * poles, width), BF16, True),
        ],
        scratch=halo_buffers + [pltpu.VMEM((poles, width), F32), pltpu.VMEM((poles, width), F32)],
        near=tuple(range(10)),
        cost=EARLY,
        name="forward",
    )(*halo, delta, totals, params)
    tail_in = chip_exchange(tail_slots)
    outs = call(
        backward_body,
        [
            ((rows, width), BF16, True),
            (pair, F32, True),
            ((3, rows, width), BF16, True),
            (pair, BF16, True),
            (pair, BF16, True),
            (pair, BF16, True),
            (pair, BF16, True),
            ((chips, poles, width), F32, True),
        ],
        scratch=halo_buffers
        + [
            pltpu.VMEM(split, BF16),
            pltpu.VMEM(split, F32),
            pltpu.VMEM((span, width), F32),
            pltpu.VMEM((span, width), F32),
            pltpu.VMEM((tokens, width), BF16),
        ],
        near=tuple(range(12)),
        name="backward",
    )(*halo, stats, delta, totals, head_in, params)
    dq_keep, dkv_keep, swap_out, out_same1, out_cross1, out_same2, out_cross2, incoming_all = outs
    back_same2 = chip_shift(out_same2, -2, False)
    back_cross2 = chip_shift(out_cross2, -2, True)
    back_same1 = chip_shift(out_same1, -1, False)
    back_cross1 = chip_shift(out_cross1, -1, True)
    swap_in = chip_shift(swap_out, 0, True)
    (far_total,) = call(
        far_body, [((2,) + pair, F32, True)], near=(0, 1, 2), cost=EARLY, name="far_sum"
    )(dkv_keep, back_same2, back_cross2)
    gate_keep, gate_give, res_keep = call(
        gate_body,
        [
            ((rows, width), BF16, True),
            ((rows + 2 * poles, width), BF16, True),
            ((poles, width), F32, True),
        ],
        scratch=[pltpu.VMEM(split, F32), pltpu.VMEM((chips, poles, width), F32)],
        near=tuple(range(8)),
        name="gate",
    )(keep_rest, given, attended, tail_totals, tail_in, incoming_all, params, far_total)
    gate_in = chip_shift(gate_give, 0, True)
    full = (rows, channels)
    wide = (full, BF16, False)
    return tuple(
        call(
            final_body,
            [wide, wide, wide, wide, ((poles, channels), F32, False)],
            near=tuple(range(8)),
            name="final",
        )(dq_keep, far_total, swap_in, back_same1, back_cross1, gate_keep, gate_in, res_keep)
    )


def solution(mesh):
    wide = P(("dp", "ctx"), "head")
    in_specs = (wide, wide, wide, wide, wide, P(None, "head"), P(None, "head"), P("head"))
    out_specs = (wide, wide, wide, wide, P("dp", "head"))
    return jax.shard_map(local, mesh=mesh, in_specs=in_specs, out_specs=out_specs, check_vma=False)
```

```python
import math

import jax
import jax.numpy as jnp
from jax import lax
from jax.experimental import pallas as pl
from jax.experimental.pallas import tpu as pltpu
from jax.sharding import PartitionSpec as P

HEAD = 128
WIN = 4
LANES = 128
SUBS = 8
GROUP = 8
EARLY = pl.CostEstimate(flops=10**11, transcendentals=0, bytes_accessed=10**8)
F32 = jnp.float32
BF16 = jnp.bfloat16
OVER_KEYS = (((0,), (0,)), ((), ()))
OVER_HEAD = (((1,), (1,)), ((), ()))


def call(body, outs, scratch=(), near=(), far=(), cost=None, name=None):
    def run(*args):
        args = list(args)
        specs = []
        for n in range(len(args)):
            space = pltpu.HBM if n in far else pltpu.VMEM
            specs.append(pl.BlockSpec(memory_space=space))
            if n in near or n in far:
                args[n] = pltpu.with_memory_space_constraint(args[n], space)
        return pl.pallas_call(
            body,
            out_shape=[
                pltpu.VMEM(s, d) if local_out else jax.ShapeDtypeStruct(s, d) for s, d, local_out in outs
            ],
            in_specs=specs,
            out_specs=[pl.BlockSpec(memory_space=pltpu.VMEM)] * len(outs),
            scratch_shapes=list(scratch),
            compiler_params=pltpu.CompilerParams(vmem_limit_bytes=8 * 1024 * 1024),
            cost_estimate=cost,
            name=name,
        )(*args)

    return run


def place():
    index = lax.axis_index("ctx")
    return lax.rem(index, 2), lax.div(index, 2)


def halves(core, width):
    own = pl.multiple_of(core * width, LANES)
    other = pl.multiple_of((1 - core) * width, LANES)
    return own, other


def pack_body(
    k, v, q, gate, cot, rates, residues, skip, keep_kv, give_kv, keep_rest, give_all, params, buf, small, sems
):
    width = k.shape[1] // 2
    poles = rates.shape[0]
    own, other = halves(place()[0], width)
    arrays = (k, v, q, gate, cot)
    copies = [pltpu.make_async_copy(a, buf.at[n], sems.at[n]) for n, a in enumerate(arrays)]
    for n, (array, first, count) in enumerate(
        ((rates, 0, poles), (residues, poles, poles), (skip, 2 * poles, 1))
    ):
        copies.append(
            pltpu.make_async_copy(array, small.at[pl.ds(first, count)], sems.at[len(arrays) + n])
        )
    for copy in copies:
        copy.start()
    for n in range(len(arrays)):
        copies[n].wait()
        give = buf[n, :, pl.ds(other, width)]
        keep = buf[n, :, pl.ds(own, width)]
        give_all[n] = give
        if n < 2:
            give_kv[n] = give
            keep_kv[n] = keep
        else:
            keep_rest[n - 2] = keep
    for copy in copies[len(arrays) :]:
        copy.wait()
    params[...] = small[0 : 2 * poles + 1, pl.ds(own, width)]


def rows3(values):
    return jnp.broadcast_to(values[:, None, :], (values.shape[0], SUBS, values.shape[1]))


def each_group(poles, width, body):
    pole_groups = poles // GROUP
    lane_groups = width // LANES

    def step(index, carry):
        lane_group = index // pole_groups
        first_lane = pl.multiple_of(lane_group * LANES, LANES)
        first_pole = pl.multiple_of((index % pole_groups) * GROUP, GROUP)
        body(first_pole, lane_group, first_lane)
        return carry

    lax.fori_loop(0, pole_groups * lane_groups, step, 0)


def head_body(keep_rest, given, params, delta, totals, slots, head_ref):
    rows, width = keep_rest.shape[1:]
    poles = totals.shape[0]
    chips = slots.shape[0]
    core, chip = place()
    own, other = halves(core, width)
    tokens = delta.shape[1]
    steps = tokens // SUBS
    mine = pl.multiple_of(core * rows, rows)
    theirs = pl.multiple_of((1 - core) * rows, rows)
    for lane_group in range(width // LANES):
        lanes = slice(lane_group * LANES, (lane_group + 1) * LANES)
        delta[lane_group, pl.ds(mine, rows), :] = keep_rest[1, :, lanes].astype(F32) * keep_rest[
            2, :, lanes
        ].astype(F32)
        delta[lane_group, pl.ds(theirs, rows), :] = given[3, :, lanes].astype(F32) * given[
            4, :, lanes
        ].astype(F32)

    def group(first_pole, lane_group, first_lane):
        rate = params[pl.ds(first_pole, GROUP), pl.ds(first_lane, LANES)]
        lam = rows3(jnp.exp(-rate))
        state = jnp.zeros((GROUP, SUBS, LANES), F32)
        for j in reversed(range(steps)):
            state = lam * state + delta[lane_group, pl.ds(j, SUBS, stride=steps), :][None]
        totals[pl.ds(first_pole, GROUP), :, pl.ds(first_lane, LANES)] = state
        block = lax.broadcasted_iota(jnp.int32, (GROUP, SUBS, LANES), 1).astype(F32)
        power = jnp.exp(-rows3(rate) * (block * steps))
        head_ref[pl.ds(first_pole, GROUP), pl.ds(first_lane, LANES)] = jnp.sum(power * state, axis=1)

    each_group(poles, width, group)
    head = head_ref[...].astype(BF16)
    for j in range(chips):
        slots[j] = head


def around(own, rate, tokens, order, out):
    decay = jnp.exp(-rate * tokens)
    value = own(order[-1])
    power = decay
    for n in reversed(order[:-1]):
        value = value + power * own(n)
        power = power * decay
    value = value / (1.0 - jnp.exp(-rate * (tokens * len(order))))
    for n in order:
        out[n] = value
        value = own(n) + decay * value


def block_ids(shape):
    return lax.broadcasted_iota(jnp.int32, shape, 1)


def entering_later(totals, incoming, lam_block):
    ids = block_ids(totals.shape)
    value = jnp.where(ids == SUBS - 1, rows3(incoming), pltpu.roll(totals, SUBS - 1, 1))
    power = lam_block
    for shift in (1, 2, 4):
        moved = pltpu.roll(value, SUBS - shift, 1)
        value = value + jnp.where(ids < SUBS - shift, power * moved, 0.0)
        power = power * power
    return value


def entering_earlier(totals, arriving, lam_block):
    ids = block_ids(totals.shape)
    value = jnp.where(ids == 0, rows3(arriving), pltpu.roll(totals, 1, 1))
    power = lam_block
    for shift in (1, 2, 4):
        moved = pltpu.roll(value, shift, 1)
        value = value + jnp.where(ids >= shift, power * moved, 0.0)
        power = power * power
    return value


def pole_weights(rate):
    tangent = jnp.tanh(rate)
    return jnp.sqrt(2.0 * tangent / (1.0 + tangent))


def merge_body(keep_kv, given, chip_kv):
    rows = keep_kv.shape[1]
    core, chip = place()
    for slot in range(2):
        chip_kv[slot, pl.ds(pl.multiple_of(core * rows, rows), rows), :] = keep_kv[slot]
        chip_kv[slot, pl.ds(pl.multiple_of((1 - core) * rows, rows), rows), :] = given[slot]


def assemble(core, keep_rest, chip_kv, given, same1, cross1, far_kv, qbuf, kbuf, vbuf):
    rows = keep_rest.shape[1]
    tokens = 2 * rows
    mine = pl.multiple_of(core * rows, rows)
    theirs = pl.multiple_of((1 - core) * rows, rows)
    qbuf[pl.ds(mine, rows), :] = keep_rest[0]
    qbuf[pl.ds(theirs, rows), :] = given[2]
    for slot, buf in ((0, kbuf), (1, vbuf)):
        buf[0:tokens, :] = far_kv[slot]
        buf[pl.ds(mine + tokens, rows), :] = same1[slot]
        buf[pl.ds(theirs + tokens, rows), :] = cross1[slot]
        buf[2 * tokens : 3 * tokens, :] = chip_kv[slot]


def allowed_pairs(rows):
    span = (WIN + 1) * rows
    key_ids = lax.broadcasted_iota(jnp.int32, (span, rows), 0)
    row_ids = lax.broadcasted_iota(jnp.int32, (span, rows), 1)
    return (key_ids > row_ids) & (key_ids <= row_ids + WIN * rows)


def forward_body(
    keep_rest,
    chip_kv,
    given,
    same1,
    cross1,
    far_kv,
    delta,
    totals,
    params,
    stats,
    attended,
    tail_totals,
    slots,
    qbuf,
    kbuf,
    vbuf,
    tail_ref,
    part_ref,
):
    rows, width = keep_rest.shape[1:]
    poles = totals.shape[0]
    tokens = delta.shape[1]
    steps = tokens // SUBS
    chips = slots.shape[0]
    core, chip = place()
    scale = 1.0 / math.sqrt(HEAD)
    assemble(core, keep_rest, chip_kv, given, same1, cross1, far_kv, qbuf, kbuf, vbuf)
    span = (WIN + 1) * rows
    allowed = allowed_pairs(rows)
    for head in range(width // HEAD):
        at_head = slice(head * HEAD, (head + 1) * HEAD)
        for block in range(tokens // rows):
            at_rows = slice(block * rows, (block + 1) * rows)
            at_keys = slice(block * rows, block * rows + span)
            scores = (
                lax.dot_general(
                    kbuf[at_keys, at_head], qbuf[at_rows, at_head], OVER_HEAD, preferred_element_type=F32
                )
                * scale
            )
            scores = jnp.where(allowed, scores, -jnp.inf)
            top = jnp.max(scores, axis=0, keepdims=True)
            raised = jnp.exp(scores - top)
            share = 1.0 / jnp.sum(raised, axis=0, keepdims=True)
            probability = raised * share
            stats[head, block, 0:1, :] = top
            stats[head, block, 1:2, :] = share
            attended[head, at_rows, :] = (
                lax.dot_general(
                    probability.astype(BF16), vbuf[at_keys, at_head], OVER_KEYS, preferred_element_type=F32
                )
                .astype(BF16)
                .astype(F32)
            )

    def tail_group(first_pole, lane_group, first_lane):
        rate = params[pl.ds(first_pole, GROUP), pl.ds(first_lane, LANES)]
        pole_at = pl.ds(first_pole, GROUP)
        lane_at = pl.ds(first_lane, LANES)
        lam = rows3(jnp.exp(-rate))
        state = jnp.zeros((GROUP, SUBS, LANES), F32)
        matched = jnp.zeros((GROUP, SUBS, LANES), F32)
        for j in range(steps):
            at = pl.ds(j, SUBS, stride=steps)
            state = lam * state + attended[lane_group, at, :][None]
            matched = matched + delta[lane_group, at, :][None] * state
        tail_totals[pole_at, :, lane_at] = state
        lam_block = rows3(jnp.exp(-rate * steps))
        entering = entering_earlier(state, jnp.zeros((GROUP, LANES), F32), lam_block)
        full = state + lam_block * entering
        matched = matched + lam * totals[pole_at, :, lane_at] * entering
        tail_ref[pole_at, lane_at] = full[:, SUBS - 1, :]
        part_ref[pole_at, lane_at] = jnp.sum(matched, axis=1)

    each_group(poles, width, tail_group)
    tail = tail_ref[...].astype(BF16)
    part = part_ref[...].astype(BF16)
    for j in range(chips):
        slots[j, 0:poles, :] = tail
        slots[j, poles : 2 * poles, :] = part


def backward_body(
    keep_rest,
    chip_kv,
    given,
    same1,
    cross1,
    far_kv,
    stats,
    delta,
    totals,
    slots_in,
    params,
    dq_keep,
    dkv_keep,
    swap_out,
    out_same1,
    out_cross1,
    out_same2,
    out_cross2,
    incoming_all,
    qbuf,
    kbuf,
    vbuf,
    adj16,
    adj32,
    dk_acc,
    dv_acc,
    dqbuf,
):
    tokens, width = qbuf.shape
    rows = tokens // 2
    poles = totals.shape[0]
    steps = tokens // SUBS
    chips = slots_in.shape[0]
    core, chip = place()
    mine = pl.multiple_of(core * rows, rows)
    theirs = pl.multiple_of((1 - core) * rows, rows)
    scale = 1.0 / math.sqrt(HEAD)
    assemble(core, keep_rest, chip_kv, given, same1, cross1, far_kv, qbuf, kbuf, vbuf)

    around(
        lambda n: slots_in[n].astype(F32),
        params[0:poles, :],
        tokens,
        list(reversed(range(chips))),
        incoming_all,
    )
    for lane_group in range(width // LANES):
        gain = params[2 * poles : 2 * poles + 1, lane_group * LANES : (lane_group + 1) * LANES]
        adj32[lane_group] = gain * delta[lane_group]

    def adjoint_group(first_pole, lane_group, first_lane):
        rate = params[pl.ds(first_pole, GROUP), pl.ds(first_lane, LANES)]
        lam = rows3(jnp.exp(-rate))
        mixing = rows3(
            params[pl.ds(poles + first_pole, GROUP), pl.ds(first_lane, LANES)] * pole_weights(rate)
        )
        lane_at = pl.ds(first_lane, LANES)
        state = entering_later(
            totals[pl.ds(first_pole, GROUP), :, lane_at],
            incoming_all[chip, pl.ds(first_pole, GROUP), lane_at],
            rows3(jnp.exp(-rate * steps)),
        )
        for j in reversed(range(steps)):
            at = pl.ds(j, SUBS, stride=steps)
            state = lam * state + delta[lane_group, at, :][None]
            adj32[lane_group, at, :] = adj32[lane_group, at, :] + jnp.sum(mixing * state, axis=0)

    each_group(poles, width, adjoint_group)
    adj16[...] = adj32[...].astype(BF16)

    span = (WIN + 1) * rows
    allowed = allowed_pairs(rows)
    for head in range(width // HEAD):
        at_head = slice(head * HEAD, (head + 1) * HEAD)
        for block in range(tokens // rows):
            at_rows = slice(block * rows, (block + 1) * rows)
            at_keys = slice(block * rows, block * rows + span)
            query = qbuf[at_rows, at_head]
            key = kbuf[at_keys, at_head]
            value = vbuf[at_keys, at_head]
            adjoint = adj16[head, at_rows, :]
            scores = lax.dot_general(key, query, OVER_HEAD, preferred_element_type=F32) * scale
            scores = jnp.where(allowed, scores, -jnp.inf)
            probability = jnp.exp(scores - stats[head, block, 0:1, :]) * stats[head, block, 1:2, :]
            rounded = probability.astype(BF16)
            weight = lax.dot_general(value, adjoint, OVER_HEAD, preferred_element_type=F32)
            inner = jnp.sum(probability * weight, axis=0, keepdims=True)
            score_adjoint = (probability * (weight - inner) * scale).astype(BF16)
            dqbuf[at_rows, at_head] = lax.dot_general(
                score_adjoint, key, OVER_KEYS, preferred_element_type=F32
            ).astype(BF16)
            dk = jnp.dot(score_adjoint, query, preferred_element_type=F32)
            dv = jnp.dot(rounded, adjoint, preferred_element_type=F32)
            if block == 0:
                dk_acc[at_keys, at_head] = dk
                dv_acc[at_keys, at_head] = dv
            else:
                edge = span - rows
                first = slice(block * rows, block * rows + edge)
                last = slice(block * rows + edge, block * rows + span)
                dk_acc[first, at_head] = dk_acc[first, at_head] + dk[:edge]
                dv_acc[first, at_head] = dv_acc[first, at_head] + dv[:edge]
                dk_acc[last, at_head] = dk[edge:]
                dv_acc[last, at_head] = dv[edge:]

    for slot, acc in ((0, dk_acc), (1, dv_acc)):
        out_same2[slot] = acc[pl.ds(mine, rows), :].astype(BF16)
        out_cross2[slot] = acc[pl.ds(theirs, rows), :].astype(BF16)
        out_same1[slot] = acc[pl.ds(mine + tokens, rows), :].astype(BF16)
        out_cross1[slot] = acc[pl.ds(theirs + tokens, rows), :].astype(BF16)
        dkv_keep[slot] = acc[pl.ds(mine + 2 * tokens, rows), :]
        swap_out[slot] = acc[pl.ds(theirs + 2 * tokens, rows), :].astype(BF16)
    swap_out[2] = dqbuf[pl.ds(theirs, rows), :]
    dq_keep[...] = dqbuf[pl.ds(mine, rows), :]


def far_body(dkv_keep, same2, cross2, total):
    total[...] = dkv_keep[...] + same2[...].astype(F32)


def gate_body(
    keep_rest,
    given,
    attended,
    tail_totals,
    slots_in,
    incoming_all,
    params,
    far_total,
    gate_keep,
    gate_give,
    res_keep,
    mix32,
    arriving_ref,
):
    core, chip = place()
    rows, width = keep_rest.shape[1:]
    poles = tail_totals.shape[0]
    tokens = attended.shape[1]
    steps = tokens // SUBS
    chips = slots_in.shape[0]
    mine = pl.multiple_of(core * rows, rows)
    theirs = pl.multiple_of((1 - core) * rows, rows)
    rate = params[0:poles, :]
    around(
        lambda n: slots_in[n, 0:poles, :].astype(F32), rate, tokens, list(range(chips)), arriving_ref
    )
    parts = slots_in[0, poles : 2 * poles, :].astype(F32)
    crossed = slots_in[0, 0:poles, :].astype(F32) * incoming_all[0]
    for n in range(1, chips):
        parts = parts + slots_in[n, poles : 2 * poles, :].astype(F32)
        crossed = crossed + slots_in[n, 0:poles, :].astype(F32) * incoming_all[n]
    total = pole_weights(rate) * (parts + jnp.exp(-rate) * crossed)
    res_keep[...] = total
    high = total.astype(BF16)
    gate_give[rows : rows + poles, :] = high
    gate_give[rows + poles : rows + 2 * poles, :] = (total - high.astype(F32)).astype(BF16)
    for lane_group in range(width // LANES):
        gain = params[2 * poles : 2 * poles + 1, lane_group * LANES : (lane_group + 1) * LANES]
        mix32[lane_group] = gain * attended[lane_group]

    def group(first_pole, lane_group, first_lane):
        rate = params[pl.ds(first_pole, GROUP), pl.ds(first_lane, LANES)]
        lam = rows3(jnp.exp(-rate))
        mixing = rows3(
            params[pl.ds(poles + first_pole, GROUP), pl.ds(first_lane, LANES)] * pole_weights(rate)
        )
        lane_at = pl.ds(first_lane, LANES)
        pole_at = pl.ds(first_pole, GROUP)
        state = entering_earlier(
            tail_totals[pole_at, :, lane_at],
            arriving_ref[chip, pole_at, lane_at],
            rows3(jnp.exp(-rate * steps)),
        )
        for j in range(steps):
            at = pl.ds(j, SUBS, stride=steps)
            state = lam * state + attended[lane_group, at, :][None]
            mix32[lane_group, at, :] = mix32[lane_group, at, :] + jnp.sum(mixing * state, axis=0)

    each_group(poles, width, group)
    for lane_group in range(width // LANES):
        lanes = slice(lane_group * LANES, (lane_group + 1) * LANES)
        gate_keep[:, lanes] = (
            keep_rest[2, :, lanes].astype(F32) * mix32[lane_group, pl.ds(mine, rows), :]
        ).astype(BF16)
        gate_give[0:rows, lanes] = (
            given[4, :, lanes].astype(F32) * mix32[lane_group, pl.ds(theirs, rows), :]
        ).astype(BF16)


def final_body(
    dq_keep, far_total, swap_in, same1, cross1, cross2, gate_keep, gate_in, res_keep, dq, dk, dv, dgate, dres
):
    rows, width = dq_keep.shape
    poles = res_keep.shape[0]
    own, other = halves(place()[0], width)
    for slot, out in ((0, dk), (1, dv)):
        out[:, pl.ds(own, width)] = (
            far_total[slot] + same1[slot].astype(F32)
        ).astype(BF16)
        out[:, pl.ds(other, width)] = (
            swap_in[slot].astype(F32) + cross1[slot].astype(F32) + cross2[slot].astype(F32)
        ).astype(BF16)
    dq[:, pl.ds(own, width)] = dq_keep[...]
    dq[:, pl.ds(other, width)] = swap_in[2]
    dgate[:, pl.ds(own, width)] = gate_keep[...]
    dgate[:, pl.ds(other, width)] = gate_in[0:rows, :]
    dres[:, pl.ds(own, width)] = res_keep[...]
    dres[:, pl.ds(other, width)] = gate_in[rows : rows + poles, :].astype(F32) + gate_in[
        rows + poles : rows + 2 * poles, :
    ].astype(F32)


def chip_shift(array, by, crossed):
    members = lax.axis_size("ctx")
    pairs = []
    for source in range(members):
        chip, core = source // 2, source % 2
        target = ((chip + by) % (members // 2)) * 2 + ((1 - core) if crossed else core)
        pairs.append((source, target))
    return lax.ppermute(array, "ctx", pairs)


def chip_exchange(slots):
    members = lax.axis_size("ctx")
    groups = [list(range(core, members, 2)) for core in range(2)]
    return lax.all_to_all(slots, "ctx", 0, 0, axis_index_groups=groups)


def local(queries, key_rows, value_rows, gate_values, cotangent, decay_rates, residues, skip_gain):
    rows, channels = queries.shape
    width = channels // 2
    poles = decay_rates.shape[0]
    chips = lax.axis_size("ctx") // 2
    tokens = 2 * rows
    skip = skip_gain.reshape(1, channels)
    groups = width // LANES
    pair = (2, rows, width)
    split = (groups, tokens, LANES)
    states = (poles, SUBS, width)
    span = (WIN + 2) * rows
    keep_kv, give_kv, keep_rest, give_all, params = call(
        pack_body,
        [
            (pair, BF16, True),
            (pair, BF16, True),
            ((3, rows, width), BF16, True),
            ((5, rows, width), BF16, True),
            ((2 * poles + 1, width), F32, True),
        ],
        scratch=[
            pltpu.VMEM((5, rows, channels), BF16),
            pltpu.VMEM((2 * poles + SUBS, channels), F32),
            pltpu.SemaphoreType.DMA((8,)),
        ],
        far=tuple(range(8)),
        name="pack",
    )(key_rows, value_rows, queries, gate_values, cotangent, decay_rates, residues, skip)
    given = chip_shift(give_all, 0, True)
    (chip_kv,) = call(merge_body, [((2, tokens, width), BF16, True)], near=(0, 1), name="chip_kv")(
        keep_kv, given
    )
    far_kv = chip_shift(chip_kv, 2, False)
    same1 = chip_shift(keep_kv, 1, False)
    cross1 = chip_shift(give_kv, 1, True)
    delta, totals, head_slots = call(
        head_body,
        [(split, F32, True), (states, F32, True), ((chips, poles, width), BF16, True)],
        scratch=[pltpu.VMEM((poles, width), F32)],
        near=(0, 1, 2),
        name="head_states",
    )(keep_rest, given, params)
    head_in = chip_exchange(head_slots)
    halo = (keep_rest, chip_kv, given, same1, cross1, far_kv)
    halo_buffers = [
        pltpu.VMEM((tokens, width), BF16),
        pltpu.VMEM((span, width), BF16),
        pltpu.VMEM((span, width), BF16),
    ]
    stats, attended, tail_totals, tail_slots = call(
        forward_body,
        [
            ((groups, 2, SUBS, rows), F32, True),
            (split, F32, True),
            (states, F32, True),
            ((chips, 2 * poles, width), BF16, True),
        ],
        scratch=halo_buffers + [pltpu.VMEM((poles, width), F32), pltpu.VMEM((poles, width), F32)],
        near=tuple(range(9)),
        cost=EARLY,
        name="forward",
    )(*halo, delta, totals, params)
    tail_in = chip_exchange(tail_slots)
    outs = call(
        backward_body,
        [
            ((rows, width), BF16, True),
            (pair, F32, True),
            ((3, rows, width), BF16, True),
            (pair, BF16, True),
            (pair, BF16, True),
            (pair, BF16, True),
            (pair, BF16, True),
            ((chips, poles, width), F32, True),
        ],
        scratch=halo_buffers
        + [
            pltpu.VMEM(split, BF16),
            pltpu.VMEM(split, F32),
            pltpu.VMEM((span, width), F32),
            pltpu.VMEM((span, width), F32),
            pltpu.VMEM((tokens, width), BF16),
        ],
        near=tuple(range(11)),
        name="backward",
    )(*halo, stats, delta, totals, head_in, params)
    dq_keep, dkv_keep, swap_out, out_same1, out_cross1, out_same2, out_cross2, incoming_all = outs
    back_same2 = chip_shift(out_same2, -2, False)
    back_cross2 = chip_shift(out_cross2, -2, True)
    back_same1 = chip_shift(out_same1, -1, False)
    back_cross1 = chip_shift(out_cross1, -1, True)
    swap_in = chip_shift(swap_out, 0, True)
    (far_total,) = call(
        far_body, [(pair, F32, True)], near=(0, 1, 2), cost=EARLY, name="far_sum"
    )(dkv_keep, back_same2, back_cross2)
    gate_keep, gate_give, res_keep = call(
        gate_body,
        [
            ((rows, width), BF16, True),
            ((rows + 2 * poles, width), BF16, True),
            ((poles, width), F32, True),
        ],
        scratch=[pltpu.VMEM(split, F32), pltpu.VMEM((chips, poles, width), F32)],
        near=tuple(range(8)),
        name="gate",
    )(keep_rest, given, attended, tail_totals, tail_in, incoming_all, params, far_total)
    gate_in = chip_shift(gate_give, 0, True)
    full = (rows, channels)
    wide = (full, BF16, False)
    return tuple(
        call(
            final_body,
            [wide, wide, wide, wide, ((poles, channels), F32, False)],
            near=tuple(range(9)),
            name="final",
        )(
            dq_keep,
            far_total,
            swap_in,
            back_same1,
            back_cross1,
            back_cross2,
            gate_keep,
            gate_in,
            res_keep,
        )
    )


def solution(mesh):
    wide = P(("dp", "ctx"), "head")
    in_specs = (wide, wide, wide, wide, wide, P(None, "head"), P(None, "head"), P("head"))
    out_specs = (wide, wide, wide, wide, P("dp", "head"))
    return jax.shard_map(local, mesh=mesh, in_specs=in_specs, out_specs=out_specs, check_vma=False)
```

```python
import math

import jax
import jax.numpy as jnp
from jax import lax
from jax.experimental import pallas as pl
from jax.experimental.pallas import tpu as pltpu
from jax.sharding import PartitionSpec as P

HEAD = 128
WIN = 4
LANES = 128
SUBS = 8
GROUP = 8
EARLY = pl.CostEstimate(flops=10**11, transcendentals=0, bytes_accessed=10**8)
F32 = jnp.float32
BF16 = jnp.bfloat16
OVER_KEYS = (((0,), (0,)), ((), ()))
OVER_HEAD = (((1,), (1,)), ((), ()))


def call(body, outs, scratch=(), near=(), far=(), cost=None, name=None):
    def run(*args):
        args = list(args)
        specs = []
        for n in range(len(args)):
            space = pltpu.HBM if n in far else pltpu.VMEM
            specs.append(pl.BlockSpec(memory_space=space))
            if n in near or n in far:
                args[n] = pltpu.with_memory_space_constraint(args[n], space)
        return pl.pallas_call(
            body,
            out_shape=[
                pltpu.VMEM(s, d) if local_out else jax.ShapeDtypeStruct(s, d) for s, d, local_out in outs
            ],
            in_specs=specs,
            out_specs=[pl.BlockSpec(memory_space=pltpu.VMEM)] * len(outs),
            scratch_shapes=list(scratch),
            compiler_params=pltpu.CompilerParams(vmem_limit_bytes=8 * 1024 * 1024),
            cost_estimate=cost,
            name=name,
        )(*args)

    return run


def place():
    index = lax.axis_index("ctx")
    return lax.rem(index, 2), lax.div(index, 2)


def halves(core, width):
    own = pl.multiple_of(core * width, LANES)
    other = pl.multiple_of((1 - core) * width, LANES)
    return own, other


def pack_body(
    k, v, q, gate, cot, rates, residues, skip, keep_kv, give_kv, keep_rest, give_all, params, buf, small, sems
):
    width = k.shape[1] // 2
    poles = rates.shape[0]
    own, other = halves(place()[0], width)
    arrays = (k, v, q, gate, cot)
    copies = [pltpu.make_async_copy(a, buf.at[n], sems.at[n]) for n, a in enumerate(arrays)]
    for n, (array, first, count) in enumerate(
        ((rates, 0, poles), (residues, poles, poles), (skip, 2 * poles, 1))
    ):
        copies.append(
            pltpu.make_async_copy(array, small.at[pl.ds(first, count)], sems.at[len(arrays) + n])
        )
    for copy in copies:
        copy.start()
    for n in range(len(arrays)):
        copies[n].wait()
        give = buf[n, :, pl.ds(other, width)]
        keep = buf[n, :, pl.ds(own, width)]
        give_all[n] = give
        if n < 2:
            give_kv[n] = give
            keep_kv[n] = keep
        else:
            keep_rest[n - 2] = keep
    for copy in copies[len(arrays) :]:
        copy.wait()
    params[...] = small[0 : 2 * poles + 1, pl.ds(own, width)]


def rows3(values):
    return jnp.broadcast_to(values[:, None, :], (values.shape[0], SUBS, values.shape[1]))


def each_group(poles, width, body):
    pole_groups = poles // GROUP
    lane_groups = width // LANES

    def step(index, carry):
        lane_group = index // pole_groups
        first_lane = pl.multiple_of(lane_group * LANES, LANES)
        first_pole = pl.multiple_of((index % pole_groups) * GROUP, GROUP)
        body(first_pole, lane_group, first_lane)
        return carry

    lax.fori_loop(0, pole_groups * lane_groups, step, 0)


def head_body(keep_rest, given, params, delta, totals, slots, head_ref):
    rows, width = keep_rest.shape[1:]
    poles = totals.shape[0]
    chips = slots.shape[0]
    core, chip = place()
    own, other = halves(core, width)
    tokens = delta.shape[1]
    steps = tokens // SUBS
    mine = pl.multiple_of(core * rows, rows)
    theirs = pl.multiple_of((1 - core) * rows, rows)
    for lane_group in range(width // LANES):
        lanes = slice(lane_group * LANES, (lane_group + 1) * LANES)
        delta[lane_group, pl.ds(mine, rows), :] = keep_rest[1, :, lanes].astype(F32) * keep_rest[
            2, :, lanes
        ].astype(F32)
        delta[lane_group, pl.ds(theirs, rows), :] = given[3, :, lanes].astype(F32) * given[
            4, :, lanes
        ].astype(F32)

    def group(first_pole, lane_group, first_lane):
        rate = params[pl.ds(first_pole, GROUP), pl.ds(first_lane, LANES)]
        lam = rows3(jnp.exp(-rate))
        state = jnp.zeros((GROUP, SUBS, LANES), F32)
        for j in reversed(range(steps)):
            state = lam * state + delta[lane_group, pl.ds(j, SUBS, stride=steps), :][None]
        totals[pl.ds(first_pole, GROUP), :, pl.ds(first_lane, LANES)] = state
        block = lax.broadcasted_iota(jnp.int32, (GROUP, SUBS, LANES), 1).astype(F32)
        power = jnp.exp(-rows3(rate) * (block * steps))
        head_ref[pl.ds(first_pole, GROUP), pl.ds(first_lane, LANES)] = jnp.sum(power * state, axis=1)

    each_group(poles, width, group)
    head = head_ref[...].astype(BF16)
    for j in range(chips):
        slots[j] = head


def around(own, rate, tokens, order, out):
    decay = jnp.exp(-rate * tokens)
    value = own(order[-1])
    power = decay
    for n in reversed(order[:-1]):
        value = value + power * own(n)
        power = power * decay
    value = value / (1.0 - jnp.exp(-rate * (tokens * len(order))))
    for n in order:
        out[n] = value
        value = own(n) + decay * value


def block_ids(shape):
    return lax.broadcasted_iota(jnp.int32, shape, 1)


def entering_later(totals, incoming, lam_block):
    ids = block_ids(totals.shape)
    value = jnp.where(ids == SUBS - 1, rows3(incoming), pltpu.roll(totals, SUBS - 1, 1))
    power = lam_block
    for shift in (1, 2, 4):
        moved = pltpu.roll(value, SUBS - shift, 1)
        value = value + jnp.where(ids < SUBS - shift, power * moved, 0.0)
        power = power * power
    return value


def entering_earlier(totals, arriving, lam_block):
    ids = block_ids(totals.shape)
    value = jnp.where(ids == 0, rows3(arriving), pltpu.roll(totals, 1, 1))
    power = lam_block
    for shift in (1, 2, 4):
        moved = pltpu.roll(value, shift, 1)
        value = value + jnp.where(ids >= shift, power * moved, 0.0)
        power = power * power
    return value


def pole_weights(rate):
    tangent = jnp.tanh(rate)
    return jnp.sqrt(2.0 * tangent / (1.0 + tangent))


def merge_body(keep_kv, given, chip_kv):
    rows = keep_kv.shape[1]
    core, chip = place()
    for slot in range(2):
        chip_kv[slot, pl.ds(pl.multiple_of(core * rows, rows), rows), :] = keep_kv[slot]
        chip_kv[slot, pl.ds(pl.multiple_of((1 - core) * rows, rows), rows), :] = given[slot]


def assemble(core, keep_rest, chip_kv, given, same1, cross1, far_kv, qbuf, kbuf, vbuf):
    rows = keep_rest.shape[1]
    tokens = 2 * rows
    mine = pl.multiple_of(core * rows, rows)
    theirs = pl.multiple_of((1 - core) * rows, rows)
    qbuf[pl.ds(mine, rows), :] = keep_rest[0]
    qbuf[pl.ds(theirs, rows), :] = given[2]
    for slot, buf in ((0, kbuf), (1, vbuf)):
        buf[0:tokens, :] = far_kv[slot]
        buf[pl.ds(mine + tokens, rows), :] = same1[slot]
        buf[pl.ds(theirs + tokens, rows), :] = cross1[slot]
        buf[2 * tokens : 3 * tokens, :] = chip_kv[slot]


def allowed_pairs(rows):
    span = (WIN + 1) * rows
    key_ids = lax.broadcasted_iota(jnp.int32, (span, rows), 0)
    row_ids = lax.broadcasted_iota(jnp.int32, (span, rows), 1)
    return (key_ids > row_ids) & (key_ids <= row_ids + WIN * rows)


def forward_body(
    keep_rest, chip_kv, given, same1, cross1, far_kv, stats, attended, qbuf, kbuf, vbuf
):
    rows, width = keep_rest.shape[1:]
    tokens = 2 * rows
    core, chip = place()
    scale = 1.0 / math.sqrt(HEAD)
    assemble(core, keep_rest, chip_kv, given, same1, cross1, far_kv, qbuf, kbuf, vbuf)
    span = (WIN + 1) * rows
    allowed = allowed_pairs(rows)
    for head in range(width // HEAD):
        at_head = slice(head * HEAD, (head + 1) * HEAD)
        for block in range(tokens // rows):
            at_rows = slice(block * rows, (block + 1) * rows)
            at_keys = slice(block * rows, block * rows + span)
            scores = (
                lax.dot_general(
                    kbuf[at_keys, at_head], qbuf[at_rows, at_head], OVER_HEAD, preferred_element_type=F32
                )
                * scale
            )
            scores = jnp.where(allowed, scores, -jnp.inf)
            top = jnp.max(scores, axis=0, keepdims=True)
            raised = jnp.exp(scores - top)
            share = 1.0 / jnp.sum(raised, axis=0, keepdims=True)
            probability = raised * share
            stats[head, block, 0:1, :] = top
            stats[head, block, 1:2, :] = share
            attended[head, at_rows, :] = (
                lax.dot_general(
                    probability.astype(BF16), vbuf[at_keys, at_head], OVER_KEYS, preferred_element_type=F32
                )
                .astype(BF16)
                .astype(F32)
            )


def tail_body(attended, delta, totals, params, tail_totals, slots, tail_ref, part_ref):
    poles, _, width = totals.shape
    steps = delta.shape[1] // SUBS
    chips = slots.shape[0]

    def tail_group(first_pole, lane_group, first_lane):
        rate = params[pl.ds(first_pole, GROUP), pl.ds(first_lane, LANES)]
        pole_at = pl.ds(first_pole, GROUP)
        lane_at = pl.ds(first_lane, LANES)
        lam = rows3(jnp.exp(-rate))
        state = jnp.zeros((GROUP, SUBS, LANES), F32)
        matched = jnp.zeros((GROUP, SUBS, LANES), F32)
        for j in range(steps):
            at = pl.ds(j, SUBS, stride=steps)
            state = lam * state + attended[lane_group, at, :][None]
            matched = matched + delta[lane_group, at, :][None] * state
        tail_totals[pole_at, :, lane_at] = state
        lam_block = rows3(jnp.exp(-rate * steps))
        entering = entering_earlier(state, jnp.zeros((GROUP, LANES), F32), lam_block)
        full = state + lam_block * entering
        matched = matched + lam * totals[pole_at, :, lane_at] * entering
        tail_ref[pole_at, lane_at] = full[:, SUBS - 1, :]
        part_ref[pole_at, lane_at] = jnp.sum(matched, axis=1)

    each_group(poles, width, tail_group)
    tail = tail_ref[...].astype(BF16)
    part = part_ref[...].astype(BF16)
    for j in range(chips):
        slots[j, 0:poles, :] = tail
        slots[j, poles : 2 * poles, :] = part


def backward_body(
    keep_rest,
    chip_kv,
    given,
    same1,
    cross1,
    far_kv,
    stats,
    delta,
    totals,
    slots_in,
    params,
    dq,
    dkv_chip,
    out_far,
    out_same1,
    out_cross1,
    incoming_all,
    qbuf,
    kbuf,
    vbuf,
    adj16,
    adj32,
    dk_acc,
    dv_acc,
):
    tokens, width = qbuf.shape
    rows = tokens // 2
    poles = totals.shape[0]
    steps = tokens // SUBS
    chips = slots_in.shape[0]
    core, chip = place()
    mine = pl.multiple_of(core * rows, rows)
    theirs = pl.multiple_of((1 - core) * rows, rows)
    scale = 1.0 / math.sqrt(HEAD)
    assemble(core, keep_rest, chip_kv, given, same1, cross1, far_kv, qbuf, kbuf, vbuf)

    around(
        lambda n: slots_in[n].astype(F32),
        params[0:poles, :],
        tokens,
        list(reversed(range(chips))),
        incoming_all,
    )
    for lane_group in range(width // LANES):
        gain = params[2 * poles : 2 * poles + 1, lane_group * LANES : (lane_group + 1) * LANES]
        adj32[lane_group] = gain * delta[lane_group]

    def adjoint_group(first_pole, lane_group, first_lane):
        rate = params[pl.ds(first_pole, GROUP), pl.ds(first_lane, LANES)]
        lam = rows3(jnp.exp(-rate))
        mixing = rows3(
            params[pl.ds(poles + first_pole, GROUP), pl.ds(first_lane, LANES)] * pole_weights(rate)
        )
        lane_at = pl.ds(first_lane, LANES)
        state = entering_later(
            totals[pl.ds(first_pole, GROUP), :, lane_at],
            incoming_all[chip, pl.ds(first_pole, GROUP), lane_at],
            rows3(jnp.exp(-rate * steps)),
        )
        for j in reversed(range(steps)):
            at = pl.ds(j, SUBS, stride=steps)
            state = lam * state + delta[lane_group, at, :][None]
            adj32[lane_group, at, :] = adj32[lane_group, at, :] + jnp.sum(mixing * state, axis=0)

    each_group(poles, width, adjoint_group)
    adj16[...] = adj32[...].astype(BF16)

    span = (WIN + 1) * rows
    allowed = allowed_pairs(rows)
    for head in range(width // HEAD):
        at_head = slice(head * HEAD, (head + 1) * HEAD)
        for block in range(tokens // rows):
            at_rows = slice(block * rows, (block + 1) * rows)
            at_keys = slice(block * rows, block * rows + span)
            query = qbuf[at_rows, at_head]
            key = kbuf[at_keys, at_head]
            value = vbuf[at_keys, at_head]
            adjoint = adj16[head, at_rows, :]
            scores = lax.dot_general(key, query, OVER_HEAD, preferred_element_type=F32) * scale
            scores = jnp.where(allowed, scores, -jnp.inf)
            probability = jnp.exp(scores - stats[head, block, 0:1, :]) * stats[head, block, 1:2, :]
            rounded = probability.astype(BF16)
            weight = lax.dot_general(value, adjoint, OVER_HEAD, preferred_element_type=F32)
            inner = jnp.sum(probability * weight, axis=0, keepdims=True)
            score_adjoint = (probability * (weight - inner) * scale).astype(BF16)
            dq[at_rows, at_head] = lax.dot_general(
                score_adjoint, key, OVER_KEYS, preferred_element_type=F32
            ).astype(BF16)
            dk = jnp.dot(score_adjoint, query, preferred_element_type=F32)
            dv = jnp.dot(rounded, adjoint, preferred_element_type=F32)
            if block == 0:
                dk_acc[at_keys, at_head] = dk
                dv_acc[at_keys, at_head] = dv
            else:
                edge = span - rows
                first = slice(block * rows, block * rows + edge)
                last = slice(block * rows + edge, block * rows + span)
                dk_acc[first, at_head] = dk_acc[first, at_head] + dk[:edge]
                dv_acc[first, at_head] = dv_acc[first, at_head] + dv[:edge]
                dk_acc[last, at_head] = dk[edge:]
                dv_acc[last, at_head] = dv[edge:]

    for slot, acc in ((0, dk_acc), (1, dv_acc)):
        out_far[slot] = acc[0:tokens, :].astype(BF16)
        out_same1[slot] = acc[pl.ds(mine + tokens, rows), :].astype(BF16)
        out_cross1[slot] = acc[pl.ds(theirs + tokens, rows), :].astype(BF16)
        dkv_chip[slot] = acc[2 * tokens : 3 * tokens, :]


def far_body(dkv_chip, far, dq, own_total, give):
    rows = own_total.shape[1]
    core, chip = place()
    mine = pl.ds(pl.multiple_of(core * rows, rows), rows)
    theirs = pl.ds(pl.multiple_of((1 - core) * rows, rows), rows)
    for slot in range(2):
        own_total[slot] = dkv_chip[slot, mine, :] + far[slot, mine, :].astype(F32)
        give[slot] = (dkv_chip[slot, theirs, :] + far[slot, theirs, :].astype(F32)).astype(BF16)
    give[2] = dq[theirs, :]


def near_body(own_total, same1, cross1, own, other):
    own[...] = (own_total[...] + same1[...].astype(F32)).astype(BF16)
    other[...] = cross1[...].astype(F32)


def gate_body(
    keep_rest,
    given,
    attended,
    tail_totals,
    slots_in,
    incoming_all,
    params,
    partner,
    gate_keep,
    gate_give,
    res_keep,
    mix32,
    arriving_ref,
):
    core, chip = place()
    rows, width = keep_rest.shape[1:]
    poles = tail_totals.shape[0]
    tokens = attended.shape[1]
    steps = tokens // SUBS
    chips = slots_in.shape[0]
    mine = pl.multiple_of(core * rows, rows)
    theirs = pl.multiple_of((1 - core) * rows, rows)
    rate = params[0:poles, :]
    around(
        lambda n: slots_in[n, 0:poles, :].astype(F32), rate, tokens, list(range(chips)), arriving_ref
    )
    parts = slots_in[0, poles : 2 * poles, :].astype(F32)
    crossed = slots_in[0, 0:poles, :].astype(F32) * incoming_all[0]
    for n in range(1, chips):
        parts = parts + slots_in[n, poles : 2 * poles, :].astype(F32)
        crossed = crossed + slots_in[n, 0:poles, :].astype(F32) * incoming_all[n]
    total = pole_weights(rate) * (parts + jnp.exp(-rate) * crossed)
    res_keep[...] = total
    high = total.astype(BF16)
    gate_give[rows : rows + poles, :] = high
    gate_give[rows + poles : rows + 2 * poles, :] = (total - high.astype(F32)).astype(BF16)
    first = rows + 2 * poles
    for slot in range(3):
        gate_give[first + slot * rows : first + (slot + 1) * rows, :] = partner[slot]
    for lane_group in range(width // LANES):
        gain = params[2 * poles : 2 * poles + 1, lane_group * LANES : (lane_group + 1) * LANES]
        mix32[lane_group] = gain * attended[lane_group]

    def group(first_pole, lane_group, first_lane):
        rate = params[pl.ds(first_pole, GROUP), pl.ds(first_lane, LANES)]
        lam = rows3(jnp.exp(-rate))
        mixing = rows3(
            params[pl.ds(poles + first_pole, GROUP), pl.ds(first_lane, LANES)] * pole_weights(rate)
        )
        lane_at = pl.ds(first_lane, LANES)
        pole_at = pl.ds(first_pole, GROUP)
        state = entering_earlier(
            tail_totals[pole_at, :, lane_at],
            arriving_ref[chip, pole_at, lane_at],
            rows3(jnp.exp(-rate * steps)),
        )
        for j in range(steps):
            at = pl.ds(j, SUBS, stride=steps)
            state = lam * state + attended[lane_group, at, :][None]
            mix32[lane_group, at, :] = mix32[lane_group, at, :] + jnp.sum(mixing * state, axis=0)

    each_group(poles, width, group)
    for lane_group in range(width // LANES):
        lanes = slice(lane_group * LANES, (lane_group + 1) * LANES)
        gate_keep[:, lanes] = (
            keep_rest[2, :, lanes].astype(F32) * mix32[lane_group, pl.ds(mine, rows), :]
        ).astype(BF16)
        gate_give[0:rows, lanes] = (
            given[4, :, lanes].astype(F32) * mix32[lane_group, pl.ds(theirs, rows), :]
        ).astype(BF16)


def final_body(all_dq, own_part, other_part, gate_keep, gate_in, res_keep, dq, dk, dv, dgate, dres):
    rows, width = gate_keep.shape
    poles = res_keep.shape[0]
    core, chip = place()
    own, other = halves(core, width)
    first = rows + 2 * poles
    for slot, out in ((0, dk), (1, dv)):
        out[:, pl.ds(own, width)] = own_part[slot]
        out[:, pl.ds(other, width)] = (
            gate_in[first + slot * rows : first + (slot + 1) * rows, :].astype(F32) + other_part[slot]
        ).astype(BF16)
    dq[:, pl.ds(own, width)] = all_dq[pl.ds(pl.multiple_of(core * rows, rows), rows), :]
    dq[:, pl.ds(other, width)] = gate_in[first + 2 * rows : first + 3 * rows, :]
    dgate[:, pl.ds(own, width)] = gate_keep[...]
    dgate[:, pl.ds(other, width)] = gate_in[0:rows, :]
    dres[:, pl.ds(own, width)] = res_keep[...]
    dres[:, pl.ds(other, width)] = gate_in[rows : rows + poles, :].astype(F32) + gate_in[
        rows + poles : rows + 2 * poles, :
    ].astype(F32)


def chip_shift(array, by, crossed):
    members = lax.axis_size("ctx")
    pairs = []
    for source in range(members):
        chip, core = source // 2, source % 2
        target = ((chip + by) % (members // 2)) * 2 + ((1 - core) if crossed else core)
        pairs.append((source, target))
    return lax.ppermute(array, "ctx", pairs)


def chip_exchange(slots):
    members = lax.axis_size("ctx")
    groups = [list(range(core, members, 2)) for core in range(2)]
    return lax.all_to_all(slots, "ctx", 0, 0, axis_index_groups=groups)


def local(queries, key_rows, value_rows, gate_values, cotangent, decay_rates, residues, skip_gain):
    rows, channels = queries.shape
    width = channels // 2
    poles = decay_rates.shape[0]
    chips = lax.axis_size("ctx") // 2
    tokens = 2 * rows
    skip = skip_gain.reshape(1, channels)
    groups = width // LANES
    pair = (2, rows, width)
    split = (groups, tokens, LANES)
    states = (poles, SUBS, width)
    span = (WIN + 2) * rows
    keep_kv, give_kv, keep_rest, give_all, params = call(
        pack_body,
        [
            (pair, BF16, True),
            (pair, BF16, True),
            ((3, rows, width), BF16, True),
            ((5, rows, width), BF16, True),
            ((2 * poles + 1, width), F32, True),
        ],
        scratch=[
            pltpu.VMEM((5, rows, channels), BF16),
            pltpu.VMEM((2 * poles + SUBS, channels), F32),
            pltpu.SemaphoreType.DMA((8,)),
        ],
        far=tuple(range(8)),
        name="pack",
    )(key_rows, value_rows, queries, gate_values, cotangent, decay_rates, residues, skip)
    given = chip_shift(give_all, 0, True)
    (chip_kv,) = call(merge_body, [((2, tokens, width), BF16, True)], near=(0, 1), name="chip_kv")(
        keep_kv, given
    )
    far_kv = chip_shift(chip_kv, 2, False)
    same1 = chip_shift(keep_kv, 1, False)
    cross1 = chip_shift(give_kv, 1, True)
    delta, totals, head_slots = call(
        head_body,
        [(split, F32, True), (states, F32, True), ((chips, poles, width), BF16, True)],
        scratch=[pltpu.VMEM((poles, width), F32)],
        near=(0, 1, 2),
        name="head_states",
    )(keep_rest, given, params)
    head_in = chip_exchange(head_slots)
    halo = (keep_rest, chip_kv, given, same1, cross1, far_kv)
    halo_buffers = [
        pltpu.VMEM((tokens, width), BF16),
        pltpu.VMEM((span, width), BF16),
        pltpu.VMEM((span, width), BF16),
    ]
    stats, attended = call(
        forward_body,
        [((groups, 2, SUBS, rows), F32, True), (split, F32, True)],
        scratch=halo_buffers,
        near=tuple(range(6)),
        cost=EARLY,
        name="forward",
    )(*halo)
    tail_totals, tail_slots = call(
        tail_body,
        [(states, F32, True), ((chips, 2 * poles, width), BF16, True)],
        scratch=[pltpu.VMEM((poles, width), F32), pltpu.VMEM((poles, width), F32)],
        near=(0, 1, 2, 3),
        name="tail",
    )(attended, delta, totals, params)
    tail_in = chip_exchange(tail_slots)
    dq, dkv_chip, out_far, out_same1, out_cross1, incoming_all = call(
        backward_body,
        [
            ((tokens, width), BF16, True),
            ((2, tokens, width), F32, True),
            ((2, tokens, width), BF16, True),
            (pair, BF16, True),
            (pair, BF16, True),
            ((chips, poles, width), F32, True),
        ],
        scratch=halo_buffers
        + [
            pltpu.VMEM(split, BF16),
            pltpu.VMEM(split, F32),
            pltpu.VMEM((span, width), F32),
            pltpu.VMEM((span, width), F32),
        ],
        near=tuple(range(11)),
        name="backward",
    )(*halo, stats, delta, totals, head_in, params)
    back_far = chip_shift(out_far, -2, False)
    back_same1 = chip_shift(out_same1, -1, False)
    back_cross1 = chip_shift(out_cross1, -1, True)
    own_total, partner = call(
        far_body,
        [(pair, F32, True), ((3, rows, width), BF16, True)],
        near=(0, 1, 2),
        cost=EARLY,
        name="far_sum",
    )(dkv_chip, back_far, dq)
    own_part, other_part = call(
        near_body,
        [(pair, BF16, True), (pair, F32, True)],
        near=(0, 1, 2),
        cost=EARLY,
        name="near_sum",
    )(own_total, back_same1, back_cross1)
    gate_keep, gate_give, res_keep = call(
        gate_body,
        [
            ((rows, width), BF16, True),
            ((4 * rows + 2 * poles, width), BF16, True),
            ((poles, width), F32, True),
        ],
        scratch=[pltpu.VMEM(split, F32), pltpu.VMEM((chips, poles, width), F32)],
        near=tuple(range(8)),
        name="gate",
    )(keep_rest, given, attended, tail_totals, tail_in, incoming_all, params, partner)
    gate_in = chip_shift(gate_give, 0, True)
    full = (rows, channels)
    wide = (full, BF16, False)
    return tuple(
        call(
            final_body,
            [wide, wide, wide, wide, ((poles, channels), F32, False)],
            near=tuple(range(6)),
            name="final",
        )(dq, own_part, other_part, gate_keep, gate_in, res_keep)
    )


def solution(mesh):
    wide = P(("dp", "ctx"), "head")
    in_specs = (wide, wide, wide, wide, wide, P(None, "head"), P(None, "head"), P("head"))
    out_specs = (wide, wide, wide, wide, P("dp", "head"))
    return jax.shard_map(local, mesh=mesh, in_specs=in_specs, out_specs=out_specs, check_vma=False)
```

```python
import math

import jax
import jax.numpy as jnp
from jax import lax
from jax.experimental import pallas as pl
from jax.experimental.pallas import tpu as pltpu
from jax.sharding import PartitionSpec as P

HEAD = 128
WIN = 4
LANES = 128
SUBS = 8
GROUP = 8
EARLY = pl.CostEstimate(flops=10**11, transcendentals=0, bytes_accessed=10**8)
F32 = jnp.float32
BF16 = jnp.bfloat16
OVER_KEYS = (((0,), (0,)), ((), ()))
OVER_HEAD = (((1,), (1,)), ((), ()))


def call(body, outs, scratch=(), near=(), far=(), cost=None, name=None):
    def run(*args):
        args = list(args)
        specs = []
        for n in range(len(args)):
            space = pltpu.HBM if n in far else pltpu.VMEM
            specs.append(pl.BlockSpec(memory_space=space))
            if n in near or n in far:
                args[n] = pltpu.with_memory_space_constraint(args[n], space)
        return pl.pallas_call(
            body,
            out_shape=[
                pltpu.VMEM(s, d) if local_out else jax.ShapeDtypeStruct(s, d) for s, d, local_out in outs
            ],
            in_specs=specs,
            out_specs=[pl.BlockSpec(memory_space=pltpu.VMEM)] * len(outs),
            scratch_shapes=list(scratch),
            compiler_params=pltpu.CompilerParams(vmem_limit_bytes=8 * 1024 * 1024),
            cost_estimate=cost,
            name=name,
        )(*args)

    return run


def place():
    index = lax.axis_index("ctx")
    return lax.rem(index, 2), lax.div(index, 2)


def halves(core, width):
    own = pl.multiple_of(core * width, LANES)
    other = pl.multiple_of((1 - core) * width, LANES)
    return own, other


def pack_body(
    k, v, q, gate, cot, rates, residues, skip, keep_kv, give_kv, keep_rest, give_all, params, buf, small, sems
):
    width = k.shape[1] // 2
    poles = rates.shape[0]
    own, other = halves(place()[0], width)
    arrays = (k, v, q, gate, cot)
    copies = [pltpu.make_async_copy(a, buf.at[n], sems.at[n]) for n, a in enumerate(arrays)]
    for n, (array, first, count) in enumerate(
        ((rates, 0, poles), (residues, poles, poles), (skip, 2 * poles, 1))
    ):
        copies.append(
            pltpu.make_async_copy(array, small.at[pl.ds(first, count)], sems.at[len(arrays) + n])
        )
    for copy in copies:
        copy.start()
    for n in range(len(arrays)):
        copies[n].wait()
        give = buf[n, :, pl.ds(other, width)]
        keep = buf[n, :, pl.ds(own, width)]
        give_all[n] = give
        if n < 2:
            give_kv[n] = give
            keep_kv[n] = keep
        else:
            keep_rest[n - 2] = keep
    for copy in copies[len(arrays) :]:
        copy.wait()
    params[...] = small[0 : 2 * poles + 1, pl.ds(own, width)]


def rows3(values):
    return jnp.broadcast_to(values[:, None, :], (values.shape[0], SUBS, values.shape[1]))


def each_group(poles, width, body):
    pole_groups = poles // GROUP
    lane_groups = width // LANES

    def step(index, carry):
        lane_group = index // pole_groups
        first_lane = pl.multiple_of(lane_group * LANES, LANES)
        first_pole = pl.multiple_of((index % pole_groups) * GROUP, GROUP)
        body(first_pole, lane_group, first_lane)
        return carry

    lax.fori_loop(0, pole_groups * lane_groups, step, 0)


def head_body(keep_rest, given, params, delta, totals, slots, head_ref):
    rows, width = keep_rest.shape[1:]
    poles = totals.shape[0]
    chips = slots.shape[0]
    core, chip = place()
    own, other = halves(core, width)
    tokens = delta.shape[1]
    steps = tokens // SUBS
    mine = pl.multiple_of(core * rows, rows)
    theirs = pl.multiple_of((1 - core) * rows, rows)
    for lane_group in range(width // LANES):
        lanes = slice(lane_group * LANES, (lane_group + 1) * LANES)
        delta[lane_group, pl.ds(mine, rows), :] = keep_rest[1, :, lanes].astype(F32) * keep_rest[
            2, :, lanes
        ].astype(F32)
        delta[lane_group, pl.ds(theirs, rows), :] = given[3, :, lanes].astype(F32) * given[
            4, :, lanes
        ].astype(F32)

    def group(first_pole, lane_group, first_lane):
        rate = params[pl.ds(first_pole, GROUP), pl.ds(first_lane, LANES)]
        lam = rows3(jnp.exp(-rate))
        state = jnp.zeros((GROUP, SUBS, LANES), F32)
        for j in reversed(range(steps)):
            state = lam * state + delta[lane_group, pl.ds(j, SUBS, stride=steps), :][None]
        totals[pl.ds(first_pole, GROUP), :, pl.ds(first_lane, LANES)] = state
        block = lax.broadcasted_iota(jnp.int32, (GROUP, SUBS, LANES), 1).astype(F32)
        power = jnp.exp(-rows3(rate) * (block * steps))
        head_ref[pl.ds(first_pole, GROUP), pl.ds(first_lane, LANES)] = jnp.sum(power * state, axis=1)

    each_group(poles, width, group)
    head = head_ref[...].astype(BF16)
    for j in range(chips):
        slots[j] = head


def around(own, rate, tokens, order, out):
    decay = jnp.exp(-rate * tokens)
    value = own(order[-1])
    power = decay
    for n in reversed(order[:-1]):
        value = value + power * own(n)
        power = power * decay
    value = value / (1.0 - jnp.exp(-rate * (tokens * len(order))))
    for n in order:
        out[n] = value
        value = own(n) + decay * value


def block_ids(shape):
    return lax.broadcasted_iota(jnp.int32, shape, 1)


def entering_later(totals, incoming, lam_block):
    ids = block_ids(totals.shape)
    value = jnp.where(ids == SUBS - 1, rows3(incoming), pltpu.roll(totals, SUBS - 1, 1))
    power = lam_block
    for shift in (1, 2, 4):
        moved = pltpu.roll(value, SUBS - shift, 1)
        value = value + jnp.where(ids < SUBS - shift, power * moved, 0.0)
        power = power * power
    return value


def entering_earlier(totals, arriving, lam_block):
    ids = block_ids(totals.shape)
    value = jnp.where(ids == 0, rows3(arriving), pltpu.roll(totals, 1, 1))
    power = lam_block
    for shift in (1, 2, 4):
        moved = pltpu.roll(value, shift, 1)
        value = value + jnp.where(ids >= shift, power * moved, 0.0)
        power = power * power
    return value


def pole_weights(rate):
    tangent = jnp.tanh(rate)
    return jnp.sqrt(2.0 * tangent / (1.0 + tangent))


def merge_body(keep_kv, given, chip_kv):
    rows = keep_kv.shape[1]
    core, chip = place()
    for slot in range(2):
        chip_kv[slot, pl.ds(pl.multiple_of(core * rows, rows), rows), :] = keep_kv[slot]
        chip_kv[slot, pl.ds(pl.multiple_of((1 - core) * rows, rows), rows), :] = given[slot]


def assemble(core, keep_rest, chip_kv, given, same1, cross1, far_kv, qbuf, kbuf, vbuf):
    rows = keep_rest.shape[1]
    tokens = 2 * rows
    mine = pl.multiple_of(core * rows, rows)
    theirs = pl.multiple_of((1 - core) * rows, rows)
    qbuf[pl.ds(mine, rows), :] = keep_rest[0]
    qbuf[pl.ds(theirs, rows), :] = given[2]
    for slot, buf in ((0, kbuf), (1, vbuf)):
        buf[0:tokens, :] = far_kv[slot]
        buf[pl.ds(mine + tokens, rows), :] = same1[slot]
        buf[pl.ds(theirs + tokens, rows), :] = cross1[slot]
        buf[2 * tokens : 3 * tokens, :] = chip_kv[slot]


def allowed_pairs(rows):
    span = (WIN + 1) * rows
    key_ids = lax.broadcasted_iota(jnp.int32, (span, rows), 0)
    row_ids = lax.broadcasted_iota(jnp.int32, (span, rows), 1)
    return (key_ids > row_ids) & (key_ids <= row_ids + WIN * rows)


def forward_body(
    keep_rest, chip_kv, given, same1, cross1, far_kv, stats, attended, qbuf, kbuf, vbuf
):
    rows, width = keep_rest.shape[1:]
    tokens = 2 * rows
    core, chip = place()
    scale = 1.0 / math.sqrt(HEAD)
    assemble(core, keep_rest, chip_kv, given, same1, cross1, far_kv, qbuf, kbuf, vbuf)
    span = (WIN + 1) * rows
    allowed = allowed_pairs(rows)
    for head in range(width // HEAD):
        at_head = slice(head * HEAD, (head + 1) * HEAD)
        for block in range(tokens // rows):
            at_rows = slice(block * rows, (block + 1) * rows)
            at_keys = slice(block * rows, block * rows + span)
            scores = (
                lax.dot_general(
                    kbuf[at_keys, at_head], qbuf[at_rows, at_head], OVER_HEAD, preferred_element_type=F32
                )
                * scale
            )
            scores = jnp.where(allowed, scores, -jnp.inf)
            top = jnp.max(scores, axis=0, keepdims=True)
            raised = jnp.exp(scores - top)
            share = 1.0 / jnp.sum(raised, axis=0, keepdims=True)
            probability = raised * share
            stats[head, block, 0:1, :] = top
            stats[head, block, 1:2, :] = share
            attended[head, at_rows, :] = (
                lax.dot_general(
                    probability.astype(BF16), vbuf[at_keys, at_head], OVER_KEYS, preferred_element_type=F32
                )
                .astype(BF16)
                .astype(F32)
            )


def tail_body(attended, delta, totals, params, tail_totals, slots, tail_ref, part_ref):
    poles, _, width = totals.shape
    steps = delta.shape[1] // SUBS
    chips = slots.shape[0]

    def tail_group(first_pole, lane_group, first_lane):
        rate = params[pl.ds(first_pole, GROUP), pl.ds(first_lane, LANES)]
        pole_at = pl.ds(first_pole, GROUP)
        lane_at = pl.ds(first_lane, LANES)
        lam = rows3(jnp.exp(-rate))
        state = jnp.zeros((GROUP, SUBS, LANES), F32)
        matched = jnp.zeros((GROUP, SUBS, LANES), F32)
        for j in range(steps):
            at = pl.ds(j, SUBS, stride=steps)
            state = lam * state + attended[lane_group, at, :][None]
            matched = matched + delta[lane_group, at, :][None] * state
        tail_totals[pole_at, :, lane_at] = state
        lam_block = rows3(jnp.exp(-rate * steps))
        entering = entering_earlier(state, jnp.zeros((GROUP, LANES), F32), lam_block)
        full = state + lam_block * entering
        matched = matched + lam * totals[pole_at, :, lane_at] * entering
        tail_ref[pole_at, lane_at] = full[:, SUBS - 1, :]
        part_ref[pole_at, lane_at] = jnp.sum(matched, axis=1)

    each_group(poles, width, tail_group)
    tail = tail_ref[...].astype(BF16)
    part = part_ref[...].astype(BF16)
    for j in range(chips):
        slots[j, 0:poles, :] = tail
        slots[j, poles : 2 * poles, :] = part


def backward_body(
    keep_rest,
    chip_kv,
    given,
    same1,
    cross1,
    far_kv,
    stats,
    tail_totals,
    delta,
    totals,
    slots_in,
    params,
    dq,
    dkv_chip,
    out_far,
    out_same1,
    out_cross1,
    incoming_all,
    qbuf,
    kbuf,
    vbuf,
    adj16,
    adj32,
    dk_acc,
    dv_acc,
):
    tokens, width = qbuf.shape
    rows = tokens // 2
    poles = totals.shape[0]
    steps = tokens // SUBS
    chips = slots_in.shape[0]
    core, chip = place()
    mine = pl.multiple_of(core * rows, rows)
    theirs = pl.multiple_of((1 - core) * rows, rows)
    scale = 1.0 / math.sqrt(HEAD)
    assemble(core, keep_rest, chip_kv, given, same1, cross1, far_kv, qbuf, kbuf, vbuf)

    around(
        lambda n: slots_in[n].astype(F32),
        params[0:poles, :],
        tokens,
        list(reversed(range(chips))),
        incoming_all,
    )
    for lane_group in range(width // LANES):
        gain = params[2 * poles : 2 * poles + 1, lane_group * LANES : (lane_group + 1) * LANES]
        adj32[lane_group] = gain * delta[lane_group]

    def adjoint_group(first_pole, lane_group, first_lane):
        rate = params[pl.ds(first_pole, GROUP), pl.ds(first_lane, LANES)]
        lam = rows3(jnp.exp(-rate))
        mixing = rows3(
            params[pl.ds(poles + first_pole, GROUP), pl.ds(first_lane, LANES)] * pole_weights(rate)
        )
        lane_at = pl.ds(first_lane, LANES)
        state = entering_later(
            totals[pl.ds(first_pole, GROUP), :, lane_at],
            incoming_all[chip, pl.ds(first_pole, GROUP), lane_at],
            rows3(jnp.exp(-rate * steps)),
        )
        for j in reversed(range(steps)):
            at = pl.ds(j, SUBS, stride=steps)
            state = lam * state + delta[lane_group, at, :][None]
            adj32[lane_group, at, :] = adj32[lane_group, at, :] + jnp.sum(mixing * state, axis=0)

    each_group(poles, width, adjoint_group)
    adj16[...] = adj32[...].astype(BF16)

    span = (WIN + 1) * rows
    allowed = allowed_pairs(rows)
    for head in range(width // HEAD):
        at_head = slice(head * HEAD, (head + 1) * HEAD)
        for block in range(tokens // rows):
            at_rows = slice(block * rows, (block + 1) * rows)
            at_keys = slice(block * rows, block * rows + span)
            query = qbuf[at_rows, at_head]
            key = kbuf[at_keys, at_head]
            value = vbuf[at_keys, at_head]
            adjoint = adj16[head, at_rows, :]
            scores = lax.dot_general(key, query, OVER_HEAD, preferred_element_type=F32) * scale
            scores = jnp.where(allowed, scores, -jnp.inf)
            probability = jnp.exp(scores - stats[head, block, 0:1, :]) * stats[head, block, 1:2, :]
            rounded = probability.astype(BF16)
            weight = lax.dot_general(value, adjoint, OVER_HEAD, preferred_element_type=F32)
            inner = jnp.sum(probability * weight, axis=0, keepdims=True)
            score_adjoint = (probability * (weight - inner) * scale).astype(BF16)
            dq[at_rows, at_head] = lax.dot_general(
                score_adjoint, key, OVER_KEYS, preferred_element_type=F32
            ).astype(BF16)
            dk = jnp.dot(score_adjoint, query, preferred_element_type=F32)
            dv = jnp.dot(rounded, adjoint, preferred_element_type=F32)
            if block == 0:
                dk_acc[at_keys, at_head] = dk
                dv_acc[at_keys, at_head] = dv
            else:
                edge = span - rows
                first = slice(block * rows, block * rows + edge)
                last = slice(block * rows + edge, block * rows + span)
                dk_acc[first, at_head] = dk_acc[first, at_head] + dk[:edge]
                dv_acc[first, at_head] = dv_acc[first, at_head] + dv[:edge]
                dk_acc[last, at_head] = dk[edge:]
                dv_acc[last, at_head] = dv[edge:]

    for slot, acc in ((0, dk_acc), (1, dv_acc)):
        out_far[slot] = acc[0:tokens, :].astype(BF16)
        out_same1[slot] = acc[pl.ds(mine + tokens, rows), :].astype(BF16)
        out_cross1[slot] = acc[pl.ds(theirs + tokens, rows), :].astype(BF16)
        dkv_chip[slot] = acc[2 * tokens : 3 * tokens, :]


def far_body(dkv_chip, far, dq, own_total, give):
    rows = own_total.shape[1]
    core, chip = place()
    mine = pl.ds(pl.multiple_of(core * rows, rows), rows)
    theirs = pl.ds(pl.multiple_of((1 - core) * rows, rows), rows)
    for slot in range(2):
        own_total[slot] = dkv_chip[slot, mine, :] + far[slot, mine, :].astype(F32)
        give[slot] = (dkv_chip[slot, theirs, :] + far[slot, theirs, :].astype(F32)).astype(BF16)
    give[2] = dq[theirs, :]


def near_body(own_total, same1, cross1, own, other):
    own[...] = (own_total[...] + same1[...].astype(F32)).astype(BF16)
    other[...] = cross1[...].astype(F32)


def gate_body(
    keep_rest,
    given,
    attended,
    tail_totals,
    slots_in,
    incoming_all,
    params,
    partner,
    gate_keep,
    gate_give,
    res_keep,
    mix32,
    arriving_ref,
):
    core, chip = place()
    rows, width = keep_rest.shape[1:]
    poles = tail_totals.shape[0]
    tokens = attended.shape[1]
    steps = tokens // SUBS
    chips = slots_in.shape[0]
    mine = pl.multiple_of(core * rows, rows)
    theirs = pl.multiple_of((1 - core) * rows, rows)
    rate = params[0:poles, :]
    around(
        lambda n: slots_in[n, 0:poles, :].astype(F32), rate, tokens, list(range(chips)), arriving_ref
    )
    parts = slots_in[0, poles : 2 * poles, :].astype(F32)
    crossed = slots_in[0, 0:poles, :].astype(F32) * incoming_all[0]
    for n in range(1, chips):
        parts = parts + slots_in[n, poles : 2 * poles, :].astype(F32)
        crossed = crossed + slots_in[n, 0:poles, :].astype(F32) * incoming_all[n]
    total = pole_weights(rate) * (parts + jnp.exp(-rate) * crossed)
    res_keep[...] = total
    high = total.astype(BF16)
    gate_give[rows : rows + poles, :] = high
    gate_give[rows + poles : rows + 2 * poles, :] = (total - high.astype(F32)).astype(BF16)
    first = rows + 2 * poles
    for slot in range(3):
        gate_give[first + slot * rows : first + (slot + 1) * rows, :] = partner[slot]
    for lane_group in range(width // LANES):
        gain = params[2 * poles : 2 * poles + 1, lane_group * LANES : (lane_group + 1) * LANES]
        mix32[lane_group] = gain * attended[lane_group]

    def group(first_pole, lane_group, first_lane):
        rate = params[pl.ds(first_pole, GROUP), pl.ds(first_lane, LANES)]
        lam = rows3(jnp.exp(-rate))
        mixing = rows3(
            params[pl.ds(poles + first_pole, GROUP), pl.ds(first_lane, LANES)] * pole_weights(rate)
        )
        lane_at = pl.ds(first_lane, LANES)
        pole_at = pl.ds(first_pole, GROUP)
        state = entering_earlier(
            tail_totals[pole_at, :, lane_at],
            arriving_ref[chip, pole_at, lane_at],
            rows3(jnp.exp(-rate * steps)),
        )
        for j in range(steps):
            at = pl.ds(j, SUBS, stride=steps)
            state = lam * state + attended[lane_group, at, :][None]
            mix32[lane_group, at, :] = mix32[lane_group, at, :] + jnp.sum(mixing * state, axis=0)

    each_group(poles, width, group)
    for lane_group in range(width // LANES):
        lanes = slice(lane_group * LANES, (lane_group + 1) * LANES)
        gate_keep[:, lanes] = (
            keep_rest[2, :, lanes].astype(F32) * mix32[lane_group, pl.ds(mine, rows), :]
        ).astype(BF16)
        gate_give[0:rows, lanes] = (
            given[4, :, lanes].astype(F32) * mix32[lane_group, pl.ds(theirs, rows), :]
        ).astype(BF16)


def final_body(all_dq, own_part, other_part, gate_keep, gate_in, res_keep, dq, dk, dv, dgate, dres):
    rows, width = gate_keep.shape
    poles = res_keep.shape[0]
    core, chip = place()
    own, other = halves(core, width)
    first = rows + 2 * poles
    for slot, out in ((0, dk), (1, dv)):
        out[:, pl.ds(own, width)] = own_part[slot]
        out[:, pl.ds(other, width)] = (
            gate_in[first + slot * rows : first + (slot + 1) * rows, :].astype(F32) + other_part[slot]
        ).astype(BF16)
    dq[:, pl.ds(own, width)] = all_dq[pl.ds(pl.multiple_of(core * rows, rows), rows), :]
    dq[:, pl.ds(other, width)] = gate_in[first + 2 * rows : first + 3 * rows, :]
    dgate[:, pl.ds(own, width)] = gate_keep[...]
    dgate[:, pl.ds(other, width)] = gate_in[0:rows, :]
    dres[:, pl.ds(own, width)] = res_keep[...]
    dres[:, pl.ds(other, width)] = gate_in[rows : rows + poles, :].astype(F32) + gate_in[
        rows + poles : rows + 2 * poles, :
    ].astype(F32)


def chip_shift(array, by, crossed):
    members = lax.axis_size("ctx")
    pairs = []
    for source in range(members):
        chip, core = source // 2, source % 2
        target = ((chip + by) % (members // 2)) * 2 + ((1 - core) if crossed else core)
        pairs.append((source, target))
    return lax.ppermute(array, "ctx", pairs)


def chip_exchange(slots):
    members = lax.axis_size("ctx")
    groups = [list(range(core, members, 2)) for core in range(2)]
    return lax.all_to_all(slots, "ctx", 0, 0, axis_index_groups=groups)


def local(queries, key_rows, value_rows, gate_values, cotangent, decay_rates, residues, skip_gain):
    rows, channels = queries.shape
    width = channels // 2
    poles = decay_rates.shape[0]
    chips = lax.axis_size("ctx") // 2
    tokens = 2 * rows
    skip = skip_gain.reshape(1, channels)
    groups = width // LANES
    pair = (2, rows, width)
    split = (groups, tokens, LANES)
    states = (poles, SUBS, width)
    span = (WIN + 2) * rows
    keep_kv, give_kv, keep_rest, give_all, params = call(
        pack_body,
        [
            (pair, BF16, True),
            (pair, BF16, True),
            ((3, rows, width), BF16, True),
            ((5, rows, width), BF16, True),
            ((2 * poles + 1, width), F32, True),
        ],
        scratch=[
            pltpu.VMEM((5, rows, channels), BF16),
            pltpu.VMEM((2 * poles + SUBS, channels), F32),
            pltpu.SemaphoreType.DMA((8,)),
        ],
        far=tuple(range(8)),
        name="pack",
    )(key_rows, value_rows, queries, gate_values, cotangent, decay_rates, residues, skip)
    given = chip_shift(give_all, 0, True)
    (chip_kv,) = call(merge_body, [((2, tokens, width), BF16, True)], near=(0, 1), name="chip_kv")(
        keep_kv, given
    )
    far_kv = chip_shift(chip_kv, 2, False)
    same1 = chip_shift(keep_kv, 1, False)
    cross1 = chip_shift(give_kv, 1, True)
    delta, totals, head_slots = call(
        head_body,
        [(split, F32, True), (states, F32, True), ((chips, poles, width), BF16, True)],
        scratch=[pltpu.VMEM((poles, width), F32)],
        near=(0, 1, 2),
        name="head_states",
    )(keep_rest, given, params)
    head_in = chip_exchange(head_slots)
    halo = (keep_rest, chip_kv, given, same1, cross1, far_kv)
    halo_buffers = [
        pltpu.VMEM((tokens, width), BF16),
        pltpu.VMEM((span, width), BF16),
        pltpu.VMEM((span, width), BF16),
    ]
    stats, attended = call(
        forward_body,
        [((groups, 2, SUBS, rows), F32, True), (split, F32, True)],
        scratch=halo_buffers,
        near=tuple(range(6)),
        cost=EARLY,
        name="forward",
    )(*halo)
    tail_totals, tail_slots = call(
        tail_body,
        [(states, F32, True), ((chips, 2 * poles, width), BF16, True)],
        scratch=[pltpu.VMEM((poles, width), F32), pltpu.VMEM((poles, width), F32)],
        near=(0, 1, 2, 3),
        name="tail",
    )(attended, delta, totals, params)
    tail_in = chip_exchange(tail_slots)
    dq, dkv_chip, out_far, out_same1, out_cross1, incoming_all = call(
        backward_body,
        [
            ((tokens, width), BF16, True),
            ((2, tokens, width), F32, True),
            ((2, tokens, width), BF16, True),
            (pair, BF16, True),
            (pair, BF16, True),
            ((chips, poles, width), F32, True),
        ],
        scratch=halo_buffers
        + [
            pltpu.VMEM(split, BF16),
            pltpu.VMEM(split, F32),
            pltpu.VMEM((span, width), F32),
            pltpu.VMEM((span, width), F32),
        ],
        near=tuple(range(12)),
        name="backward",
    )(*halo, stats, tail_totals, delta, totals, head_in, params)
    back_far = chip_shift(out_far, -2, False)
    back_same1 = chip_shift(out_same1, -1, False)
    back_cross1 = chip_shift(out_cross1, -1, True)
    own_total, partner = call(
        far_body,
        [(pair, F32, True), ((3, rows, width), BF16, True)],
        near=(0, 1, 2),
        cost=EARLY,
        name="far_sum",
    )(dkv_chip, back_far, dq)
    own_part, other_part = call(
        near_body,
        [(pair, BF16, True), (pair, F32, True)],
        near=(0, 1, 2),
        cost=EARLY,
        name="near_sum",
    )(own_total, back_same1, back_cross1)
    gate_keep, gate_give, res_keep = call(
        gate_body,
        [
            ((rows, width), BF16, True),
            ((4 * rows + 2 * poles, width), BF16, True),
            ((poles, width), F32, True),
        ],
        scratch=[pltpu.VMEM(split, F32), pltpu.VMEM((chips, poles, width), F32)],
        near=tuple(range(8)),
        name="gate",
    )(keep_rest, given, attended, tail_totals, tail_in, incoming_all, params, partner)
    gate_in = chip_shift(gate_give, 0, True)
    full = (rows, channels)
    wide = (full, BF16, False)
    return tuple(
        call(
            final_body,
            [wide, wide, wide, wide, ((poles, channels), F32, False)],
            near=tuple(range(6)),
            name="final",
        )(dq, own_part, other_part, gate_keep, gate_in, res_keep)
    )


def solution(mesh):
    wide = P(("dp", "ctx"), "head")
    in_specs = (wide, wide, wide, wide, wide, P(None, "head"), P(None, "head"), P("head"))
    out_specs = (wide, wide, wide, wide, P("dp", "head"))
    return jax.shard_map(local, mesh=mesh, in_specs=in_specs, out_specs=out_specs, check_vma=False)
```

```python
import math

import jax
import jax.numpy as jnp
from jax import lax
from jax.experimental import pallas as pl
from jax.experimental.pallas import tpu as pltpu
from jax.sharding import PartitionSpec as P

HEAD = 128
WIN = 4
LANES = 128
SUBS = 8
GROUP = 8
EARLY = pl.CostEstimate(flops=10**11, transcendentals=0, bytes_accessed=10**8)
F32 = jnp.float32
BF16 = jnp.bfloat16
OVER_KEYS = (((0,), (0,)), ((), ()))
OVER_HEAD = (((1,), (1,)), ((), ()))


def call(body, outs, scratch=(), near=(), far=(), cost=None, name=None):
    def run(*args):
        args = list(args)
        specs = []
        for n in range(len(args)):
            space = pltpu.HBM if n in far else pltpu.VMEM
            specs.append(pl.BlockSpec(memory_space=space))
            if n in near or n in far:
                args[n] = pltpu.with_memory_space_constraint(args[n], space)
        return pl.pallas_call(
            body,
            out_shape=[
                pltpu.VMEM(s, d) if local_out else jax.ShapeDtypeStruct(s, d) for s, d, local_out in outs
            ],
            in_specs=specs,
            out_specs=[pl.BlockSpec(memory_space=pltpu.VMEM)] * len(outs),
            scratch_shapes=list(scratch),
            compiler_params=pltpu.CompilerParams(vmem_limit_bytes=8 * 1024 * 1024),
            cost_estimate=cost,
            name=name,
        )(*args)

    return run


def place():
    index = lax.axis_index("ctx")
    return lax.rem(index, 2), lax.div(index, 2)


def halves(core, width):
    own = pl.multiple_of(core * width, LANES)
    other = pl.multiple_of((1 - core) * width, LANES)
    return own, other


def pack_body(
    k, v, q, gate, cot, rates, residues, skip, keep_kv, keep_rest, give_all, params, buf, small, sems
):
    width = k.shape[1] // 2
    poles = rates.shape[0]
    own, other = halves(place()[0], width)
    arrays = (k, v, q, gate, cot)
    copies = [pltpu.make_async_copy(a, buf.at[n], sems.at[n]) for n, a in enumerate(arrays)]
    for n, (array, first, count) in enumerate(
        ((rates, 0, poles), (residues, poles, poles), (skip, 2 * poles, 1))
    ):
        copies.append(
            pltpu.make_async_copy(array, small.at[pl.ds(first, count)], sems.at[len(arrays) + n])
        )
    for copy in copies:
        copy.start()
    for n in range(len(arrays)):
        copies[n].wait()
        keep = buf[n, :, pl.ds(own, width)]
        give_all[n] = buf[n, :, pl.ds(other, width)]
        if n < 2:
            keep_kv[n] = keep
        else:
            keep_rest[n - 2] = keep
    for copy in copies[len(arrays) :]:
        copy.wait()
    params[...] = small[0 : 2 * poles + 1, pl.ds(own, width)]


def rows3(values):
    return jnp.broadcast_to(values[:, None, :], (values.shape[0], SUBS, values.shape[1]))


def each_group(poles, width, body):
    pole_groups = poles // GROUP
    lane_groups = width // LANES

    def step(index, carry):
        lane_group = index // pole_groups
        first_lane = pl.multiple_of(lane_group * LANES, LANES)
        first_pole = pl.multiple_of((index % pole_groups) * GROUP, GROUP)
        body(first_pole, lane_group, first_lane)
        return carry

    lax.fori_loop(0, pole_groups * lane_groups, step, 0)


def head_body(keep_rest, given, params, delta, totals, slots, head_ref):
    rows, width = keep_rest.shape[1:]
    poles = totals.shape[0]
    chips = slots.shape[0]
    core, chip = place()
    own, other = halves(core, width)
    tokens = delta.shape[1]
    steps = tokens // SUBS
    mine = pl.multiple_of(core * rows, rows)
    theirs = pl.multiple_of((1 - core) * rows, rows)
    for lane_group in range(width // LANES):
        lanes = slice(lane_group * LANES, (lane_group + 1) * LANES)
        delta[lane_group, pl.ds(mine, rows), :] = keep_rest[1, :, lanes].astype(F32) * keep_rest[
            2, :, lanes
        ].astype(F32)
        delta[lane_group, pl.ds(theirs, rows), :] = given[3, :, lanes].astype(F32) * given[
            4, :, lanes
        ].astype(F32)

    def group(first_pole, lane_group, first_lane):
        rate = params[pl.ds(first_pole, GROUP), pl.ds(first_lane, LANES)]
        lam = rows3(jnp.exp(-rate))
        state = jnp.zeros((GROUP, SUBS, LANES), F32)
        for j in reversed(range(steps)):
            state = lam * state + delta[lane_group, pl.ds(j, SUBS, stride=steps), :][None]
        totals[pl.ds(first_pole, GROUP), :, pl.ds(first_lane, LANES)] = state
        block = lax.broadcasted_iota(jnp.int32, (GROUP, SUBS, LANES), 1).astype(F32)
        power = jnp.exp(-rows3(rate) * (block * steps))
        head_ref[pl.ds(first_pole, GROUP), pl.ds(first_lane, LANES)] = jnp.sum(power * state, axis=1)

    each_group(poles, width, group)
    head = head_ref[...].astype(BF16)
    for j in range(chips):
        slots[j] = head


def around(own, rate, tokens, order, out):
    decay = jnp.exp(-rate * tokens)
    value = own(order[-1])
    power = decay
    for n in reversed(order[:-1]):
        value = value + power * own(n)
        power = power * decay
    value = value / (1.0 - jnp.exp(-rate * (tokens * len(order))))
    for n in order:
        out[n] = value
        value = own(n) + decay * value


def block_ids(shape):
    return lax.broadcasted_iota(jnp.int32, shape, 1)


def entering_later(totals, incoming, lam_block):
    ids = block_ids(totals.shape)
    value = jnp.where(ids == SUBS - 1, rows3(incoming), pltpu.roll(totals, SUBS - 1, 1))
    power = lam_block
    for shift in (1, 2, 4):
        moved = pltpu.roll(value, SUBS - shift, 1)
        value = value + jnp.where(ids < SUBS - shift, power * moved, 0.0)
        power = power * power
    return value


def entering_earlier(totals, arriving, lam_block):
    ids = block_ids(totals.shape)
    value = jnp.where(ids == 0, rows3(arriving), pltpu.roll(totals, 1, 1))
    power = lam_block
    for shift in (1, 2, 4):
        moved = pltpu.roll(value, shift, 1)
        value = value + jnp.where(ids >= shift, power * moved, 0.0)
        power = power * power
    return value


def pole_weights(rate):
    tangent = jnp.tanh(rate)
    return jnp.sqrt(2.0 * tangent / (1.0 + tangent))


def merge_body(keep_kv, given, chip_kv):
    rows = keep_kv.shape[1]
    core, chip = place()
    for slot in range(2):
        chip_kv[slot, pl.ds(pl.multiple_of(core * rows, rows), rows), :] = keep_kv[slot]
        chip_kv[slot, pl.ds(pl.multiple_of((1 - core) * rows, rows), rows), :] = given[slot]


def assemble(core, keep_rest, chip_kv, given, near_kv, far_kv, qbuf, kbuf, vbuf):
    rows = keep_rest.shape[1]
    tokens = 2 * rows
    mine = pl.multiple_of(core * rows, rows)
    theirs = pl.multiple_of((1 - core) * rows, rows)
    qbuf[pl.ds(mine, rows), :] = keep_rest[0]
    qbuf[pl.ds(theirs, rows), :] = given[2]
    for slot, buf in ((0, kbuf), (1, vbuf)):
        buf[0:tokens, :] = far_kv[slot]
        buf[tokens : 2 * tokens, :] = near_kv[slot]
        buf[2 * tokens : 3 * tokens, :] = chip_kv[slot]


def allowed_pairs(rows):
    span = (WIN + 1) * rows
    key_ids = lax.broadcasted_iota(jnp.int32, (span, rows), 0)
    row_ids = lax.broadcasted_iota(jnp.int32, (span, rows), 1)
    return (key_ids > row_ids) & (key_ids <= row_ids + WIN * rows)


def forward_body(
    keep_rest, chip_kv, given, near_kv, far_kv, stats, attended, qbuf, kbuf, vbuf
):
    rows, width = keep_rest.shape[1:]
    tokens = 2 * rows
    core, chip = place()
    scale = 1.0 / math.sqrt(HEAD)
    assemble(core, keep_rest, chip_kv, given, near_kv, far_kv, qbuf, kbuf, vbuf)
    span = (WIN + 1) * rows
    allowed = allowed_pairs(rows)
    for head in range(width // HEAD):
        at_head = slice(head * HEAD, (head + 1) * HEAD)
        for block in range(tokens // rows):
            at_rows = slice(block * rows, (block + 1) * rows)
            at_keys = slice(block * rows, block * rows + span)
            scores = (
                lax.dot_general(
                    kbuf[at_keys, at_head], qbuf[at_rows, at_head], OVER_HEAD, preferred_element_type=F32
                )
                * scale
            )
            scores = jnp.where(allowed, scores, -jnp.inf)
            top = jnp.max(scores, axis=0, keepdims=True)
            raised = jnp.exp(scores - top)
            share = 1.0 / jnp.sum(raised, axis=0, keepdims=True)
            probability = raised * share
            stats[head, block, 0:1, :] = top
            stats[head, block, 1:2, :] = share
            attended[head, at_rows, :] = (
                lax.dot_general(
                    probability.astype(BF16), vbuf[at_keys, at_head], OVER_KEYS, preferred_element_type=F32
                )
                .astype(BF16)
                .astype(F32)
            )


def tail_body(attended, delta, totals, params, tail_totals, slots, tail_ref, part_ref):
    poles, _, width = totals.shape
    steps = delta.shape[1] // SUBS
    chips = slots.shape[0]

    def tail_group(first_pole, lane_group, first_lane):
        rate = params[pl.ds(first_pole, GROUP), pl.ds(first_lane, LANES)]
        pole_at = pl.ds(first_pole, GROUP)
        lane_at = pl.ds(first_lane, LANES)
        lam = rows3(jnp.exp(-rate))
        state = jnp.zeros((GROUP, SUBS, LANES), F32)
        matched = jnp.zeros((GROUP, SUBS, LANES), F32)
        for j in range(steps):
            at = pl.ds(j, SUBS, stride=steps)
            state = lam * state + attended[lane_group, at, :][None]
            matched = matched + delta[lane_group, at, :][None] * state
        tail_totals[pole_at, :, lane_at] = state
        lam_block = rows3(jnp.exp(-rate * steps))
        entering = entering_earlier(state, jnp.zeros((GROUP, LANES), F32), lam_block)
        full = state + lam_block * entering
        matched = matched + lam * totals[pole_at, :, lane_at] * entering
        tail_ref[pole_at, lane_at] = full[:, SUBS - 1, :]
        part_ref[pole_at, lane_at] = jnp.sum(matched, axis=1)

    each_group(poles, width, tail_group)
    tail = tail_ref[...].astype(BF16)
    part = part_ref[...].astype(BF16)
    for j in range(chips):
        slots[j, 0:poles, :] = tail
        slots[j, poles : 2 * poles, :] = part


def backward_body(
    keep_rest,
    chip_kv,
    given,
    near_kv,
    far_kv,
    stats,
    tail_totals,
    delta,
    totals,
    slots_in,
    params,
    dq,
    dkv_chip,
    out_far,
    out_same1,
    out_cross1,
    incoming_all,
    qbuf,
    kbuf,
    vbuf,
    adj16,
    adj32,
    dk_acc,
    dv_acc,
):
    tokens, width = qbuf.shape
    rows = tokens // 2
    poles = totals.shape[0]
    steps = tokens // SUBS
    chips = slots_in.shape[0]
    core, chip = place()
    mine = pl.multiple_of(core * rows, rows)
    theirs = pl.multiple_of((1 - core) * rows, rows)
    scale = 1.0 / math.sqrt(HEAD)
    assemble(core, keep_rest, chip_kv, given, near_kv, far_kv, qbuf, kbuf, vbuf)

    around(
        lambda n: slots_in[n].astype(F32),
        params[0:poles, :],
        tokens,
        list(reversed(range(chips))),
        incoming_all,
    )
    for lane_group in range(width // LANES):
        gain = params[2 * poles : 2 * poles + 1, lane_group * LANES : (lane_group + 1) * LANES]
        adj32[lane_group] = gain * delta[lane_group]

    def adjoint_group(first_pole, lane_group, first_lane):
        rate = params[pl.ds(first_pole, GROUP), pl.ds(first_lane, LANES)]
        lam = rows3(jnp.exp(-rate))
        mixing = rows3(
            params[pl.ds(poles + first_pole, GROUP), pl.ds(first_lane, LANES)] * pole_weights(rate)
        )
        lane_at = pl.ds(first_lane, LANES)
        state = entering_later(
            totals[pl.ds(first_pole, GROUP), :, lane_at],
            incoming_all[chip, pl.ds(first_pole, GROUP), lane_at],
            rows3(jnp.exp(-rate * steps)),
        )
        for j in reversed(range(steps)):
            at = pl.ds(j, SUBS, stride=steps)
            state = lam * state + delta[lane_group, at, :][None]
            adj32[lane_group, at, :] = adj32[lane_group, at, :] + jnp.sum(mixing * state, axis=0)

    each_group(poles, width, adjoint_group)
    adj16[...] = adj32[...].astype(BF16)

    span = (WIN + 1) * rows
    allowed = allowed_pairs(rows)
    for head in range(width // HEAD):
        at_head = slice(head * HEAD, (head + 1) * HEAD)
        for block in range(tokens // rows):
            at_rows = slice(block * rows, (block + 1) * rows)
            at_keys = slice(block * rows, block * rows + span)
            query = qbuf[at_rows, at_head]
            key = kbuf[at_keys, at_head]
            value = vbuf[at_keys, at_head]
            adjoint = adj16[head, at_rows, :]
            scores = lax.dot_general(key, query, OVER_HEAD, preferred_element_type=F32) * scale
            scores = jnp.where(allowed, scores, -jnp.inf)
            probability = jnp.exp(scores - stats[head, block, 0:1, :]) * stats[head, block, 1:2, :]
            rounded = probability.astype(BF16)
            weight = lax.dot_general(value, adjoint, OVER_HEAD, preferred_element_type=F32)
            inner = jnp.sum(probability * weight, axis=0, keepdims=True)
            score_adjoint = (probability * (weight - inner) * scale).astype(BF16)
            dq[at_rows, at_head] = lax.dot_general(
                score_adjoint, key, OVER_KEYS, preferred_element_type=F32
            ).astype(BF16)
            dk = jnp.dot(score_adjoint, query, preferred_element_type=F32)
            dv = jnp.dot(rounded, adjoint, preferred_element_type=F32)
            if block == 0:
                dk_acc[at_keys, at_head] = dk
                dv_acc[at_keys, at_head] = dv
            else:
                edge = span - rows
                first = slice(block * rows, block * rows + edge)
                last = slice(block * rows + edge, block * rows + span)
                dk_acc[first, at_head] = dk_acc[first, at_head] + dk[:edge]
                dv_acc[first, at_head] = dv_acc[first, at_head] + dv[:edge]
                dk_acc[last, at_head] = dk[edge:]
                dv_acc[last, at_head] = dv[edge:]

    for slot, acc in ((0, dk_acc), (1, dv_acc)):
        out_far[slot] = acc[0:tokens, :].astype(BF16)
        out_same1[slot] = acc[pl.ds(mine + tokens, rows), :].astype(BF16)
        out_cross1[slot] = acc[pl.ds(theirs + tokens, rows), :].astype(BF16)
        dkv_chip[slot] = acc[2 * tokens : 3 * tokens, :]


def far_body(dkv_chip, far, dq, own_total, give):
    rows = own_total.shape[1]
    core, chip = place()
    mine = pl.ds(pl.multiple_of(core * rows, rows), rows)
    theirs = pl.ds(pl.multiple_of((1 - core) * rows, rows), rows)
    for slot in range(2):
        own_total[slot] = dkv_chip[slot, mine, :] + far[slot, mine, :].astype(F32)
        give[slot] = (dkv_chip[slot, theirs, :] + far[slot, theirs, :].astype(F32)).astype(BF16)
    give[2] = dq[theirs, :]


def near_body(own_total, same1, cross1, own, other):
    own[...] = (own_total[...] + same1[...].astype(F32)).astype(BF16)
    other[...] = cross1[...].astype(F32)


def gate_body(
    keep_rest,
    given,
    attended,
    tail_totals,
    slots_in,
    incoming_all,
    params,
    partner,
    gate_keep,
    gate_give,
    res_keep,
    mix32,
    arriving_ref,
):
    core, chip = place()
    rows, width = keep_rest.shape[1:]
    poles = tail_totals.shape[0]
    tokens = attended.shape[1]
    steps = tokens // SUBS
    chips = slots_in.shape[0]
    mine = pl.multiple_of(core * rows, rows)
    theirs = pl.multiple_of((1 - core) * rows, rows)
    rate = params[0:poles, :]
    around(
        lambda n: slots_in[n, 0:poles, :].astype(F32), rate, tokens, list(range(chips)), arriving_ref
    )
    parts = slots_in[0, poles : 2 * poles, :].astype(F32)
    crossed = slots_in[0, 0:poles, :].astype(F32) * incoming_all[0]
    for n in range(1, chips):
        parts = parts + slots_in[n, poles : 2 * poles, :].astype(F32)
        crossed = crossed + slots_in[n, 0:poles, :].astype(F32) * incoming_all[n]
    total = pole_weights(rate) * (parts + jnp.exp(-rate) * crossed)
    res_keep[...] = total
    high = total.astype(BF16)
    gate_give[rows : rows + poles, :] = high
    gate_give[rows + poles : rows + 2 * poles, :] = (total - high.astype(F32)).astype(BF16)
    first = rows + 2 * poles
    for slot in range(3):
        gate_give[first + slot * rows : first + (slot + 1) * rows, :] = partner[slot]
    for lane_group in range(width // LANES):
        gain = params[2 * poles : 2 * poles + 1, lane_group * LANES : (lane_group + 1) * LANES]
        mix32[lane_group] = gain * attended[lane_group]

    def group(first_pole, lane_group, first_lane):
        rate = params[pl.ds(first_pole, GROUP), pl.ds(first_lane, LANES)]
        lam = rows3(jnp.exp(-rate))
        mixing = rows3(
            params[pl.ds(poles + first_pole, GROUP), pl.ds(first_lane, LANES)] * pole_weights(rate)
        )
        lane_at = pl.ds(first_lane, LANES)
        pole_at = pl.ds(first_pole, GROUP)
        state = entering_earlier(
            tail_totals[pole_at, :, lane_at],
            arriving_ref[chip, pole_at, lane_at],
            rows3(jnp.exp(-rate * steps)),
        )
        for j in range(steps):
            at = pl.ds(j, SUBS, stride=steps)
            state = lam * state + attended[lane_group, at, :][None]
            mix32[lane_group, at, :] = mix32[lane_group, at, :] + jnp.sum(mixing * state, axis=0)

    each_group(poles, width, group)
    for lane_group in range(width // LANES):
        lanes = slice(lane_group * LANES, (lane_group + 1) * LANES)
        gate_keep[:, lanes] = (
            keep_rest[2, :, lanes].astype(F32) * mix32[lane_group, pl.ds(mine, rows), :]
        ).astype(BF16)
        gate_give[0:rows, lanes] = (
            given[4, :, lanes].astype(F32) * mix32[lane_group, pl.ds(theirs, rows), :]
        ).astype(BF16)


def final_body(all_dq, own_part, other_part, gate_keep, gate_in, res_keep, dq, dk, dv, dgate, dres):
    rows, width = gate_keep.shape
    poles = res_keep.shape[0]
    core, chip = place()
    own, other = halves(core, width)
    first = rows + 2 * poles
    for slot, out in ((0, dk), (1, dv)):
        out[:, pl.ds(own, width)] = own_part[slot]
        out[:, pl.ds(other, width)] = (
            gate_in[first + slot * rows : first + (slot + 1) * rows, :].astype(F32) + other_part[slot]
        ).astype(BF16)
    dq[:, pl.ds(own, width)] = all_dq[pl.ds(pl.multiple_of(core * rows, rows), rows), :]
    dq[:, pl.ds(other, width)] = gate_in[first + 2 * rows : first + 3 * rows, :]
    dgate[:, pl.ds(own, width)] = gate_keep[...]
    dgate[:, pl.ds(other, width)] = gate_in[0:rows, :]
    dres[:, pl.ds(own, width)] = res_keep[...]
    dres[:, pl.ds(other, width)] = gate_in[rows : rows + poles, :].astype(F32) + gate_in[
        rows + poles : rows + 2 * poles, :
    ].astype(F32)


def chip_shift(array, by, crossed):
    members = lax.axis_size("ctx")
    pairs = []
    for source in range(members):
        chip, core = source // 2, source % 2
        target = ((chip + by) % (members // 2)) * 2 + ((1 - core) if crossed else core)
        pairs.append((source, target))
    return lax.ppermute(array, "ctx", pairs)


def chip_exchange(slots):
    members = lax.axis_size("ctx")
    groups = [list(range(core, members, 2)) for core in range(2)]
    return lax.all_to_all(slots, "ctx", 0, 0, axis_index_groups=groups)


def local(queries, key_rows, value_rows, gate_values, cotangent, decay_rates, residues, skip_gain):
    rows, channels = queries.shape
    width = channels // 2
    poles = decay_rates.shape[0]
    chips = lax.axis_size("ctx") // 2
    tokens = 2 * rows
    skip = skip_gain.reshape(1, channels)
    groups = width // LANES
    pair = (2, rows, width)
    split = (groups, tokens, LANES)
    states = (poles, SUBS, width)
    span = (WIN + 2) * rows
    keep_kv, keep_rest, give_all, params = call(
        pack_body,
        [
            (pair, BF16, True),
            ((3, rows, width), BF16, True),
            ((5, rows, width), BF16, True),
            ((2 * poles + 1, width), F32, True),
        ],
        scratch=[
            pltpu.VMEM((5, rows, channels), BF16),
            pltpu.VMEM((2 * poles + SUBS, channels), F32),
            pltpu.SemaphoreType.DMA((8,)),
        ],
        far=tuple(range(8)),
        name="pack",
    )(key_rows, value_rows, queries, gate_values, cotangent, decay_rates, residues, skip)
    given = chip_shift(give_all, 0, True)
    (chip_kv,) = call(merge_body, [((2, tokens, width), BF16, True)], near=(0, 1), name="chip_kv")(
        keep_kv, given
    )
    far_kv = chip_shift(chip_kv, 2, False)
    near_kv = chip_shift(chip_kv, 1, False)
    delta, totals, head_slots = call(
        head_body,
        [(split, F32, True), (states, F32, True), ((chips, poles, width), BF16, True)],
        scratch=[pltpu.VMEM((poles, width), F32)],
        near=(0, 1, 2),
        name="head_states",
    )(keep_rest, given, params)
    head_in = chip_exchange(head_slots)
    halo = (keep_rest, chip_kv, given, near_kv, far_kv)
    halo_buffers = [
        pltpu.VMEM((tokens, width), BF16),
        pltpu.VMEM((span, width), BF16),
        pltpu.VMEM((span, width), BF16),
    ]
    stats, attended = call(
        forward_body,
        [((groups, 2, SUBS, rows), F32, True), (split, F32, True)],
        scratch=halo_buffers,
        near=tuple(range(5)),
        cost=EARLY,
        name="forward",
    )(*halo)
    tail_totals, tail_slots = call(
        tail_body,
        [(states, F32, True), ((chips, 2 * poles, width), BF16, True)],
        scratch=[pltpu.VMEM((poles, width), F32), pltpu.VMEM((poles, width), F32)],
        near=(0, 1, 2, 3),
        name="tail",
    )(attended, delta, totals, params)
    tail_in = chip_exchange(tail_slots)
    dq, dkv_chip, out_far, out_same1, out_cross1, incoming_all = call(
        backward_body,
        [
            ((tokens, width), BF16, True),
            ((2, tokens, width), F32, True),
            ((2, tokens, width), BF16, True),
            (pair, BF16, True),
            (pair, BF16, True),
            ((chips, poles, width), F32, True),
        ],
        scratch=halo_buffers
        + [
            pltpu.VMEM(split, BF16),
            pltpu.VMEM(split, F32),
            pltpu.VMEM((span, width), F32),
            pltpu.VMEM((span, width), F32),
        ],
        near=tuple(range(11)),
        name="backward",
    )(*halo, stats, tail_totals, delta, totals, head_in, params)
    back_far = chip_shift(out_far, -2, False)
    back_same1 = chip_shift(out_same1, -1, False)
    back_cross1 = chip_shift(out_cross1, -1, True)
    own_total, partner = call(
        far_body,
        [(pair, F32, True), ((3, rows, width), BF16, True)],
        near=(0, 1, 2),
        cost=EARLY,
        name="far_sum",
    )(dkv_chip, back_far, dq)
    own_part, other_part = call(
        near_body,
        [(pair, BF16, True), (pair, F32, True)],
        near=(0, 1, 2),
        cost=EARLY,
        name="near_sum",
    )(own_total, back_same1, back_cross1)
    gate_keep, gate_give, res_keep = call(
        gate_body,
        [
            ((rows, width), BF16, True),
            ((4 * rows + 2 * poles, width), BF16, True),
            ((poles, width), F32, True),
        ],
        scratch=[pltpu.VMEM(split, F32), pltpu.VMEM((chips, poles, width), F32)],
        near=tuple(range(8)),
        name="gate",
    )(keep_rest, given, attended, tail_totals, tail_in, incoming_all, params, partner)
    gate_in = chip_shift(gate_give, 0, True)
    full = (rows, channels)
    wide = (full, BF16, False)
    return tuple(
        call(
            final_body,
            [wide, wide, wide, wide, ((poles, channels), F32, False)],
            near=tuple(range(6)),
            name="final",
        )(dq, own_part, other_part, gate_keep, gate_in, res_keep)
    )


def solution(mesh):
    wide = P(("dp", "ctx"), "head")
    in_specs = (wide, wide, wide, wide, wide, P(None, "head"), P(None, "head"), P("head"))
    out_specs = (wide, wide, wide, wide, P("dp", "head"))
    return jax.shard_map(local, mesh=mesh, in_specs=in_specs, out_specs=out_specs, check_vma=False)
```

```python
import math

import jax
import jax.numpy as jnp
from jax import lax
from jax.experimental import pallas as pl
from jax.experimental.pallas import tpu as pltpu
from jax.sharding import PartitionSpec as P

HEAD = 128
WIN = 4
LANES = 128
SUBS = 8
GROUP = 8
EARLY = pl.CostEstimate(flops=10**11, transcendentals=0, bytes_accessed=10**8)
F32 = jnp.float32
BF16 = jnp.bfloat16
OVER_KEYS = (((0,), (0,)), ((), ()))
OVER_HEAD = (((1,), (1,)), ((), ()))


def call(body, outs, scratch=(), near=(), far=(), cost=None, name=None):
    def run(*args):
        args = list(args)
        specs = []
        for n in range(len(args)):
            space = pltpu.HBM if n in far else pltpu.VMEM
            specs.append(pl.BlockSpec(memory_space=space))
            if n in near or n in far:
                args[n] = pltpu.with_memory_space_constraint(args[n], space)
        return pl.pallas_call(
            body,
            out_shape=[
                pltpu.VMEM(s, d) if local_out else jax.ShapeDtypeStruct(s, d) for s, d, local_out in outs
            ],
            in_specs=specs,
            out_specs=[pl.BlockSpec(memory_space=pltpu.VMEM)] * len(outs),
            scratch_shapes=list(scratch),
            compiler_params=pltpu.CompilerParams(vmem_limit_bytes=8 * 1024 * 1024),
            cost_estimate=cost,
            name=name,
        )(*args)

    return run


def place():
    index = lax.axis_index("ctx")
    return lax.rem(index, 2), lax.div(index, 2)


def halves(core, width):
    own = pl.multiple_of(core * width, LANES)
    other = pl.multiple_of((1 - core) * width, LANES)
    return own, other


def pack_body(
    k, v, q, gate, cot, rates, residues, skip, keep_kv, keep_rest, give_all, params, buf, small, sems
):
    width = k.shape[1] // 2
    poles = rates.shape[0]
    own, other = halves(place()[0], width)
    arrays = (k, v, q, gate, cot)
    copies = [pltpu.make_async_copy(a, buf.at[n], sems.at[n]) for n, a in enumerate(arrays)]
    for n, (array, first, count) in enumerate(
        ((rates, 0, poles), (residues, poles, poles), (skip, 2 * poles, 1))
    ):
        copies.append(
            pltpu.make_async_copy(array, small.at[pl.ds(first, count)], sems.at[len(arrays) + n])
        )
    for copy in copies:
        copy.start()
    for n in range(len(arrays)):
        copies[n].wait()
        keep = buf[n, :, pl.ds(own, width)]
        give_all[n] = buf[n, :, pl.ds(other, width)]
        if n < 2:
            keep_kv[n] = keep
        else:
            keep_rest[n - 2] = keep
    for copy in copies[len(arrays) :]:
        copy.wait()
    params[...] = small[0 : 2 * poles + 1, pl.ds(own, width)]


def rows3(values):
    return jnp.broadcast_to(values[:, None, :], (values.shape[0], SUBS, values.shape[1]))


def each_group(poles, width, body):
    pole_groups = poles // GROUP
    lane_groups = width // LANES

    def step(index, carry):
        lane_group = index // pole_groups
        first_lane = pl.multiple_of(lane_group * LANES, LANES)
        first_pole = pl.multiple_of((index % pole_groups) * GROUP, GROUP)
        body(first_pole, lane_group, first_lane)
        return carry

    lax.fori_loop(0, pole_groups * lane_groups, step, 0)


def head_body(keep_rest, given, params, delta, totals, slots, head_ref):
    rows, width = keep_rest.shape[1:]
    poles = totals.shape[0]
    chips = slots.shape[0]
    core, chip = place()
    own, other = halves(core, width)
    tokens = delta.shape[1]
    steps = tokens // SUBS
    mine = pl.multiple_of(core * rows, rows)
    theirs = pl.multiple_of((1 - core) * rows, rows)
    for lane_group in range(width // LANES):
        lanes = slice(lane_group * LANES, (lane_group + 1) * LANES)
        delta[lane_group, pl.ds(mine, rows), :] = keep_rest[1, :, lanes].astype(F32) * keep_rest[
            2, :, lanes
        ].astype(F32)
        delta[lane_group, pl.ds(theirs, rows), :] = given[3, :, lanes].astype(F32) * given[
            4, :, lanes
        ].astype(F32)

    def group(first_pole, lane_group, first_lane):
        rate = params[pl.ds(first_pole, GROUP), pl.ds(first_lane, LANES)]
        lam = rows3(jnp.exp(-rate))
        state = jnp.zeros((GROUP, SUBS, LANES), F32)
        for j in reversed(range(steps)):
            state = lam * state + delta[lane_group, pl.ds(j, SUBS, stride=steps), :][None]
        totals[pl.ds(first_pole, GROUP), :, pl.ds(first_lane, LANES)] = state
        block = lax.broadcasted_iota(jnp.int32, (GROUP, SUBS, LANES), 1).astype(F32)
        power = jnp.exp(-rows3(rate) * (block * steps))
        head_ref[pl.ds(first_pole, GROUP), pl.ds(first_lane, LANES)] = jnp.sum(power * state, axis=1)

    each_group(poles, width, group)
    head = head_ref[...].astype(BF16)
    for j in range(chips):
        slots[j] = head


def around(own, rate, tokens, order, out):
    decay = jnp.exp(-rate * tokens)
    value = own(order[-1])
    power = decay
    for n in reversed(order[:-1]):
        value = value + power * own(n)
        power = power * decay
    value = value / (1.0 - jnp.exp(-rate * (tokens * len(order))))
    for n in order:
        out[n] = value
        value = own(n) + decay * value


def block_ids(shape):
    return lax.broadcasted_iota(jnp.int32, shape, 1)


def entering_later(totals, incoming, lam_block):
    ids = block_ids(totals.shape)
    value = jnp.where(ids == SUBS - 1, rows3(incoming), pltpu.roll(totals, SUBS - 1, 1))
    power = lam_block
    for shift in (1, 2, 4):
        moved = pltpu.roll(value, SUBS - shift, 1)
        value = value + jnp.where(ids < SUBS - shift, power * moved, 0.0)
        power = power * power
    return value


def entering_earlier(totals, arriving, lam_block):
    ids = block_ids(totals.shape)
    value = jnp.where(ids == 0, rows3(arriving), pltpu.roll(totals, 1, 1))
    power = lam_block
    for shift in (1, 2, 4):
        moved = pltpu.roll(value, shift, 1)
        value = value + jnp.where(ids >= shift, power * moved, 0.0)
        power = power * power
    return value


def pole_weights(rate):
    tangent = jnp.tanh(rate)
    return jnp.sqrt(2.0 * tangent / (1.0 + tangent))


def merge_body(keep_kv, given, chip_kv):
    rows = keep_kv.shape[1]
    core, chip = place()
    for slot in range(2):
        chip_kv[slot, pl.ds(pl.multiple_of(core * rows, rows), rows), :] = keep_kv[slot]
        chip_kv[slot, pl.ds(pl.multiple_of((1 - core) * rows, rows), rows), :] = given[slot]


def assemble(core, keep_rest, chip_kv, given, near_kv, far_kv, qbuf, kbuf, vbuf):
    rows = keep_rest.shape[1]
    tokens = 2 * rows
    mine = pl.multiple_of(core * rows, rows)
    theirs = pl.multiple_of((1 - core) * rows, rows)
    qbuf[pl.ds(mine, rows), :] = keep_rest[0]
    qbuf[pl.ds(theirs, rows), :] = given[2]
    for slot, buf in ((0, kbuf), (1, vbuf)):
        buf[0:tokens, :] = far_kv[slot]
        buf[tokens : 2 * tokens, :] = near_kv[slot]
        buf[2 * tokens : 3 * tokens, :] = chip_kv[slot]


def allowed_pairs(rows):
    span = (WIN + 1) * rows
    key_ids = lax.broadcasted_iota(jnp.int32, (span, rows), 0)
    row_ids = lax.broadcasted_iota(jnp.int32, (span, rows), 1)
    return (key_ids > row_ids) & (key_ids <= row_ids + WIN * rows)


def forward_body(
    keep_rest, chip_kv, given, near_kv, far_kv, stats, attended, qbuf, kbuf, vbuf
):
    rows, width = keep_rest.shape[1:]
    tokens = 2 * rows
    core, chip = place()
    scale = 1.0 / math.sqrt(HEAD)
    assemble(core, keep_rest, chip_kv, given, near_kv, far_kv, qbuf, kbuf, vbuf)
    span = (WIN + 1) * rows
    allowed = allowed_pairs(rows)
    for head in range(width // HEAD):
        at_head = slice(head * HEAD, (head + 1) * HEAD)
        for block in range(tokens // rows):
            at_rows = slice(block * rows, (block + 1) * rows)
            at_keys = slice(block * rows, block * rows + span)
            scores = (
                lax.dot_general(
                    kbuf[at_keys, at_head], qbuf[at_rows, at_head], OVER_HEAD, preferred_element_type=F32
                )
                * scale
            )
            scores = jnp.where(allowed, scores, -jnp.inf)
            top = jnp.max(scores, axis=0, keepdims=True)
            raised = jnp.exp(scores - top)
            share = 1.0 / jnp.sum(raised, axis=0, keepdims=True)
            probability = raised * share
            stats[head, block, 0:1, :] = top
            stats[head, block, 1:2, :] = share
            attended[head, at_rows, :] = (
                lax.dot_general(
                    probability.astype(BF16), vbuf[at_keys, at_head], OVER_KEYS, preferred_element_type=F32
                )
                .astype(BF16)
                .astype(F32)
            )


def tail_body(attended, delta, totals, params, tail_totals, slots, tail_ref, part_ref):
    poles, _, width = totals.shape
    steps = delta.shape[1] // SUBS
    chips = slots.shape[0]

    def tail_group(first_pole, lane_group, first_lane):
        rate = params[pl.ds(first_pole, GROUP), pl.ds(first_lane, LANES)]
        pole_at = pl.ds(first_pole, GROUP)
        lane_at = pl.ds(first_lane, LANES)
        lam = rows3(jnp.exp(-rate))
        state = jnp.zeros((GROUP, SUBS, LANES), F32)
        matched = jnp.zeros((GROUP, SUBS, LANES), F32)
        for j in range(steps):
            at = pl.ds(j, SUBS, stride=steps)
            state = lam * state + attended[lane_group, at, :][None]
            matched = matched + delta[lane_group, at, :][None] * state
        tail_totals[pole_at, :, lane_at] = state
        lam_block = rows3(jnp.exp(-rate * steps))
        entering = entering_earlier(state, jnp.zeros((GROUP, LANES), F32), lam_block)
        full = state + lam_block * entering
        matched = matched + lam * totals[pole_at, :, lane_at] * entering
        tail_ref[pole_at, lane_at] = full[:, SUBS - 1, :]
        part_ref[pole_at, lane_at] = jnp.sum(matched, axis=1)

    each_group(poles, width, tail_group)
    tail = tail_ref[...].astype(BF16)
    part = part_ref[...].astype(BF16)
    for j in range(chips):
        slots[j, 0:poles, :] = tail
        slots[j, poles : 2 * poles, :] = part


def backward_body(
    keep_rest,
    chip_kv,
    given,
    near_kv,
    far_kv,
    stats,
    tail_totals,
    delta,
    totals,
    slots_in,
    params,
    dq,
    dkv_chip,
    out_far,
    out_near,
    incoming_all,
    qbuf,
    kbuf,
    vbuf,
    adj16,
    adj32,
    dk_acc,
    dv_acc,
):
    tokens, width = qbuf.shape
    rows = tokens // 2
    poles = totals.shape[0]
    steps = tokens // SUBS
    chips = slots_in.shape[0]
    core, chip = place()
    mine = pl.multiple_of(core * rows, rows)
    theirs = pl.multiple_of((1 - core) * rows, rows)
    scale = 1.0 / math.sqrt(HEAD)
    assemble(core, keep_rest, chip_kv, given, near_kv, far_kv, qbuf, kbuf, vbuf)

    around(
        lambda n: slots_in[n].astype(F32),
        params[0:poles, :],
        tokens,
        list(reversed(range(chips))),
        incoming_all,
    )
    for lane_group in range(width // LANES):
        gain = params[2 * poles : 2 * poles + 1, lane_group * LANES : (lane_group + 1) * LANES]
        adj32[lane_group] = gain * delta[lane_group]

    def adjoint_group(first_pole, lane_group, first_lane):
        rate = params[pl.ds(first_pole, GROUP), pl.ds(first_lane, LANES)]
        lam = rows3(jnp.exp(-rate))
        mixing = rows3(
            params[pl.ds(poles + first_pole, GROUP), pl.ds(first_lane, LANES)] * pole_weights(rate)
        )
        lane_at = pl.ds(first_lane, LANES)
        state = entering_later(
            totals[pl.ds(first_pole, GROUP), :, lane_at],
            incoming_all[chip, pl.ds(first_pole, GROUP), lane_at],
            rows3(jnp.exp(-rate * steps)),
        )
        for j in reversed(range(steps)):
            at = pl.ds(j, SUBS, stride=steps)
            state = lam * state + delta[lane_group, at, :][None]
            adj32[lane_group, at, :] = adj32[lane_group, at, :] + jnp.sum(mixing * state, axis=0)

    each_group(poles, width, adjoint_group)
    adj16[...] = adj32[...].astype(BF16)

    span = (WIN + 1) * rows
    allowed = allowed_pairs(rows)
    for head in range(width // HEAD):
        at_head = slice(head * HEAD, (head + 1) * HEAD)
        for block in range(tokens // rows):
            at_rows = slice(block * rows, (block + 1) * rows)
            at_keys = slice(block * rows, block * rows + span)
            query = qbuf[at_rows, at_head]
            key = kbuf[at_keys, at_head]
            value = vbuf[at_keys, at_head]
            adjoint = adj16[head, at_rows, :]
            scores = lax.dot_general(key, query, OVER_HEAD, preferred_element_type=F32) * scale
            scores = jnp.where(allowed, scores, -jnp.inf)
            probability = jnp.exp(scores - stats[head, block, 0:1, :]) * stats[head, block, 1:2, :]
            rounded = probability.astype(BF16)
            weight = lax.dot_general(value, adjoint, OVER_HEAD, preferred_element_type=F32)
            inner = jnp.sum(probability * weight, axis=0, keepdims=True)
            score_adjoint = (probability * (weight - inner) * scale).astype(BF16)
            dq[at_rows, at_head] = lax.dot_general(
                score_adjoint, key, OVER_KEYS, preferred_element_type=F32
            ).astype(BF16)
            dk = jnp.dot(score_adjoint, query, preferred_element_type=F32)
            dv = jnp.dot(rounded, adjoint, preferred_element_type=F32)
            if block == 0:
                dk_acc[at_keys, at_head] = dk
                dv_acc[at_keys, at_head] = dv
            else:
                edge = span - rows
                first = slice(block * rows, block * rows + edge)
                last = slice(block * rows + edge, block * rows + span)
                dk_acc[first, at_head] = dk_acc[first, at_head] + dk[:edge]
                dv_acc[first, at_head] = dv_acc[first, at_head] + dv[:edge]
                dk_acc[last, at_head] = dk[edge:]
                dv_acc[last, at_head] = dv[edge:]

    for slot, acc in ((0, dk_acc), (1, dv_acc)):
        out_far[slot] = acc[0:tokens, :].astype(BF16)
        out_near[slot] = acc[tokens : 2 * tokens, :].astype(BF16)
        dkv_chip[slot] = acc[2 * tokens : 3 * tokens, :]


def sum_body(dkv_chip, far, near, dq, own_part, give):
    rows = own_part.shape[1]
    core, chip = place()
    mine = pl.ds(pl.multiple_of(core * rows, rows), rows)
    theirs = pl.ds(pl.multiple_of((1 - core) * rows, rows), rows)
    for at, out in ((mine, own_part), (theirs, give)):
        for slot in range(2):
            out[slot] = (
                dkv_chip[slot, at, :] + near[slot, at, :].astype(F32) + far[slot, at, :].astype(F32)
            ).astype(BF16)
    give[2] = dq[theirs, :]


def gate_body(
    keep_rest,
    given,
    attended,
    tail_totals,
    slots_in,
    incoming_all,
    params,
    partner,
    gate_keep,
    gate_give,
    res_keep,
    mix32,
    arriving_ref,
):
    core, chip = place()
    rows, width = keep_rest.shape[1:]
    poles = tail_totals.shape[0]
    tokens = attended.shape[1]
    steps = tokens // SUBS
    chips = slots_in.shape[0]
    mine = pl.multiple_of(core * rows, rows)
    theirs = pl.multiple_of((1 - core) * rows, rows)
    rate = params[0:poles, :]
    around(
        lambda n: slots_in[n, 0:poles, :].astype(F32), rate, tokens, list(range(chips)), arriving_ref
    )
    parts = slots_in[0, poles : 2 * poles, :].astype(F32)
    crossed = slots_in[0, 0:poles, :].astype(F32) * incoming_all[0]
    for n in range(1, chips):
        parts = parts + slots_in[n, poles : 2 * poles, :].astype(F32)
        crossed = crossed + slots_in[n, 0:poles, :].astype(F32) * incoming_all[n]
    total = pole_weights(rate) * (parts + jnp.exp(-rate) * crossed)
    res_keep[...] = total
    high = total.astype(BF16)
    gate_give[rows : rows + poles, :] = high
    gate_give[rows + poles : rows + 2 * poles, :] = (total - high.astype(F32)).astype(BF16)
    first = rows + 2 * poles
    for slot in range(3):
        gate_give[first + slot * rows : first + (slot + 1) * rows, :] = partner[slot]
    for lane_group in range(width // LANES):
        gain = params[2 * poles : 2 * poles + 1, lane_group * LANES : (lane_group + 1) * LANES]
        mix32[lane_group] = gain * attended[lane_group]

    def group(first_pole, lane_group, first_lane):
        rate = params[pl.ds(first_pole, GROUP), pl.ds(first_lane, LANES)]
        lam = rows3(jnp.exp(-rate))
        mixing = rows3(
            params[pl.ds(poles + first_pole, GROUP), pl.ds(first_lane, LANES)] * pole_weights(rate)
        )
        lane_at = pl.ds(first_lane, LANES)
        pole_at = pl.ds(first_pole, GROUP)
        state = entering_earlier(
            tail_totals[pole_at, :, lane_at],
            arriving_ref[chip, pole_at, lane_at],
            rows3(jnp.exp(-rate * steps)),
        )
        for j in range(steps):
            at = pl.ds(j, SUBS, stride=steps)
            state = lam * state + attended[lane_group, at, :][None]
            mix32[lane_group, at, :] = mix32[lane_group, at, :] + jnp.sum(mixing * state, axis=0)

    each_group(poles, width, group)
    for lane_group in range(width // LANES):
        lanes = slice(lane_group * LANES, (lane_group + 1) * LANES)
        gate_keep[:, lanes] = (
            keep_rest[2, :, lanes].astype(F32) * mix32[lane_group, pl.ds(mine, rows), :]
        ).astype(BF16)
        gate_give[0:rows, lanes] = (
            given[4, :, lanes].astype(F32) * mix32[lane_group, pl.ds(theirs, rows), :]
        ).astype(BF16)


def final_body(all_dq, own_part, gate_keep, gate_in, res_keep, dq, dk, dv, dgate, dres):
    rows, width = gate_keep.shape
    poles = res_keep.shape[0]
    core, chip = place()
    own, other = halves(core, width)
    first = rows + 2 * poles
    for slot, out in ((0, dk), (1, dv)):
        out[:, pl.ds(own, width)] = own_part[slot]
        out[:, pl.ds(other, width)] = gate_in[first + slot * rows : first + (slot + 1) * rows, :]
    dq[:, pl.ds(own, width)] = all_dq[pl.ds(pl.multiple_of(core * rows, rows), rows), :]
    dq[:, pl.ds(other, width)] = gate_in[first + 2 * rows : first + 3 * rows, :]
    dgate[:, pl.ds(own, width)] = gate_keep[...]
    dgate[:, pl.ds(other, width)] = gate_in[0:rows, :]
    dres[:, pl.ds(own, width)] = res_keep[...]
    dres[:, pl.ds(other, width)] = gate_in[rows : rows + poles, :].astype(F32) + gate_in[
        rows + poles : rows + 2 * poles, :
    ].astype(F32)


def chip_shift(array, by, crossed):
    members = lax.axis_size("ctx")
    pairs = []
    for source in range(members):
        chip, core = source // 2, source % 2
        target = ((chip + by) % (members // 2)) * 2 + ((1 - core) if crossed else core)
        pairs.append((source, target))
    return lax.ppermute(array, "ctx", pairs)


def chip_exchange(slots):
    members = lax.axis_size("ctx")
    groups = [list(range(core, members, 2)) for core in range(2)]
    return lax.all_to_all(slots, "ctx", 0, 0, axis_index_groups=groups)


def local(queries, key_rows, value_rows, gate_values, cotangent, decay_rates, residues, skip_gain):
    rows, channels = queries.shape
    width = channels // 2
    poles = decay_rates.shape[0]
    chips = lax.axis_size("ctx") // 2
    tokens = 2 * rows
    skip = skip_gain.reshape(1, channels)
    groups = width // LANES
    pair = (2, rows, width)
    split = (groups, tokens, LANES)
    states = (poles, SUBS, width)
    span = (WIN + 2) * rows
    keep_kv, keep_rest, give_all, params = call(
        pack_body,
        [
            (pair, BF16, True),
            ((3, rows, width), BF16, True),
            ((5, rows, width), BF16, True),
            ((2 * poles + 1, width), F32, True),
        ],
        scratch=[
            pltpu.VMEM((5, rows, channels), BF16),
            pltpu.VMEM((2 * poles + SUBS, channels), F32),
            pltpu.SemaphoreType.DMA((8,)),
        ],
        far=tuple(range(8)),
        name="pack",
    )(key_rows, value_rows, queries, gate_values, cotangent, decay_rates, residues, skip)
    given = chip_shift(give_all, 0, True)
    (chip_kv,) = call(merge_body, [((2, tokens, width), BF16, True)], near=(0, 1), name="chip_kv")(
        keep_kv, given
    )
    far_kv = chip_shift(chip_kv, 2, False)
    near_kv = chip_shift(chip_kv, 1, False)
    delta, totals, head_slots = call(
        head_body,
        [(split, F32, True), (states, F32, True), ((chips, poles, width), BF16, True)],
        scratch=[pltpu.VMEM((poles, width), F32)],
        near=(0, 1, 2),
        name="head_states",
    )(keep_rest, given, params)
    head_in = chip_exchange(head_slots)
    halo = (keep_rest, chip_kv, given, near_kv, far_kv)
    halo_buffers = [
        pltpu.VMEM((tokens, width), BF16),
        pltpu.VMEM((span, width), BF16),
        pltpu.VMEM((span, width), BF16),
    ]
    stats, attended = call(
        forward_body,
        [((groups, 2, SUBS, rows), F32, True), (split, F32, True)],
        scratch=halo_buffers,
        near=tuple(range(5)),
        cost=EARLY,
        name="forward",
    )(*halo)
    tail_totals, tail_slots = call(
        tail_body,
        [(states, F32, True), ((chips, 2 * poles, width), BF16, True)],
        scratch=[pltpu.VMEM((poles, width), F32), pltpu.VMEM((poles, width), F32)],
        near=(0, 1, 2, 3),
        name="tail",
    )(attended, delta, totals, params)
    tail_in = chip_exchange(tail_slots)
    dq, dkv_chip, out_far, out_near, incoming_all = call(
        backward_body,
        [
            ((tokens, width), BF16, True),
            ((2, tokens, width), F32, True),
            ((2, tokens, width), BF16, True),
            ((2, tokens, width), BF16, True),
            ((chips, poles, width), F32, True),
        ],
        scratch=halo_buffers
        + [
            pltpu.VMEM(split, BF16),
            pltpu.VMEM(split, F32),
            pltpu.VMEM((span, width), F32),
            pltpu.VMEM((span, width), F32),
        ],
        near=tuple(range(11)),
        name="backward",
    )(*halo, stats, tail_totals, delta, totals, head_in, params)
    back_far = chip_shift(out_far, -2, False)
    back_near = chip_shift(out_near, -1, False)
    own_part, partner = call(
        sum_body,
        [(pair, BF16, True), ((3, rows, width), BF16, True)],
        near=(0, 1, 2, 3),
        cost=EARLY,
        name="block_sums",
    )(dkv_chip, back_far, back_near, dq)
    gate_keep, gate_give, res_keep = call(
        gate_body,
        [
            ((rows, width), BF16, True),
            ((4 * rows + 2 * poles, width), BF16, True),
            ((poles, width), F32, True),
        ],
        scratch=[pltpu.VMEM(split, F32), pltpu.VMEM((chips, poles, width), F32)],
        near=tuple(range(8)),
        name="gate",
    )(keep_rest, given, attended, tail_totals, tail_in, incoming_all, params, partner)
    gate_in = chip_shift(gate_give, 0, True)
    full = (rows, channels)
    wide = (full, BF16, False)
    return tuple(
        call(
            final_body,
            [wide, wide, wide, wide, ((poles, channels), F32, False)],
            near=tuple(range(5)),
            name="final",
        )(dq, own_part, gate_keep, gate_in, res_keep)
    )


def solution(mesh):
    wide = P(("dp", "ctx"), "head")
    in_specs = (wide, wide, wide, wide, wide, P(None, "head"), P(None, "head"), P("head"))
    out_specs = (wide, wide, wide, wide, P("dp", "head"))
    return jax.shard_map(local, mesh=mesh, in_specs=in_specs, out_specs=out_specs, check_vma=False)
```

```python
import math

import jax
import jax.numpy as jnp
from jax import lax
from jax.experimental import pallas as pl
from jax.experimental.pallas import tpu as pltpu
from jax.sharding import PartitionSpec as P

HEAD = 128
WIN = 4
LANES = 128
SUBS = 8
GROUP = 8
EARLY = pl.CostEstimate(flops=10**11, transcendentals=0, bytes_accessed=10**8)
F32 = jnp.float32
BF16 = jnp.bfloat16
OVER_KEYS = (((0,), (0,)), ((), ()))
OVER_HEAD = (((1,), (1,)), ((), ()))


def call(body, outs, scratch=(), near=(), far=(), cost=None, name=None):
    def run(*args):
        args = list(args)
        specs = []
        for n in range(len(args)):
            space = pltpu.HBM if n in far else pltpu.VMEM
            specs.append(pl.BlockSpec(memory_space=space))
            if n in near or n in far:
                args[n] = pltpu.with_memory_space_constraint(args[n], space)
        return pl.pallas_call(
            body,
            out_shape=[
                pltpu.VMEM(s, d) if local_out else jax.ShapeDtypeStruct(s, d) for s, d, local_out in outs
            ],
            in_specs=specs,
            out_specs=[pl.BlockSpec(memory_space=pltpu.VMEM)] * len(outs),
            scratch_shapes=list(scratch),
            compiler_params=pltpu.CompilerParams(vmem_limit_bytes=8 * 1024 * 1024),
            cost_estimate=cost,
            name=name,
        )(*args)

    return run


def place():
    index = lax.axis_index("ctx")
    return lax.rem(index, 2), lax.div(index, 2)


def halves(core, width):
    own = pl.multiple_of(core * width, LANES)
    other = pl.multiple_of((1 - core) * width, LANES)
    return own, other


def pack_body(
    k, v, q, gate, cot, rates, residues, skip, keep_kv, keep_rest, give_all, params, buf, small, sems
):
    width = k.shape[1] // 2
    poles = rates.shape[0]
    own, other = halves(place()[0], width)
    arrays = (k, v, q, gate, cot)
    copies = [pltpu.make_async_copy(a, buf.at[n], sems.at[n]) for n, a in enumerate(arrays)]
    for n, (array, first, count) in enumerate(
        ((rates, 0, poles), (residues, poles, poles), (skip, 2 * poles, 1))
    ):
        copies.append(
            pltpu.make_async_copy(array, small.at[pl.ds(first, count)], sems.at[len(arrays) + n])
        )
    for copy in copies:
        copy.start()
    for n in range(len(arrays)):
        copies[n].wait()
        keep = buf[n, :, pl.ds(own, width)]
        give_all[n] = buf[n, :, pl.ds(other, width)]
        if n < 2:
            keep_kv[n] = keep
        else:
            keep_rest[n - 2] = keep
    for copy in copies[len(arrays) :]:
        copy.wait()
    params[...] = small[0 : 2 * poles + 1, pl.ds(own, width)]


def rows3(values):
    return jnp.broadcast_to(values[:, None, :], (values.shape[0], SUBS, values.shape[1]))


def each_group(poles, width, body):
    pole_groups = poles // GROUP
    lane_groups = width // LANES

    def step(index, carry):
        lane_group = index // pole_groups
        first_lane = pl.multiple_of(lane_group * LANES, LANES)
        first_pole = pl.multiple_of((index % pole_groups) * GROUP, GROUP)
        body(first_pole, lane_group, first_lane)
        return carry

    lax.fori_loop(0, pole_groups * lane_groups, step, 0)


def head_body(keep_rest, given, params, delta, totals, slots, head_ref):
    rows, width = keep_rest.shape[1:]
    poles = totals.shape[0]
    chips = slots.shape[0]
    core, chip = place()
    own, other = halves(core, width)
    tokens = delta.shape[1]
    steps = tokens // SUBS
    mine = pl.multiple_of(core * rows, rows)
    theirs = pl.multiple_of((1 - core) * rows, rows)
    for lane_group in range(width // LANES):
        lanes = slice(lane_group * LANES, (lane_group + 1) * LANES)
        delta[lane_group, pl.ds(mine, rows), :] = keep_rest[1, :, lanes].astype(F32) * keep_rest[
            2, :, lanes
        ].astype(F32)
        delta[lane_group, pl.ds(theirs, rows), :] = given[3, :, lanes].astype(F32) * given[
            4, :, lanes
        ].astype(F32)

    def group(first_pole, lane_group, first_lane):
        rate = params[pl.ds(first_pole, GROUP), pl.ds(first_lane, LANES)]
        lam = rows3(jnp.exp(-rate))
        state = jnp.zeros((GROUP, SUBS, LANES), F32)
        for j in reversed(range(steps)):
            state = lam * state + delta[lane_group, pl.ds(j, SUBS, stride=steps), :][None]
        totals[pl.ds(first_pole, GROUP), :, pl.ds(first_lane, LANES)] = state
        block = lax.broadcasted_iota(jnp.int32, (GROUP, SUBS, LANES), 1).astype(F32)
        power = jnp.exp(-rows3(rate) * (block * steps))
        head_ref[pl.ds(first_pole, GROUP), pl.ds(first_lane, LANES)] = jnp.sum(power * state, axis=1)

    each_group(poles, width, group)
    head = head_ref[...].astype(BF16)
    for j in range(chips):
        slots[j] = head


def around(own, rate, tokens, order, out):
    decay = jnp.exp(-rate * tokens)
    value = own(order[-1])
    power = decay
    for n in reversed(order[:-1]):
        value = value + power * own(n)
        power = power * decay
    value = value / (1.0 - jnp.exp(-rate * (tokens * len(order))))
    for n in order:
        out[n] = value
        value = own(n) + decay * value


def block_ids(shape):
    return lax.broadcasted_iota(jnp.int32, shape, 1)


def entering_later(totals, incoming, lam_block):
    ids = block_ids(totals.shape)
    value = jnp.where(ids == SUBS - 1, rows3(incoming), pltpu.roll(totals, SUBS - 1, 1))
    power = lam_block
    for shift in (1, 2, 4):
        moved = pltpu.roll(value, SUBS - shift, 1)
        value = value + jnp.where(ids < SUBS - shift, power * moved, 0.0)
        power = power * power
    return value


def entering_earlier(totals, arriving, lam_block):
    ids = block_ids(totals.shape)
    value = jnp.where(ids == 0, rows3(arriving), pltpu.roll(totals, 1, 1))
    power = lam_block
    for shift in (1, 2, 4):
        moved = pltpu.roll(value, shift, 1)
        value = value + jnp.where(ids >= shift, power * moved, 0.0)
        power = power * power
    return value


def pole_weights(rate):
    tangent = jnp.tanh(rate)
    return jnp.sqrt(2.0 * tangent / (1.0 + tangent))


def merge_body(keep_kv, given, chip_kv):
    rows = keep_kv.shape[1]
    core, chip = place()
    for slot in range(2):
        chip_kv[slot, pl.ds(pl.multiple_of(core * rows, rows), rows), :] = keep_kv[slot]
        chip_kv[slot, pl.ds(pl.multiple_of((1 - core) * rows, rows), rows), :] = given[slot]


def assemble(core, keep_rest, chip_kv, given, near_kv, far_kv, qbuf, kbuf, vbuf):
    rows = keep_rest.shape[1]
    tokens = 2 * rows
    mine = pl.multiple_of(core * rows, rows)
    theirs = pl.multiple_of((1 - core) * rows, rows)
    qbuf[pl.ds(mine, rows), :] = keep_rest[0]
    qbuf[pl.ds(theirs, rows), :] = given[2]
    for slot, buf in ((0, kbuf), (1, vbuf)):
        buf[0:tokens, :] = far_kv[slot]
        buf[tokens : 2 * tokens, :] = near_kv[slot]
        buf[2 * tokens : 3 * tokens, :] = chip_kv[slot]


def allowed_pairs(rows):
    span = (WIN + 1) * rows
    key_ids = lax.broadcasted_iota(jnp.int32, (span, rows), 0)
    row_ids = lax.broadcasted_iota(jnp.int32, (span, rows), 1)
    return (key_ids > row_ids) & (key_ids <= row_ids + WIN * rows)


def forward_body(
    keep_rest, chip_kv, given, near_kv, far_kv, stats, attended, qbuf, kbuf, vbuf
):
    rows, width = keep_rest.shape[1:]
    tokens = 2 * rows
    core, chip = place()
    scale = 1.0 / math.sqrt(HEAD)
    assemble(core, keep_rest, chip_kv, given, near_kv, far_kv, qbuf, kbuf, vbuf)
    span = (WIN + 1) * rows
    allowed = allowed_pairs(rows)
    for head in range(width // HEAD):
        at_head = slice(head * HEAD, (head + 1) * HEAD)
        for block in range(tokens // rows):
            at_rows = slice(block * rows, (block + 1) * rows)
            at_keys = slice(block * rows, block * rows + span)
            scores = (
                lax.dot_general(
                    kbuf[at_keys, at_head], qbuf[at_rows, at_head], OVER_HEAD, preferred_element_type=F32
                )
                * scale
            )
            scores = jnp.where(allowed, scores, -jnp.inf)
            top = jnp.max(scores, axis=0, keepdims=True)
            raised = jnp.exp(scores - top)
            share = 1.0 / jnp.sum(raised, axis=0, keepdims=True)
            probability = raised * share
            stats[head, block, 0:1, :] = top
            stats[head, block, 1:2, :] = share
            attended[head, at_rows, :] = (
                lax.dot_general(
                    probability.astype(BF16), vbuf[at_keys, at_head], OVER_KEYS, preferred_element_type=F32
                )
                .astype(BF16)
                .astype(F32)
            )


def tail_body(attended, delta, totals, params, tail_totals, slots, tail_ref, part_ref):
    poles, _, width = totals.shape
    steps = delta.shape[1] // SUBS
    chips = slots.shape[0]

    def tail_group(first_pole, lane_group, first_lane):
        rate = params[pl.ds(first_pole, GROUP), pl.ds(first_lane, LANES)]
        pole_at = pl.ds(first_pole, GROUP)
        lane_at = pl.ds(first_lane, LANES)
        lam = rows3(jnp.exp(-rate))
        state = jnp.zeros((GROUP, SUBS, LANES), F32)
        matched = jnp.zeros((GROUP, SUBS, LANES), F32)
        for j in range(steps):
            at = pl.ds(j, SUBS, stride=steps)
            state = lam * state + attended[lane_group, at, :][None]
            matched = matched + delta[lane_group, at, :][None] * state
        tail_totals[pole_at, :, lane_at] = state
        lam_block = rows3(jnp.exp(-rate * steps))
        entering = entering_earlier(state, jnp.zeros((GROUP, LANES), F32), lam_block)
        full = state + lam_block * entering
        matched = matched + lam * totals[pole_at, :, lane_at] * entering
        tail_ref[pole_at, lane_at] = full[:, SUBS - 1, :]
        part_ref[pole_at, lane_at] = jnp.sum(matched, axis=1)

    each_group(poles, width, tail_group)
    tail = tail_ref[...].astype(BF16)
    part = part_ref[...].astype(BF16)
    for j in range(chips):
        slots[j, 0:poles, :] = tail
        slots[j, poles : 2 * poles, :] = part


def backward_body(
    keep_rest,
    chip_kv,
    given,
    near_kv,
    far_kv,
    stats,
    tail_totals,
    delta,
    totals,
    slots_in,
    params,
    dq,
    dkv_chip,
    out_far,
    out_same1,
    out_cross1,
    incoming_all,
    qbuf,
    kbuf,
    vbuf,
    adj16,
    adj32,
    dk_acc,
    dv_acc,
):
    tokens, width = qbuf.shape
    rows = tokens // 2
    poles = totals.shape[0]
    steps = tokens // SUBS
    chips = slots_in.shape[0]
    core, chip = place()
    mine = pl.multiple_of(core * rows, rows)
    theirs = pl.multiple_of((1 - core) * rows, rows)
    scale = 1.0 / math.sqrt(HEAD)
    assemble(core, keep_rest, chip_kv, given, near_kv, far_kv, qbuf, kbuf, vbuf)

    around(
        lambda n: slots_in[n].astype(F32),
        params[0:poles, :],
        tokens,
        list(reversed(range(chips))),
        incoming_all,
    )
    for lane_group in range(width // LANES):
        gain = params[2 * poles : 2 * poles + 1, lane_group * LANES : (lane_group + 1) * LANES]
        adj32[lane_group] = gain * delta[lane_group]

    def adjoint_group(first_pole, lane_group, first_lane):
        rate = params[pl.ds(first_pole, GROUP), pl.ds(first_lane, LANES)]
        lam = rows3(jnp.exp(-rate))
        mixing = rows3(
            params[pl.ds(poles + first_pole, GROUP), pl.ds(first_lane, LANES)] * pole_weights(rate)
        )
        lane_at = pl.ds(first_lane, LANES)
        state = entering_later(
            totals[pl.ds(first_pole, GROUP), :, lane_at],
            incoming_all[chip, pl.ds(first_pole, GROUP), lane_at],
            rows3(jnp.exp(-rate * steps)),
        )
        for j in reversed(range(steps)):
            at = pl.ds(j, SUBS, stride=steps)
            state = lam * state + delta[lane_group, at, :][None]
            adj32[lane_group, at, :] = adj32[lane_group, at, :] + jnp.sum(mixing * state, axis=0)

    each_group(poles, width, adjoint_group)
    adj16[...] = adj32[...].astype(BF16)

    span = (WIN + 1) * rows
    allowed = allowed_pairs(rows)
    for head in range(width // HEAD):
        at_head = slice(head * HEAD, (head + 1) * HEAD)
        for block in range(tokens // rows):
            at_rows = slice(block * rows, (block + 1) * rows)
            at_keys = slice(block * rows, block * rows + span)
            query = qbuf[at_rows, at_head]
            key = kbuf[at_keys, at_head]
            value = vbuf[at_keys, at_head]
            adjoint = adj16[head, at_rows, :]
            scores = lax.dot_general(key, query, OVER_HEAD, preferred_element_type=F32) * scale
            scores = jnp.where(allowed, scores, -jnp.inf)
            probability = jnp.exp(scores - stats[head, block, 0:1, :]) * stats[head, block, 1:2, :]
            rounded = probability.astype(BF16)
            weight = lax.dot_general(value, adjoint, OVER_HEAD, preferred_element_type=F32)
            inner = jnp.sum(probability * weight, axis=0, keepdims=True)
            score_adjoint = (probability * (weight - inner) * scale).astype(BF16)
            dq[at_rows, at_head] = lax.dot_general(
                score_adjoint, key, OVER_KEYS, preferred_element_type=F32
            ).astype(BF16)
            dk = jnp.dot(score_adjoint, query, preferred_element_type=F32)
            dv = jnp.dot(rounded, adjoint, preferred_element_type=F32)
            if block == 0:
                dk_acc[at_keys, at_head] = dk
                dv_acc[at_keys, at_head] = dv
            else:
                edge = span - rows
                first = slice(block * rows, block * rows + edge)
                last = slice(block * rows + edge, block * rows + span)
                dk_acc[first, at_head] = dk_acc[first, at_head] + dk[:edge]
                dv_acc[first, at_head] = dv_acc[first, at_head] + dv[:edge]
                dk_acc[last, at_head] = dk[edge:]
                dv_acc[last, at_head] = dv[edge:]

    for slot, acc in ((0, dk_acc), (1, dv_acc)):
        out_far[slot] = acc[0:tokens, :].astype(BF16)
        out_same1[slot] = acc[pl.ds(mine + tokens, rows), :].astype(BF16)
        out_cross1[slot] = acc[pl.ds(theirs + tokens, rows), :].astype(BF16)
        dkv_chip[slot] = acc[2 * tokens : 3 * tokens, :]


def far_body(dkv_chip, far, dq, own_total, give):
    rows = own_total.shape[1]
    core, chip = place()
    mine = pl.ds(pl.multiple_of(core * rows, rows), rows)
    theirs = pl.ds(pl.multiple_of((1 - core) * rows, rows), rows)
    for slot in range(2):
        own_total[slot] = dkv_chip[slot, mine, :] + far[slot, mine, :].astype(F32)
        give[slot] = (dkv_chip[slot, theirs, :] + far[slot, theirs, :].astype(F32)).astype(BF16)
    give[2] = dq[theirs, :]


def local_mix_body(attended, tail_totals, params, partner, mix):
    poles, _, width = tail_totals.shape
    steps = attended.shape[1] // SUBS
    for lane_group in range(width // LANES):
        gain = params[2 * poles : 2 * poles + 1, lane_group * LANES : (lane_group + 1) * LANES]
        mix[lane_group] = gain * attended[lane_group]

    def group(first_pole, lane_group, first_lane):
        rate = params[pl.ds(first_pole, GROUP), pl.ds(first_lane, LANES)]
        lam = rows3(jnp.exp(-rate))
        mixing = rows3(
            params[pl.ds(poles + first_pole, GROUP), pl.ds(first_lane, LANES)] * pole_weights(rate)
        )
        state = entering_earlier(
            tail_totals[pl.ds(first_pole, GROUP), :, pl.ds(first_lane, LANES)],
            jnp.zeros((GROUP, LANES), F32),
            rows3(jnp.exp(-rate * steps)),
        )
        for j in range(steps):
            at = pl.ds(j, SUBS, stride=steps)
            state = lam * state + attended[lane_group, at, :][None]
            mix[lane_group, at, :] = mix[lane_group, at, :] + jnp.sum(mixing * state, axis=0)

    each_group(poles, width, group)


def gate_body(
    keep_rest,
    given,
    local_mix,
    slots_in,
    incoming_all,
    params,
    partner,
    gate_keep,
    gate_give,
    res_keep,
    mix32,
    arriving_ref,
):
    core, chip = place()
    rows, width = keep_rest.shape[1:]
    chips, poles, _ = incoming_all.shape
    tokens = local_mix.shape[1]
    steps = tokens // SUBS
    mine = pl.multiple_of(core * rows, rows)
    theirs = pl.multiple_of((1 - core) * rows, rows)
    rate = params[0:poles, :]
    around(
        lambda n: slots_in[n, 0:poles, :].astype(F32), rate, tokens, list(range(chips)), arriving_ref
    )
    mix32[...] = local_mix[...]

    def group(first_pole, lane_group, first_lane):
        rate = params[pl.ds(first_pole, GROUP), pl.ds(first_lane, LANES)]
        lam = rows3(jnp.exp(-rate))
        mixing = params[pl.ds(poles + first_pole, GROUP), pl.ds(first_lane, LANES)] * pole_weights(rate)
        arriving = arriving_ref[chip, pl.ds(first_pole, GROUP), pl.ds(first_lane, LANES)]
        blocks = block_ids((GROUP, SUBS, LANES)).astype(F32)
        value = rows3(mixing * arriving) * jnp.exp(-rows3(rate) * (blocks * steps))
        for j in range(steps):
            at = pl.ds(j, SUBS, stride=steps)
            value = lam * value
            mix32[lane_group, at, :] = mix32[lane_group, at, :] + jnp.sum(value, axis=0)

    each_group(poles, width, group)
    for lane_group in range(width // LANES):
        lanes = slice(lane_group * LANES, (lane_group + 1) * LANES)
        gate_keep[:, lanes] = (
            keep_rest[2, :, lanes].astype(F32) * mix32[lane_group, pl.ds(mine, rows), :]
        ).astype(BF16)
        gate_give[0:rows, lanes] = (
            given[4, :, lanes].astype(F32) * mix32[lane_group, pl.ds(theirs, rows), :]
        ).astype(BF16)
    parts = slots_in[0, poles : 2 * poles, :].astype(F32)
    crossed = slots_in[0, 0:poles, :].astype(F32) * incoming_all[0]
    for n in range(1, chips):
        parts = parts + slots_in[n, poles : 2 * poles, :].astype(F32)
        crossed = crossed + slots_in[n, 0:poles, :].astype(F32) * incoming_all[n]
    total = pole_weights(rate) * (parts + jnp.exp(-rate) * crossed)
    res_keep[...] = total
    high = total.astype(BF16)
    gate_give[rows : rows + poles, :] = high
    gate_give[rows + poles : rows + 2 * poles, :] = (total - high.astype(F32)).astype(BF16)


def near_body(own_total, same1, cross1, own, other):
    own[...] = (own_total[...] + same1[...].astype(F32)).astype(BF16)
    other[...] = cross1[...].astype(F32)


def block_body(all_dq, own_part, other_part, swapped, dq, dk, dv):
    _, rows, width = own_part.shape
    core, chip = place()
    own, other = halves(core, width)
    for slot, out in ((0, dk), (1, dv)):
        out[:, pl.ds(own, width)] = own_part[slot]
        out[:, pl.ds(other, width)] = (swapped[slot].astype(F32) + other_part[slot]).astype(BF16)
    dq[:, pl.ds(own, width)] = all_dq[pl.ds(pl.multiple_of(core * rows, rows), rows), :]
    dq[:, pl.ds(other, width)] = swapped[2]


def final_body(gate_keep, gate_in, res_keep, dgate, dres):
    rows, width = gate_keep.shape
    poles = res_keep.shape[0]
    own, other = halves(place()[0], width)
    dgate[:, pl.ds(own, width)] = gate_keep[...]
    dgate[:, pl.ds(other, width)] = gate_in[0:rows, :]
    dres[:, pl.ds(own, width)] = res_keep[...]
    dres[:, pl.ds(other, width)] = gate_in[rows : rows + poles, :].astype(F32) + gate_in[
        rows + poles : rows + 2 * poles, :
    ].astype(F32)


def chip_shift(array, by, crossed):
    members = lax.axis_size("ctx")
    pairs = []
    for source in range(members):
        chip, core = source // 2, source % 2
        target = ((chip + by) % (members // 2)) * 2 + ((1 - core) if crossed else core)
        pairs.append((source, target))
    return lax.ppermute(array, "ctx", pairs)


def chip_exchange(slots):
    members = lax.axis_size("ctx")
    groups = [list(range(core, members, 2)) for core in range(2)]
    return lax.all_to_all(slots, "ctx", 0, 0, axis_index_groups=groups)


def local(queries, key_rows, value_rows, gate_values, cotangent, decay_rates, residues, skip_gain):
    rows, channels = queries.shape
    width = channels // 2
    poles = decay_rates.shape[0]
    chips = lax.axis_size("ctx") // 2
    tokens = 2 * rows
    skip = skip_gain.reshape(1, channels)
    groups = width // LANES
    pair = (2, rows, width)
    split = (groups, tokens, LANES)
    states = (poles, SUBS, width)
    span = (WIN + 2) * rows
    keep_kv, keep_rest, give_all, params = call(
        pack_body,
        [
            (pair, BF16, True),
            ((3, rows, width), BF16, True),
            ((5, rows, width), BF16, True),
            ((2 * poles + 1, width), F32, True),
        ],
        scratch=[
            pltpu.VMEM((5, rows, channels), BF16),
            pltpu.VMEM((2 * poles + SUBS, channels), F32),
            pltpu.SemaphoreType.DMA((8,)),
        ],
        far=tuple(range(8)),
        name="pack",
    )(key_rows, value_rows, queries, gate_values, cotangent, decay_rates, residues, skip)
    given = chip_shift(give_all, 0, True)
    (chip_kv,) = call(merge_body, [((2, tokens, width), BF16, True)], near=(0, 1), name="chip_kv")(
        keep_kv, given
    )
    far_kv = chip_shift(chip_kv, 2, False)
    near_kv = chip_shift(chip_kv, 1, False)
    delta, totals, head_slots = call(
        head_body,
        [(split, F32, True), (states, F32, True), ((chips, poles, width), BF16, True)],
        scratch=[pltpu.VMEM((poles, width), F32)],
        near=(0, 1, 2),
        name="head_states",
    )(keep_rest, given, params)
    head_in = chip_exchange(head_slots)
    halo = (keep_rest, chip_kv, given, near_kv, far_kv)
    halo_buffers = [
        pltpu.VMEM((tokens, width), BF16),
        pltpu.VMEM((span, width), BF16),
        pltpu.VMEM((span, width), BF16),
    ]
    stats, attended = call(
        forward_body,
        [((groups, 2, SUBS, rows), F32, True), (split, F32, True)],
        scratch=halo_buffers,
        near=tuple(range(5)),
        cost=EARLY,
        name="forward",
    )(*halo)
    tail_totals, tail_slots = call(
        tail_body,
        [(states, F32, True), ((chips, 2 * poles, width), BF16, True)],
        scratch=[pltpu.VMEM((poles, width), F32), pltpu.VMEM((poles, width), F32)],
        near=(0, 1, 2, 3),
        name="tail",
    )(attended, delta, totals, params)
    tail_in = chip_exchange(tail_slots)
    dq, dkv_chip, out_far, out_same1, out_cross1, incoming_all = call(
        backward_body,
        [
            ((tokens, width), BF16, True),
            ((2, tokens, width), F32, True),
            ((2, tokens, width), BF16, True),
            (pair, BF16, True),
            (pair, BF16, True),
            ((chips, poles, width), F32, True),
        ],
        scratch=halo_buffers
        + [
            pltpu.VMEM(split, BF16),
            pltpu.VMEM(split, F32),
            pltpu.VMEM((span, width), F32),
            pltpu.VMEM((span, width), F32),
        ],
        near=tuple(range(11)),
        name="backward",
    )(*halo, stats, tail_totals, delta, totals, head_in, params)
    back_far = chip_shift(out_far, -2, False)
    back_same1 = chip_shift(out_same1, -1, False)
    back_cross1 = chip_shift(out_cross1, -1, True)
    own_total, partner = call(
        far_body,
        [(pair, F32, True), ((3, rows, width), BF16, True)],
        near=(0, 1, 2),
        cost=EARLY,
        name="far_sum",
    )(dkv_chip, back_far, dq)
    (local_mix,) = call(local_mix_body, [(split, F32, True)], near=(0, 1, 2, 3), name="local_mix")(
        attended, tail_totals, params, partner
    )
    gate_keep, gate_give, res_keep = call(
        gate_body,
        [
            ((rows, width), BF16, True),
            ((rows + 2 * poles, width), BF16, True),
            ((poles, width), F32, True),
        ],
        scratch=[pltpu.VMEM(split, F32), pltpu.VMEM((chips, poles, width), F32)],
        near=tuple(range(7)),
        name="gate",
    )(keep_rest, given, local_mix, tail_in, incoming_all, params, partner)
    swapped = chip_shift(partner, 0, True)
    gate_in = chip_shift(gate_give, 0, True)
    wide = ((rows, channels), BF16, False)
    own_part, other_part = call(
        near_body,
        [(pair, BF16, True), (pair, F32, True)],
        near=(0, 1, 2),
        cost=EARLY,
        name="near_sum",
    )(own_total, back_same1, back_cross1)
    dq, dk, dv = call(block_body, [wide, wide, wide], near=tuple(range(4)), name="blocks")(
        dq, own_part, other_part, swapped
    )
    dgate, dres = call(
        final_body, [wide, ((poles, channels), F32, False)], near=(0, 1, 2), name="final"
    )(gate_keep, gate_in, res_keep)
    return dq, dk, dv, dgate, dres


def solution(mesh):
    wide = P(("dp", "ctx"), "head")
    in_specs = (wide, wide, wide, wide, wide, P(None, "head"), P(None, "head"), P("head"))
    out_specs = (wide, wide, wide, wide, P("dp", "head"))
    return jax.shard_map(local, mesh=mesh, in_specs=in_specs, out_specs=out_specs, check_vma=False)
```

```python
import math

import jax
import jax.numpy as jnp
from jax import lax
from jax.experimental import pallas as pl
from jax.experimental.pallas import tpu as pltpu
from jax.sharding import PartitionSpec as P

HEAD = 128
WIN = 4
LANES = 128
SUBS = 8
GROUP = 8
EARLY = pl.CostEstimate(flops=10**11, transcendentals=0, bytes_accessed=10**8)
F32 = jnp.float32
BF16 = jnp.bfloat16
OVER_KEYS = (((0,), (0,)), ((), ()))
OVER_HEAD = (((1,), (1,)), ((), ()))


def call(body, outs, scratch=(), near=(), far=(), cost=None, name=None):
    def run(*args):
        args = list(args)
        specs = []
        for n in range(len(args)):
            space = pltpu.HBM if n in far else pltpu.VMEM
            specs.append(pl.BlockSpec(memory_space=space))
            if n in near or n in far:
                args[n] = pltpu.with_memory_space_constraint(args[n], space)
        return pl.pallas_call(
            body,
            out_shape=[
                pltpu.VMEM(s, d) if local_out else jax.ShapeDtypeStruct(s, d) for s, d, local_out in outs
            ],
            in_specs=specs,
            out_specs=[pl.BlockSpec(memory_space=pltpu.VMEM)] * len(outs),
            scratch_shapes=list(scratch),
            compiler_params=pltpu.CompilerParams(vmem_limit_bytes=8 * 1024 * 1024),
            cost_estimate=cost,
            name=name,
        )(*args)

    return run


def place():
    index = lax.axis_index("ctx")
    return lax.rem(index, 2), lax.div(index, 2)


def halves(core, width):
    own = pl.multiple_of(core * width, LANES)
    other = pl.multiple_of((1 - core) * width, LANES)
    return own, other


def pack_body(
    k, v, q, gate, cot, rates, residues, skip, keep_kv, keep_rest, give_all, params, buf, small, sems
):
    width = k.shape[1] // 2
    poles = rates.shape[0]
    own, other = halves(place()[0], width)
    arrays = (k, v, q, gate, cot)
    copies = [pltpu.make_async_copy(a, buf.at[n], sems.at[n]) for n, a in enumerate(arrays)]
    for n, (array, first, count) in enumerate(
        ((rates, 0, poles), (residues, poles, poles), (skip, 2 * poles, 1))
    ):
        copies.append(
            pltpu.make_async_copy(array, small.at[pl.ds(first, count)], sems.at[len(arrays) + n])
        )
    for copy in copies:
        copy.start()
    for n in range(len(arrays)):
        copies[n].wait()
        keep = buf[n, :, pl.ds(own, width)]
        give_all[n] = buf[n, :, pl.ds(other, width)]
        if n < 2:
            keep_kv[n] = keep
        else:
            keep_rest[n - 2] = keep
    for copy in copies[len(arrays) :]:
        copy.wait()
    params[...] = small[0 : 2 * poles + 1, pl.ds(own, width)]


def rows3(values):
    return jnp.broadcast_to(values[:, None, :], (values.shape[0], SUBS, values.shape[1]))


def each_group(poles, width, body):
    pole_groups = poles // GROUP
    lane_groups = width // LANES

    def step(index, carry):
        lane_group = index // pole_groups
        first_lane = pl.multiple_of(lane_group * LANES, LANES)
        first_pole = pl.multiple_of((index % pole_groups) * GROUP, GROUP)
        body(first_pole, lane_group, first_lane)
        return carry

    lax.fori_loop(0, pole_groups * lane_groups, step, 0)


def head_body(keep_rest, given, params, delta, totals, slots, head_ref):
    rows, width = keep_rest.shape[1:]
    poles = totals.shape[0]
    chips = slots.shape[0]
    core, chip = place()
    own, other = halves(core, width)
    tokens = delta.shape[1]
    steps = tokens // SUBS
    mine = pl.multiple_of(core * rows, rows)
    theirs = pl.multiple_of((1 - core) * rows, rows)
    for lane_group in range(width // LANES):
        lanes = slice(lane_group * LANES, (lane_group + 1) * LANES)
        delta[lane_group, pl.ds(mine, rows), :] = keep_rest[1, :, lanes].astype(F32) * keep_rest[
            2, :, lanes
        ].astype(F32)
        delta[lane_group, pl.ds(theirs, rows), :] = given[3, :, lanes].astype(F32) * given[
            4, :, lanes
        ].astype(F32)

    def group(first_pole, lane_group, first_lane):
        rate = params[pl.ds(first_pole, GROUP), pl.ds(first_lane, LANES)]
        lam = rows3(jnp.exp(-rate))
        state = jnp.zeros((GROUP, SUBS, LANES), F32)
        for j in reversed(range(steps)):
            state = lam * state + delta[lane_group, pl.ds(j, SUBS, stride=steps), :][None]
        totals[pl.ds(first_pole, GROUP), :, pl.ds(first_lane, LANES)] = state
        block = lax.broadcasted_iota(jnp.int32, (GROUP, SUBS, LANES), 1).astype(F32)
        power = jnp.exp(-rows3(rate) * (block * steps))
        head_ref[pl.ds(first_pole, GROUP), pl.ds(first_lane, LANES)] = jnp.sum(power * state, axis=1)

    each_group(poles, width, group)
    head = head_ref[...].astype(BF16)
    for j in range(chips):
        slots[j] = head


def around(own, rate, tokens, order, out):
    decay = jnp.exp(-rate * tokens)
    value = own(order[-1])
    power = decay
    for n in reversed(order[:-1]):
        value = value + power * own(n)
        power = power * decay
    value = value / (1.0 - jnp.exp(-rate * (tokens * len(order))))
    for n in order:
        out[n] = value
        value = own(n) + decay * value


def block_ids(shape):
    return lax.broadcasted_iota(jnp.int32, shape, 1)


def entering_later(totals, incoming, lam_block):
    ids = block_ids(totals.shape)
    value = jnp.where(ids == SUBS - 1, rows3(incoming), pltpu.roll(totals, SUBS - 1, 1))
    power = lam_block
    for shift in (1, 2, 4):
        moved = pltpu.roll(value, SUBS - shift, 1)
        value = value + jnp.where(ids < SUBS - shift, power * moved, 0.0)
        power = power * power
    return value


def entering_earlier(totals, arriving, lam_block):
    ids = block_ids(totals.shape)
    value = jnp.where(ids == 0, rows3(arriving), pltpu.roll(totals, 1, 1))
    power = lam_block
    for shift in (1, 2, 4):
        moved = pltpu.roll(value, shift, 1)
        value = value + jnp.where(ids >= shift, power * moved, 0.0)
        power = power * power
    return value


def pole_weights(rate):
    tangent = jnp.tanh(rate)
    return jnp.sqrt(2.0 * tangent / (1.0 + tangent))


def merge_body(keep_kv, given, chip_kv):
    rows = keep_kv.shape[1]
    core, chip = place()
    for slot in range(2):
        chip_kv[slot, pl.ds(pl.multiple_of(core * rows, rows), rows), :] = keep_kv[slot]
        chip_kv[slot, pl.ds(pl.multiple_of((1 - core) * rows, rows), rows), :] = given[slot]


def assemble(core, keep_rest, chip_kv, given, near_kv, far_kv, qbuf, kbuf, vbuf):
    rows = keep_rest.shape[1]
    tokens = 2 * rows
    mine = pl.multiple_of(core * rows, rows)
    theirs = pl.multiple_of((1 - core) * rows, rows)
    qbuf[pl.ds(mine, rows), :] = keep_rest[0]
    qbuf[pl.ds(theirs, rows), :] = given[2]
    for slot, buf in ((0, kbuf), (1, vbuf)):
        buf[0:tokens, :] = far_kv[slot]
        buf[tokens : 2 * tokens, :] = near_kv[slot]
        buf[2 * tokens : 3 * tokens, :] = chip_kv[slot]


def masked(scores):
    rows = scores.shape[1]
    key_ids = lax.broadcasted_iota(jnp.int32, (rows, rows), 0)
    row_ids = lax.broadcasted_iota(jnp.int32, (rows, rows), 1)
    oldest = jnp.where(key_ids > row_ids, scores[:rows], -jnp.inf)
    newest = jnp.where(key_ids <= row_ids, scores[WIN * rows :], -jnp.inf)
    return jnp.concatenate([oldest, scores[rows : WIN * rows], newest], axis=0)


def forward_body(
    keep_rest, chip_kv, given, near_kv, far_kv, stats, attended, qbuf, kbuf, vbuf
):
    rows, width = keep_rest.shape[1:]
    tokens = 2 * rows
    core, chip = place()
    scale = 1.0 / math.sqrt(HEAD)
    assemble(core, keep_rest, chip_kv, given, near_kv, far_kv, qbuf, kbuf, vbuf)
    span = (WIN + 1) * rows
    for head in range(width // HEAD):
        at_head = slice(head * HEAD, (head + 1) * HEAD)
        for block in range(tokens // rows):
            at_rows = slice(block * rows, (block + 1) * rows)
            at_keys = slice(block * rows, block * rows + span)
            scores = (
                lax.dot_general(
                    kbuf[at_keys, at_head], qbuf[at_rows, at_head], OVER_HEAD, preferred_element_type=F32
                )
                * scale
            )
            scores = masked(scores)
            top = jnp.max(scores, axis=0, keepdims=True)
            raised = jnp.exp(scores - top)
            share = 1.0 / jnp.sum(raised, axis=0, keepdims=True)
            probability = raised * share
            stats[head, block, 0:1, :] = top
            stats[head, block, 1:2, :] = share
            attended[head, at_rows, :] = (
                lax.dot_general(
                    probability.astype(BF16), vbuf[at_keys, at_head], OVER_KEYS, preferred_element_type=F32
                )
                .astype(BF16)
                .astype(F32)
            )


def tail_body(attended, delta, totals, params, tail_totals, slots, tail_ref, part_ref):
    poles, _, width = totals.shape
    steps = delta.shape[1] // SUBS
    chips = slots.shape[0]

    def tail_group(first_pole, lane_group, first_lane):
        rate = params[pl.ds(first_pole, GROUP), pl.ds(first_lane, LANES)]
        pole_at = pl.ds(first_pole, GROUP)
        lane_at = pl.ds(first_lane, LANES)
        lam = rows3(jnp.exp(-rate))
        state = jnp.zeros((GROUP, SUBS, LANES), F32)
        matched = jnp.zeros((GROUP, SUBS, LANES), F32)
        for j in range(steps):
            at = pl.ds(j, SUBS, stride=steps)
            state = lam * state + attended[lane_group, at, :][None]
            matched = matched + delta[lane_group, at, :][None] * state
        tail_totals[pole_at, :, lane_at] = state
        lam_block = rows3(jnp.exp(-rate * steps))
        entering = entering_earlier(state, jnp.zeros((GROUP, LANES), F32), lam_block)
        full = state + lam_block * entering
        matched = matched + lam * totals[pole_at, :, lane_at] * entering
        tail_ref[pole_at, lane_at] = full[:, SUBS - 1, :]
        part_ref[pole_at, lane_at] = jnp.sum(matched, axis=1)

    each_group(poles, width, tail_group)
    tail = tail_ref[...].astype(BF16)
    part = part_ref[...].astype(BF16)
    for j in range(chips):
        slots[j, 0:poles, :] = tail
        slots[j, poles : 2 * poles, :] = part


def backward_body(
    keep_rest,
    chip_kv,
    given,
    near_kv,
    far_kv,
    stats,
    tail_totals,
    delta,
    totals,
    slots_in,
    params,
    dq,
    dkv_chip,
    out_far,
    out_same1,
    out_cross1,
    incoming_all,
    qbuf,
    kbuf,
    vbuf,
    adj16,
    adj32,
    dk_acc,
    dv_acc,
):
    tokens, width = qbuf.shape
    rows = tokens // 2
    poles = totals.shape[0]
    steps = tokens // SUBS
    chips = slots_in.shape[0]
    core, chip = place()
    mine = pl.multiple_of(core * rows, rows)
    theirs = pl.multiple_of((1 - core) * rows, rows)
    scale = 1.0 / math.sqrt(HEAD)
    assemble(core, keep_rest, chip_kv, given, near_kv, far_kv, qbuf, kbuf, vbuf)

    around(
        lambda n: slots_in[n].astype(F32),
        params[0:poles, :],
        tokens,
        list(reversed(range(chips))),
        incoming_all,
    )
    for lane_group in range(width // LANES):
        gain = params[2 * poles : 2 * poles + 1, lane_group * LANES : (lane_group + 1) * LANES]
        adj32[lane_group] = gain * delta[lane_group]

    def adjoint_group(first_pole, lane_group, first_lane):
        rate = params[pl.ds(first_pole, GROUP), pl.ds(first_lane, LANES)]
        lam = rows3(jnp.exp(-rate))
        mixing = rows3(
            params[pl.ds(poles + first_pole, GROUP), pl.ds(first_lane, LANES)] * pole_weights(rate)
        )
        lane_at = pl.ds(first_lane, LANES)
        state = entering_later(
            totals[pl.ds(first_pole, GROUP), :, lane_at],
            incoming_all[chip, pl.ds(first_pole, GROUP), lane_at],
            rows3(jnp.exp(-rate * steps)),
        )
        for j in reversed(range(steps)):
            at = pl.ds(j, SUBS, stride=steps)
            state = lam * state + delta[lane_group, at, :][None]
            adj32[lane_group, at, :] = adj32[lane_group, at, :] + jnp.sum(mixing * state, axis=0)

    each_group(poles, width, adjoint_group)
    adj16[...] = adj32[...].astype(BF16)

    span = (WIN + 1) * rows
    for head in range(width // HEAD):
        at_head = slice(head * HEAD, (head + 1) * HEAD)
        for block in range(tokens // rows):
            at_rows = slice(block * rows, (block + 1) * rows)
            at_keys = slice(block * rows, block * rows + span)
            query = qbuf[at_rows, at_head]
            key = kbuf[at_keys, at_head]
            value = vbuf[at_keys, at_head]
            adjoint = adj16[head, at_rows, :]
            scores = lax.dot_general(key, query, OVER_HEAD, preferred_element_type=F32) * scale
            scores = masked(scores)
            probability = jnp.exp(scores - stats[head, block, 0:1, :]) * stats[head, block, 1:2, :]
            rounded = probability.astype(BF16)
            weight = lax.dot_general(value, adjoint, OVER_HEAD, preferred_element_type=F32)
            inner = jnp.sum(probability * weight, axis=0, keepdims=True)
            score_adjoint = (probability * (weight - inner) * scale).astype(BF16)
            dq[at_rows, at_head] = lax.dot_general(
                score_adjoint, key, OVER_KEYS, preferred_element_type=F32
            ).astype(BF16)
            dk = jnp.dot(score_adjoint, query, preferred_element_type=F32)
            dv = jnp.dot(rounded, adjoint, preferred_element_type=F32)
            if block == 0:
                dk_acc[at_keys, at_head] = dk
                dv_acc[at_keys, at_head] = dv
            else:
                edge = span - rows
                first = slice(block * rows, block * rows + edge)
                last = slice(block * rows + edge, block * rows + span)
                dk_acc[first, at_head] = dk_acc[first, at_head] + dk[:edge]
                dv_acc[first, at_head] = dv_acc[first, at_head] + dv[:edge]
                dk_acc[last, at_head] = dk[edge:]
                dv_acc[last, at_head] = dv[edge:]

    for slot, acc in ((0, dk_acc), (1, dv_acc)):
        out_far[slot] = acc[0:tokens, :].astype(BF16)
        out_same1[slot] = acc[pl.ds(mine + tokens, rows), :].astype(BF16)
        out_cross1[slot] = acc[pl.ds(theirs + tokens, rows), :].astype(BF16)
        dkv_chip[slot] = acc[2 * tokens : 3 * tokens, :]


def far_body(dkv_chip, far, dq, own_total, give):
    rows = own_total.shape[1]
    core, chip = place()
    mine = pl.ds(pl.multiple_of(core * rows, rows), rows)
    theirs = pl.ds(pl.multiple_of((1 - core) * rows, rows), rows)
    for slot in range(2):
        own_total[slot] = dkv_chip[slot, mine, :] + far[slot, mine, :].astype(F32)
        give[slot] = (dkv_chip[slot, theirs, :] + far[slot, theirs, :].astype(F32)).astype(BF16)
    give[2] = dq[theirs, :]


def local_mix_body(attended, tail_totals, params, partner, mix):
    poles, _, width = tail_totals.shape
    steps = attended.shape[1] // SUBS
    for lane_group in range(width // LANES):
        gain = params[2 * poles : 2 * poles + 1, lane_group * LANES : (lane_group + 1) * LANES]
        mix[lane_group] = gain * attended[lane_group]

    def group(first_pole, lane_group, first_lane):
        rate = params[pl.ds(first_pole, GROUP), pl.ds(first_lane, LANES)]
        lam = rows3(jnp.exp(-rate))
        mixing = rows3(
            params[pl.ds(poles + first_pole, GROUP), pl.ds(first_lane, LANES)] * pole_weights(rate)
        )
        state = entering_earlier(
            tail_totals[pl.ds(first_pole, GROUP), :, pl.ds(first_lane, LANES)],
            jnp.zeros((GROUP, LANES), F32),
            rows3(jnp.exp(-rate * steps)),
        )
        for j in range(steps):
            at = pl.ds(j, SUBS, stride=steps)
            state = lam * state + attended[lane_group, at, :][None]
            mix[lane_group, at, :] = mix[lane_group, at, :] + jnp.sum(mixing * state, axis=0)

    each_group(poles, width, group)


def gate_body(
    keep_rest,
    given,
    local_mix,
    slots_in,
    incoming_all,
    params,
    partner,
    gate_keep,
    gate_give,
    res_keep,
    mix32,
    arriving_ref,
):
    core, chip = place()
    rows, width = keep_rest.shape[1:]
    chips, poles, _ = incoming_all.shape
    tokens = local_mix.shape[1]
    steps = tokens // SUBS
    mine = pl.multiple_of(core * rows, rows)
    theirs = pl.multiple_of((1 - core) * rows, rows)
    rate = params[0:poles, :]
    around(
        lambda n: slots_in[n, 0:poles, :].astype(F32), rate, tokens, list(range(chips)), arriving_ref
    )
    mix32[...] = local_mix[...]

    def group(first_pole, lane_group, first_lane):
        rate = params[pl.ds(first_pole, GROUP), pl.ds(first_lane, LANES)]
        lam = rows3(jnp.exp(-rate))
        mixing = params[pl.ds(poles + first_pole, GROUP), pl.ds(first_lane, LANES)] * pole_weights(rate)
        arriving = arriving_ref[chip, pl.ds(first_pole, GROUP), pl.ds(first_lane, LANES)]
        blocks = block_ids((GROUP, SUBS, LANES)).astype(F32)
        value = rows3(mixing * arriving) * jnp.exp(-rows3(rate) * (blocks * steps))
        for j in range(steps):
            at = pl.ds(j, SUBS, stride=steps)
            value = lam * value
            mix32[lane_group, at, :] = mix32[lane_group, at, :] + jnp.sum(value, axis=0)

    each_group(poles, width, group)
    for lane_group in range(width // LANES):
        lanes = slice(lane_group * LANES, (lane_group + 1) * LANES)
        gate_keep[:, lanes] = (
            keep_rest[2, :, lanes].astype(F32) * mix32[lane_group, pl.ds(mine, rows), :]
        ).astype(BF16)
        gate_give[0:rows, lanes] = (
            given[4, :, lanes].astype(F32) * mix32[lane_group, pl.ds(theirs, rows), :]
        ).astype(BF16)
    parts = slots_in[0, poles : 2 * poles, :].astype(F32)
    crossed = slots_in[0, 0:poles, :].astype(F32) * incoming_all[0]
    for n in range(1, chips):
        parts = parts + slots_in[n, poles : 2 * poles, :].astype(F32)
        crossed = crossed + slots_in[n, 0:poles, :].astype(F32) * incoming_all[n]
    total = pole_weights(rate) * (parts + jnp.exp(-rate) * crossed)
    res_keep[...] = total
    high = total.astype(BF16)
    gate_give[rows : rows + poles, :] = high
    gate_give[rows + poles : rows + 2 * poles, :] = (total - high.astype(F32)).astype(BF16)


def near_body(own_total, same1, cross1, own, other):
    own[...] = (own_total[...] + same1[...].astype(F32)).astype(BF16)
    other[...] = cross1[...].astype(F32)


def block_body(all_dq, own_part, other_part, swapped, dq, dk, dv):
    _, rows, width = own_part.shape
    core, chip = place()
    own, other = halves(core, width)
    for slot, out in ((0, dk), (1, dv)):
        out[:, pl.ds(own, width)] = own_part[slot]
        out[:, pl.ds(other, width)] = (swapped[slot].astype(F32) + other_part[slot]).astype(BF16)
    dq[:, pl.ds(own, width)] = all_dq[pl.ds(pl.multiple_of(core * rows, rows), rows), :]
    dq[:, pl.ds(other, width)] = swapped[2]


def final_body(gate_keep, gate_in, res_keep, dgate, dres):
    rows, width = gate_keep.shape
    poles = res_keep.shape[0]
    own, other = halves(place()[0], width)
    dgate[:, pl.ds(own, width)] = gate_keep[...]
    dgate[:, pl.ds(other, width)] = gate_in[0:rows, :]
    dres[:, pl.ds(own, width)] = res_keep[...]
    dres[:, pl.ds(other, width)] = gate_in[rows : rows + poles, :].astype(F32) + gate_in[
        rows + poles : rows + 2 * poles, :
    ].astype(F32)


def chip_shift(array, by, crossed):
    members = lax.axis_size("ctx")
    pairs = []
    for source in range(members):
        chip, core = source // 2, source % 2
        target = ((chip + by) % (members // 2)) * 2 + ((1 - core) if crossed else core)
        pairs.append((source, target))
    return lax.ppermute(array, "ctx", pairs)


def chip_exchange(slots):
    members = lax.axis_size("ctx")
    groups = [list(range(core, members, 2)) for core in range(2)]
    return lax.all_to_all(slots, "ctx", 0, 0, axis_index_groups=groups)


def local(queries, key_rows, value_rows, gate_values, cotangent, decay_rates, residues, skip_gain):
    rows, channels = queries.shape
    width = channels // 2
    poles = decay_rates.shape[0]
    chips = lax.axis_size("ctx") // 2
    tokens = 2 * rows
    skip = skip_gain.reshape(1, channels)
    groups = width // LANES
    pair = (2, rows, width)
    split = (groups, tokens, LANES)
    states = (poles, SUBS, width)
    span = (WIN + 2) * rows
    keep_kv, keep_rest, give_all, params = call(
        pack_body,
        [
            (pair, BF16, True),
            ((3, rows, width), BF16, True),
            ((5, rows, width), BF16, True),
            ((2 * poles + 1, width), F32, True),
        ],
        scratch=[
            pltpu.VMEM((5, rows, channels), BF16),
            pltpu.VMEM((2 * poles + SUBS, channels), F32),
            pltpu.SemaphoreType.DMA((8,)),
        ],
        far=tuple(range(8)),
        name="pack",
    )(key_rows, value_rows, queries, gate_values, cotangent, decay_rates, residues, skip)
    given = chip_shift(give_all, 0, True)
    (chip_kv,) = call(merge_body, [((2, tokens, width), BF16, True)], near=(0, 1), name="chip_kv")(
        keep_kv, given
    )
    far_kv = chip_shift(chip_kv, 2, False)
    near_kv = chip_shift(chip_kv, 1, False)
    delta, totals, head_slots = call(
        head_body,
        [(split, F32, True), (states, F32, True), ((chips, poles, width), BF16, True)],
        scratch=[pltpu.VMEM((poles, width), F32)],
        near=(0, 1, 2),
        name="head_states",
    )(keep_rest, given, params)
    head_in = chip_exchange(head_slots)
    halo = (keep_rest, chip_kv, given, near_kv, far_kv)
    halo_buffers = [
        pltpu.VMEM((tokens, width), BF16),
        pltpu.VMEM((span, width), BF16),
        pltpu.VMEM((span, width), BF16),
    ]
    stats, attended = call(
        forward_body,
        [((groups, 2, SUBS, rows), F32, True), (split, F32, True)],
        scratch=halo_buffers,
        near=tuple(range(5)),
        cost=EARLY,
        name="forward",
    )(*halo)
    tail_totals, tail_slots = call(
        tail_body,
        [(states, F32, True), ((chips, 2 * poles, width), BF16, True)],
        scratch=[pltpu.VMEM((poles, width), F32), pltpu.VMEM((poles, width), F32)],
        near=(0, 1, 2, 3),
        name="tail",
    )(attended, delta, totals, params)
    tail_in = chip_exchange(tail_slots)
    dq, dkv_chip, out_far, out_same1, out_cross1, incoming_all = call(
        backward_body,
        [
            ((tokens, width), BF16, True),
            ((2, tokens, width), F32, True),
            ((2, tokens, width), BF16, True),
            (pair, BF16, True),
            (pair, BF16, True),
            ((chips, poles, width), F32, True),
        ],
        scratch=halo_buffers
        + [
            pltpu.VMEM(split, BF16),
            pltpu.VMEM(split, F32),
            pltpu.VMEM((span, width), F32),
            pltpu.VMEM((span, width), F32),
        ],
        near=tuple(range(11)),
        name="backward",
    )(*halo, stats, tail_totals, delta, totals, head_in, params)
    back_far = chip_shift(out_far, -2, False)
    back_same1 = chip_shift(out_same1, -1, False)
    back_cross1 = chip_shift(out_cross1, -1, True)
    own_total, partner = call(
        far_body,
        [(pair, F32, True), ((3, rows, width), BF16, True)],
        near=(0, 1, 2),
        cost=EARLY,
        name="far_sum",
    )(dkv_chip, back_far, dq)
    (local_mix,) = call(local_mix_body, [(split, F32, True)], near=(0, 1, 2, 3), name="local_mix")(
        attended, tail_totals, params, partner
    )
    gate_keep, gate_give, res_keep = call(
        gate_body,
        [
            ((rows, width), BF16, True),
            ((rows + 2 * poles, width), BF16, True),
            ((poles, width), F32, True),
        ],
        scratch=[pltpu.VMEM(split, F32), pltpu.VMEM((chips, poles, width), F32)],
        near=tuple(range(7)),
        name="gate",
    )(keep_rest, given, local_mix, tail_in, incoming_all, params, partner)
    swapped = chip_shift(partner, 0, True)
    gate_in = chip_shift(gate_give, 0, True)
    wide = ((rows, channels), BF16, False)
    own_part, other_part = call(
        near_body,
        [(pair, BF16, True), (pair, F32, True)],
        near=(0, 1, 2),
        cost=EARLY,
        name="near_sum",
    )(own_total, back_same1, back_cross1)
    dq, dk, dv = call(block_body, [wide, wide, wide], near=tuple(range(4)), name="blocks")(
        dq, own_part, other_part, swapped
    )
    dgate, dres = call(
        final_body, [wide, ((poles, channels), F32, False)], near=(0, 1, 2), name="final"
    )(gate_keep, gate_in, res_keep)
    return dq, dk, dv, dgate, dres


def solution(mesh):
    wide = P(("dp", "ctx"), "head")
    in_specs = (wide, wide, wide, wide, wide, P(None, "head"), P(None, "head"), P("head"))
    out_specs = (wide, wide, wide, wide, P("dp", "head"))
    return jax.shard_map(local, mesh=mesh, in_specs=in_specs, out_specs=out_specs, check_vma=False)
```
